32 devices in a mesh: seq: 8 (over y, x, core), mp: 4 (over z).
Axes of the slice: x: 2, y: 2, z: 4, core: 2. Of those that a mesh axis runs over, the one named last changes fastest.
Arguments:
- first_half: float32 [4096, 1024], P('seq', 'mp'), may hold values from -6 to 6
- second_half: float32 [4096, 1024], P('seq', 'mp'), may hold values from -6 to 6
- bucket_order: int32 [4, 8, 4096], P(None, 'mp'), may hold values from 0 to 4095, as said below
- attend_gain: float32 [1024], replicated, may hold values from 0.1 to 1.9
- attend_shift: float32 [1024], replicated, may hold values from -3 to 3
- queries: bfloat16 [1024, 1024], P(None, 'mp'), may hold values from -2 to 2
- values: bfloat16 [1024, 1024], P(None, 'mp'), may hold values from -0.1875 to 0.1875
- mixing: bfloat16 [1024, 1024], P('mp'), may hold values from -0.75 to 0.75
- feed_gain: float32 [1024], replicated, may hold values from 0.1 to 1.9
- feed_shift: float32 [1024], replicated, may hold values from -3 to 3
- expand: bfloat16 [1024, 4096], P(None, 'mp'), may hold values from -0.1875 to 0.1875
- expand_bias: float32 [4096], P('mp'), may hold values from -3 to 3
- contract: bfloat16 [4096, 1024], P('mp'), may hold values from -0.125 to 0.125
- contract_bias: float32 [1024], replicated, may hold values from -3 to 3
- cot_first: float32 [4096, 1024], P('seq', 'mp'), may hold values from -6 to 6
- cot_second: float32 [4096, 1024], P('seq', 'mp'), may hold values from -6 to 6
Outputs:
- out_first: float32 [4096, 1024], P('seq', 'mp')
- out_second: float32 [4096, 1024], P('seq', 'mp')
- grad_first: float32 [4096, 1024], P('seq', 'mp')
- grad_second: float32 [4096, 1024], P('seq', 'mp')
- grad_attend_gain: float32 [1024], P('seq')
- grad_attend_shift: float32 [1024], P('seq')
- grad_queries: float32 [1024, 1024], P('seq', 'mp')
- grad_values: float32 [1024, 1024], P('seq', 'mp')
- grad_mixing: float32 [1024, 1024], P('mp', 'seq')
- grad_feed_gain: float32 [1024], P('seq')
- grad_feed_shift: float32 [1024], P('seq')
- grad_expand: float32 [1024, 4096], P('seq', 'mp')
- grad_expand_bias: float32 [4096], P(('mp', 'seq'))
- grad_contract: float32 [4096, 1024], P('mp', 'seq')
- grad_contract_bias: float32 [1024], P('seq')
The draws below stay inside these ranges and needn't reach their ends.
Inputs may be any that keep to these rules, and one draw needn't show every extreme that they name: For every round and head, bucket_order lists each of the 4096 byte positions once; every aligned block of 512 entries takes exactly 64 positions from each aligned block of 512 byte positions.
All inputs are finite; a program needn't handle non-finite values.
Results may differ from the reference program's by a relative error of at most 0.033.
Values may be sent and summed in bfloat16 or wider, within the bound.
A program may use at most 192 MiB of HBM per device.

```python
import math
import jax
import jax.numpy as jnp
from jax import lax

D = 1024
H = 8
DH = 128
FF = 4096
SPAN = 64
ROUNDS = 4
TOK_DEV = 512
TOKENS = 4096


def draw_bucket_order(key, part):
    blocks = TOKENS // TOK_DEV
    piece_rows = TOK_DEV // blocks
    total_draws = ROUNDS * H * blocks
    first_keys = jax.random.split(jax.random.fold_in(key, 11), total_draws)
    second_keys = jax.random.split(jax.random.fold_in(key, 23), total_draws)
    inside = jax.vmap(lambda one_key: jax.random.permutation(one_key, TOK_DEV))(first_keys)
    inside = inside.astype(jnp.int32).reshape(ROUNDS, H, blocks, blocks, piece_rows)
    source_start = jnp.arange(blocks, dtype=jnp.int32)[None, None, :, None, None] * TOK_DEV
    arrived = jnp.transpose(inside + source_start, (0, 1, 3, 2, 4)).reshape(ROUNDS, H, blocks, TOK_DEV)
    shuffle = jax.vmap(lambda one_key: jax.random.permutation(one_key, TOK_DEV))(second_keys)
    shuffle = shuffle.astype(jnp.int32).reshape(ROUNDS, H, blocks, TOK_DEV)
    placed = jnp.take_along_axis(arrived, shuffle, axis=-1)
    return placed.reshape(ROUNDS, H, TOKENS).astype(jnp.int32)


def steps_of(own_key, shape, shards, least, top_value):
    loudness = 1.0
    for dim, shards_of in shards:
        heights = jax.random.uniform(jax.random.fold_in(jax.random.fold_in(own_key, 6), dim), (shards_of,), jnp.float32, least / len(shards), top_value / len(shards))
        loudness = loudness * jnp.repeat(jnp.exp(heights), shape[dim] // shards_of).reshape((-1,) + (1,) * (len(shape) - 1 - dim))
    return loudness


def centred(rng, shape, scale, most, cuts=(), kind=jnp.bfloat16):
    array = jax.random.normal(rng, shape, jnp.float32) * scale
    if len(cuts) > 0:
        array = steps_of(rng, shape, cuts, -0.22, 0.18) * array
    return jnp.clip(array, min=-most, max=most).astype(kind)


def setup_inputs(seed: int = 0) -> dict:
    arg_keys = jax.random.split(jax.random.key(seed), 17)
    return {
        "first_half": centred(arg_keys[0], (TOKENS, D), 1.0, 6.0, ((0, 8), (1, 4)), jnp.float32),
        "second_half": centred(arg_keys[1], (TOKENS, D), 1.0, 6.0, ((0, 8), (1, 4)), jnp.float32),
        "bucket_order": draw_bucket_order(jax.random.fold_in(arg_keys[16], 71), 0),
        "attend_gain": jnp.clip(1.0 + 0.18 * jax.random.normal(arg_keys[3], (D,), jnp.float32), 0.1, 1.9),
        "attend_shift": centred(arg_keys[4], (D,), 0.5, 3.0, (), jnp.float32),
        "queries": centred(arg_keys[5], (D, H * DH), (D // DH) ** -0.5, 2.0, ((1, 4),)),
        "values": centred(arg_keys[6], (D, H * DH), D ** -0.5, 0.1875, ((1, 4),)),
        "mixing": centred(arg_keys[7], (H * DH, D), (H * DH // 16) ** -0.5, 0.75, ((0, 4),)),
        "feed_gain": jnp.clip(1.0 + 0.18 * jax.random.normal(arg_keys[8], (D,), jnp.float32), 0.1, 1.9),
        "feed_shift": centred(arg_keys[9], (D,), 0.5, 3.0, (), jnp.float32),
        "expand": centred(arg_keys[10], (D, FF), D ** -0.5, 0.1875, ((1, 4),)),
        "expand_bias": centred(arg_keys[11], (FF,), 0.5, 3.0, ((0, 4),), jnp.float32),
        "contract": centred(arg_keys[12], (FF, D), (FF // 2) ** -0.5, 0.125, ((0, 4),)),
        "contract_bias": centred(arg_keys[13], (D,), 0.5, 3.0, (), jnp.float32),
        "cot_first": centred(arg_keys[14], (TOKENS, D), 1.0, 6.0, ((0, 8), (1, 4)), jnp.float32),
        "cot_second": centred(arg_keys[15], (TOKENS, D), 1.0, 6.0, ((0, 8), (1, 4)), jnp.float32),
    }


@jax.custom_vjp
def low(v):
    return lax.optimization_barrier(v.astype(jnp.bfloat16)).astype(jnp.float32)

@jax.custom_vjp
def low_back(v):
    return v

def low_keep(v):
    return (low(v), None)

def low_pass(kept, grad):
    return (grad,)

def back_keep(v):
    return (v, None)

def back_low(kept, grad):
    return (low(grad),)
low.defvjp(low_keep, low_pass)
low_back.defvjp(back_keep, back_low)
EPSILON = 1e-06
SELF_SCORE = -100000.0
MASKED = -1000000000.0

def matmul(left, right):
    return jnp.dot(left, right, precision=lax.Precision.HIGHEST, preferred_element_type=jnp.float32)

def normalize(source_rows, gain_row, shift_row):
    center = source_rows - lax.optimization_barrier(jnp.mean(source_rows, axis=-1, keepdims=True))
    spread = lax.optimization_barrier(jnp.mean(center * center, axis=-1, keepdims=True))
    return center * lax.rsqrt(spread + EPSILON) * gain_row + shift_row

def log_total(values_in, reduce_axis):
    highest = lax.optimization_barrier(jnp.max(values_in, axis=reduce_axis, keepdims=True))
    summed = lax.optimization_barrier(jnp.sum(jnp.exp(values_in - highest), axis=reduce_axis, keepdims=True))
    return jnp.squeeze(highest + jnp.log(summed), axis=reduce_axis)

def neighbours(source_array, blocks):
    blocked = source_array.reshape((blocks, SPAN) + source_array.shape[1:])
    return jnp.concatenate([jnp.roll(blocked, 1, axis=0), blocked], axis=1)

def bucket_attend(sorted_qk, sorted_value, hash_order):
    blocks = TOKENS // SPAN
    unit_keys = low(sorted_qk * lax.rsqrt(lax.optimization_barrier(jnp.sum(sorted_qk * sorted_qk, axis=-1, keepdims=True)) + EPSILON))
    key_slots = neighbours(unit_keys, blocks)
    value_slots = neighbours(sorted_value, blocks)
    key_positions = neighbours(hash_order, blocks)
    query_block = sorted_qk.reshape(blocks, SPAN, DH)
    query_positions = hash_order.reshape(blocks, SPAN)
    raw_scores = low_back(jnp.einsum('cqd,ckd->cqk', query_block, key_slots, precision=lax.Precision.HIGHEST) * (1.0 / math.sqrt(DH)))
    earlier = key_positions[:, None, :] < query_positions[:, :, None]
    itself = key_positions[:, None, :] == query_positions[:, :, None]
    scores = jnp.where(earlier, raw_scores, jnp.where(itself, SELF_SCORE, MASKED))
    log_sums = log_total(scores, -1)
    weights_low = low(jnp.exp(scores - log_sums[..., None]))
    bucket_out = jnp.einsum('cqk,ckd->cqd', weights_low, value_slots, precision=lax.Precision.HIGHEST)
    return (bucket_out.reshape(TOKENS, DH), log_sums.reshape(TOKENS))

def head_rounds(packed):
    shared_head, value_head, order_head = packed
    round_outs = []
    round_sums = []
    for hash_round in range(ROUNDS):
        hash_order = order_head[hash_round]
        sorted_qk = low_back(shared_head[hash_order])
        sorted_value = low_back(value_head[hash_order])
        bucket_out, log_sums = bucket_attend(sorted_qk, sorted_value, hash_order)
        bucket_out = low_back(low(bucket_out))
        round_outs.append(jnp.zeros_like(bucket_out).at[hash_order].set(bucket_out))
        round_sums.append(jnp.zeros_like(log_sums).at[hash_order].set(log_sums))
    stacked_outs = jnp.stack(round_outs)
    stacked_sums = jnp.stack(round_sums)
    weights = jnp.exp(stacked_sums - log_total(stacked_sums, 0)[None])
    return lax.optimization_barrier(jnp.sum(weights[..., None] * stacked_outs, axis=0))

def reference(first_half, second_half, bucket_order, attend_gain, attend_shift, queries, values, mixing, feed_gain, feed_shift, expand, expand_bias, contract, contract_bias, cot_first, cot_second):
    order_heads = jnp.transpose(bucket_order, (1, 0, 2)).astype(jnp.int32)
    row_block = min(TOKENS, 4096)

    def forward(first_half, second_half, attend_gain, attend_shift, queries, values, mixing, feed_gain, feed_shift, expand, expand_bias, contract, contract_bias):
        attend_rows = low(normalize(second_half, attend_gain, attend_shift))
        shared = low_back(low(matmul(attend_rows, queries)))
        value_rows = low_back(low(matmul(attend_rows, values)))
        shared_heads = jnp.transpose(shared.reshape(TOKENS, H, DH), (1, 0, 2))
        value_heads = jnp.transpose(value_rows.reshape(TOKENS, H, DH), (1, 0, 2))
        merged = lax.map(jax.checkpoint(head_rounds), (shared_heads, value_heads, order_heads))
        mixed_in = low(jnp.transpose(merged, (1, 0, 2)).reshape(TOKENS, H * DH))
        attention = low_back(matmul(mixed_in, mixing))
        out_first = first_half + attention

        def feed_block(block_rows):
            feed_rows = low(normalize(block_rows, feed_gain, feed_shift))
            hidden_pre = low_back(matmul(feed_rows, expand) + expand_bias)
            active = low(jax.nn.gelu(hidden_pre, approximate=False))
            return low_back(matmul(active, contract) + contract_bias)
        feed_out = lax.map(jax.checkpoint(feed_block), out_first.reshape(TOKENS // row_block, row_block, D)).reshape(TOKENS, D)
        return (out_first, second_half + feed_out)
    inputs = (first_half.astype(jnp.float32), second_half.astype(jnp.float32), attend_gain.astype(jnp.float32), attend_shift.astype(jnp.float32), queries.astype(jnp.float32), values.astype(jnp.float32), mixing.astype(jnp.float32), feed_gain.astype(jnp.float32), feed_shift.astype(jnp.float32), expand.astype(jnp.float32), expand_bias.astype(jnp.float32), contract.astype(jnp.float32), contract_bias.astype(jnp.float32))
    outputs, pullback = jax.vjp(forward, *inputs)
    grads = pullback((cot_first.astype(jnp.float32), cot_second.astype(jnp.float32)))
    return (outputs[0], outputs[1], grads[0], grads[1], grads[2], grads[3], grads[4], grads[5], grads[6], grads[7], grads[8], grads[9], grads[10], grads[11], grads[12])
```

```python
import functools
import math

import jax
import jax.numpy as jnp
from jax import lax
from jax.experimental import pallas as pl
from jax.experimental.pallas import tpu as pltpu
from jax.sharding import PartitionSpec as P

DH = 128
SPAN = 64
EPSILON = 1e-06
SELF_SCORE = -100000.0
MASKED = -1000000000.0
F32 = jnp.float32
BF16 = jnp.bfloat16
MESH = pl.DeviceIdType.MESH
VMEM = pl.BlockSpec(memory_space=pltpu.VMEM)
ROW = (((1,), (1,)), ((), ()))
COL = (((0,), (0,)), ((), ()))


def dot(a, b):
    return jnp.dot(a, b, preferred_element_type=F32)


def dot_nt(a, b):
    return lax.dot_general(a, b, ROW, preferred_element_type=F32)


def dot_tn(a, b):
    return lax.dot_general(a, b, COL, preferred_element_type=F32)


def remote(src, dst, send_sem, recv_sem, axis, index):
    return pltpu.make_async_remote_copy(
        src_ref=src,
        dst_ref=dst,
        send_sem=send_sem,
        recv_sem=recv_sem,
        device_id={axis: index},
        device_id_type=MESH,
    )


def greet(n, m, g, me):
    barrier = pltpu.get_barrier_semaphore()

    @pl.loop(1, n)
    def _(i):
        pl.semaphore_signal(
            barrier, inc=1, device_id={"seq": lax.rem(g + i, n)}, device_id_type=MESH
        )

    @pl.loop(1, m)
    def _(i):
        pl.semaphore_signal(
            barrier, inc=1, device_id={"mp": lax.rem(me + i, m)}, device_id_type=MESH
        )

    pl.semaphore_wait(barrier, n + m - 2)


def iota(shape, dim):
    return lax.broadcasted_iota(jnp.int32, shape, dim)


def fiota(shape, dim):
    return iota(shape, dim).astype(F32)


def split3(x):
    hi = x.astype(BF16).astype(F32)
    rest = x - hi
    mid = rest.astype(BF16).astype(F32)
    return hi, mid, rest - mid


def columns3(x):
    hi, mid, low = split3(x)
    lane = iota((x.shape[0], 128), 1)
    return jnp.where(lane == 0, hi, jnp.where(lane == 1, mid, jnp.where(lane == 2, low, 0.0)))


def rows3(x):
    hi, mid, low = split3(x)
    part = iota((16, x.shape[1]), 0)
    return jnp.where(part == 0, hi, jnp.where(part == 1, mid, jnp.where(part == 2, low, 0.0)))


def column_to_row(x, onehot):
    packed = jnp.transpose(columns3(x))[0:16].astype(BF16)
    return jnp.sum(dot_nt(packed, onehot), axis=0, keepdims=True)


def row_to_column(x, onehot):
    return jnp.sum(dot_nt(onehot, rows3(x).astype(BF16)), axis=1, keepdims=True)


def onehot_rows(row, count):
    return jnp.where(fiota((count, row.shape[1]), 0) == row, 1.0, 0.0).astype(BF16)


def onehot_columns(column, count):
    return jnp.where(fiota((column.shape[0], count), 1) == column, 1.0, 0.0).astype(BF16)


def line_start(me, m, buf, send, recv, chunk):
    @pl.when(me < m - 1)
    def _():
        remote(buf.at[me, chunk], buf.at[me, chunk], send.at[0, me, chunk], recv.at[0, me, chunk], "mp", me + 1).start()

    @pl.when(me > 0)
    def _():
        remote(buf.at[me, chunk], buf.at[me, chunk], send.at[1, me, chunk], recv.at[1, me, chunk], "mp", me - 1).start()


def line_step(me, m, buf, send, recv, chunk, hop):
    @pl.when(me - hop >= 0)
    def _():
        src = me - hop
        part = buf.at[src, chunk]
        remote(part, part, send.at[0, src, chunk], recv.at[0, src, chunk], "mp", me - 1).wait_recv()

        @pl.when(me < m - 1)
        def _():
            remote(part, part, send.at[0, src, chunk], recv.at[0, src, chunk], "mp", me + 1).start()

    @pl.when(me + hop < m)
    def _():
        src = me + hop
        part = buf.at[src, chunk]
        remote(part, part, send.at[1, src, chunk], recv.at[1, src, chunk], "mp", me + 1).wait_recv()

        @pl.when(me > 0)
        def _():
            remote(part, part, send.at[1, src, chunk], recv.at[1, src, chunk], "mp", me - 1).start()


def line_drain(me, m, buf, send, recv, chunk):
    for hop in range(m):

        @pl.when((me - hop >= 0) & (me < m - 1))
        def _():
            part = buf.at[me - hop, chunk]
            remote(part, part, send.at[0, me - hop, chunk], recv.at[0, me - hop, chunk], "mp", me + 1).wait_send()

        @pl.when((me + hop < m) & (me > 0))
        def _():
            part = buf.at[me + hop, chunk]
            remote(part, part, send.at[1, me + hop, chunk], recv.at[1, me + hop, chunk], "mp", me - 1).wait_send()


def spread(n, g, src, dst, piece, send_sem, recv_sem):
    own = pl.multiple_of(g * piece, piece)
    dst[pl.ds(own, piece)] = src[pl.ds(own, piece)]

    @pl.loop(1, n)
    def _(i):
        d = lax.rem(g + i, n)
        there = pl.multiple_of(d * piece, piece)
        remote(src.at[pl.ds(there, piece)], dst.at[pl.ds(own, piece)], send_sem, recv_sem, "seq", d).start()


def all_of(buf, rows, send_sem, recv_sem, g):
    part = buf.at[pl.ds(0, rows)]
    return remote(part, part, send_sem, recv_sem, "seq", g)


def rank_rows(keys_row, keys_col):
    return jnp.sum(jnp.where(keys_col < keys_row, 1.0, 0.0), axis=0, keepdims=True)


def front_kernel(
    n, m, heads, piece,
    second, first_cot, second_cot, order, gain, shift, wq, wv,
    rows_out, cot_out, ext, ro_out, wts_out, mixed_out, merged_out, rank_out, send_out, pos_out, kpos_out, zbuf,
    paired, outgoing, arrived, returning, back, unit, pos_ext, poscol, rankcol, sendcol, lsecol, lse_send, lse_recv,
    zs, zr, cs, cr, ins, inr, prs, prr, bks, bkr, lss, lsr,
):
    g = lax.axis_index("seq")
    me = lax.axis_index("mp")
    tokens, width = rows_out.shape
    part_width = second.shape[1]
    count = order.shape[0]
    rounds = count // heads
    blocks = tokens // SPAN
    chunks = zbuf.shape[1]
    chunk_rows = tokens // chunks
    greet(n, m, g, me)

    for chunk in range(chunks):
        zbuf[me, chunk] = second[chunk * chunk_rows : (chunk + 1) * chunk_rows].astype(BF16)
        line_start(me, m, zbuf, zs, zr, chunk)

    start = pl.multiple_of(g * tokens, tokens)
    before = pl.multiple_of(lax.rem(g + n - 1, n) * tokens + tokens - 128, 128)
    own_pos = order[:, pl.ds(start, tokens)].astype(F32)
    pos_ext[:, 0:SPAN] = order[:, pl.ds(before, 128)][:, 128 - SPAN :].astype(F32)
    pos_ext[:, SPAN : SPAN + tokens] = own_pos
    for block in range(blocks):
        kpos_out[block] = pos_ext[:, block * SPAN : (block + 2) * SPAN]
    pos_out[...] = own_pos
    total = order.shape[1]
    place = jnp.right_shift(iota((1, total), 1), tokens.bit_length() - 1).astype(F32)
    high = jnp.right_shift(iota((32, tokens), 1), 4) == iota((32, tokens), 0)
    low = jnp.where(jnp.bitwise_and(iota((16, tokens), 1), 15) == iota((16, tokens), 0), 1.0, 0.0).astype(BF16)
    token = fiota((1, tokens), 1)
    for item in range(count):
        local = order[item : item + 1, :] - g * tokens
        a = jnp.where(jnp.right_shift(local, 4) == iota((32, total), 0), place, 0.0).astype(BF16)
        b = jnp.where(jnp.bitwise_and(local, 15) == iota((16, total), 0), 1.0, 0.0).astype(BF16)
        table = dot_nt(a, b).astype(BF16)
        target = jnp.sum(jnp.where(high, dot(table, low), 0.0), axis=0, keepdims=True)
        send_out[item : item + 1, :] = target * tokens + token
    keys_row = send_out[...]
    keys_col = jnp.transpose(keys_row)
    pos_col = jnp.transpose(own_pos)
    hops = [(hop, chunk) for hop in range(1, m) for chunk in range(chunks)]
    for item in range(count):
        poscol[item] = pos_col[:, item : item + 1]
        send_out[item : item + 1, :] = rank_rows(keys_row[item : item + 1], keys_col[:, item : item + 1])
        rank_out[item : item + 1, :] = rank_rows(own_pos[item : item + 1], pos_col[:, item : item + 1])
        if item < len(hops):
            line_step(me, m, zbuf, zs, zr, hops[item][1], hops[item][0])
    for hop, chunk in hops[count:]:
        line_step(me, m, zbuf, zs, zr, chunk, hop)
    send_col = jnp.transpose(send_out[...])
    rank_col = jnp.transpose(rank_out[...])
    for item in range(count):
        sendcol[item] = send_col[:, item : item + 1]
        rankcol[item] = rank_col[:, item : item + 1]

    for chunk in range(chunks):
        part = slice(chunk * chunk_rows, (chunk + 1) * chunk_rows)
        rows = jnp.concatenate([zbuf[s, chunk].astype(F32) for s in range(m)], axis=1)
        center = rows - jnp.mean(rows, axis=1, keepdims=True)
        var = jnp.mean(center * center, axis=1, keepdims=True)
        normed = (center * lax.rsqrt(var + EPSILON) * gain[...] + shift[...]).astype(BF16)
        rows_out[part, :] = normed
        q = dot(normed, wq[...]).astype(BF16)
        v = dot(normed, wv[...]).astype(BF16)
        for h in range(heads):
            paired[h, part, 0:DH] = q[:, h * DH : (h + 1) * DH]
            paired[h, part, DH : 2 * DH] = v[:, h * DH : (h + 1) * DH]

    for k, cot in enumerate((second_cot, first_cot)[: cot_out.shape[0]]):
        cot_out[k, me] = cot[...].astype(BF16)

        @pl.loop(1, m)
        def _(i):
            peer = lax.rem(me + i, m)
            remote(cot_out.at[k, me], cot_out.at[k, me], cs.at[k, i], cr.at[k, me], "mp", peer).start()

    @pl.loop(0, count)
    def _(item):
        select = onehot_rows(send_out[pl.ds(item, 1), :], tokens)
        outgoing[item] = dot(select, paired[lax.rem(item, heads)]).astype(BF16)
        spread(n, g, outgoing.at[item], arrived.at[item], piece, ins.at[item], inr.at[item])

    peers_rows = (n - 1) * piece
    after = lax.rem(g + 1, n)

    @pl.loop(0, count + 1)
    def _(step):
        @pl.when(step < count)
        def _():
            item = step
            all_of(arrived.at[item], peers_rows, ins.at[item], inr.at[item], g).wait_recv()
            select = onehot_columns(rankcol[item], tokens)
            ext[item, SPAN:, :] = dot(select, arrived[item]).astype(BF16)
            remote(ext.at[item, pl.ds(tokens, SPAN)], ext.at[item, pl.ds(0, SPAN)], prs.at[item], prr.at[item], "seq", after).start()

        @pl.when(step > 0)
        def _():
            item = step - 1
            remote(ext.at[item, pl.ds(tokens, SPAN)], ext.at[item, pl.ds(0, SPAN)], prs.at[item], prr.at[item], "seq", after).wait_recv()
            w = ext[item, :, 0:DH].astype(F32)
            unit[...] = (w * lax.rsqrt(jnp.sum(w * w, axis=1, keepdims=True) + EPSILON)).astype(BF16)
            outs = []
            sums = []
            for block in range(blocks):
                lo = block * SPAN
                q = ext[item, lo + SPAN : lo + 2 * SPAN, 0:DH]
                raw = dot_nt(q, unit[lo : lo + 2 * SPAN]) * (1.0 / math.sqrt(DH))
                key_pos = kpos_out[block, pl.ds(item, 1), :]
                query_pos = poscol[item, lo : lo + SPAN]
                scores = jnp.where(
                    key_pos < query_pos, raw, jnp.where(key_pos == query_pos, SELF_SCORE, MASKED)
                )
                peak = jnp.max(scores, axis=1, keepdims=True)
                lse = peak + jnp.log(jnp.sum(jnp.exp(scores - peak), axis=1, keepdims=True))
                probs = jnp.exp(scores - lse).astype(BF16)
                outs.append(dot(probs, ext[item, lo : lo + 2 * SPAN, DH : 2 * DH]).astype(BF16))
                sums.append(lse)
            select = onehot_rows(rank_out[pl.ds(item, 1), :], tokens)
            returning[item] = dot(select, jnp.concatenate(outs, axis=0)).astype(BF16)
            spread(n, g, returning.at[item], back.at[item], piece, bks.at[item], bkr.at[item])
            lse_row = column_to_row(jnp.concatenate(sums, axis=0), select)
            for d in range(n):
                lse_send[d, pl.ds(item, 1), 0:piece] = lse_row[:, d * piece : (d + 1) * piece]

    lse_recv[g] = lse_send[g]

    @pl.loop(1, n)
    def _(i):
        d = lax.rem(g + i, n)
        remote(lse_send.at[d], lse_recv.at[g], lss, lsr, "seq", d).start()

    all_of(lse_recv, n - 1, lss, lsr, g).wait_recv()
    lse_rows = jnp.concatenate([lse_recv[d][:, 0:piece] for d in range(n)], axis=1)
    pos_ext[:, 0:tokens] = lse_rows

    @pl.loop(0, count)
    def _(item):
        all_of(back.at[item], peers_rows, bks.at[item], bkr.at[item], g).wait_recv()
        select = onehot_columns(sendcol[item], tokens)
        ro_out[item] = dot(select, back[item]).astype(BF16)
        lsecol[item] = row_to_column(pos_ext[pl.ds(item, 1), 0:tokens], select)

    lane = iota((tokens, 128), 1)
    weights = jnp.zeros((tokens, 128), F32)
    for h in range(heads):
        logs = [lsecol[r * heads + h] for r in range(rounds)]
        peak = functools.reduce(jnp.maximum, logs)
        full = peak + jnp.log(sum(jnp.exp(x - peak) for x in logs))
        merged = jnp.zeros((tokens, DH), F32)
        for r in range(rounds):
            w = jnp.exp(logs[r] - full)
            weights = jnp.where(lane == r * heads + h, w, weights)
            merged = merged + w * ro_out[r * heads + h].astype(F32)
        merged_out[:, h * DH : (h + 1) * DH] = merged
        mixed_out[:, h * DH : (h + 1) * DH] = merged.astype(BF16)
    wts_out[...] = weights

    for chunk in range(chunks):
        line_drain(me, m, zbuf, zs, zr, chunk)
    for k in range(cot_out.shape[0]):

        @pl.loop(1, m)
        def _(i):
            src = lax.rem(me + i, m)
            remote(cot_out.at[k, src], cot_out.at[k, src], cs.at[k, i], cr.at[k, src], "mp", src).wait()

    @pl.loop(0, count)
    def _(item):
        all_of(outgoing.at[item], peers_rows, ins.at[item], inr.at[item], g).wait_send()
        all_of(returning.at[item], peers_rows, bks.at[item], bkr.at[item], g).wait_send()
        remote(ext.at[item, pl.ds(tokens, SPAN)], ext.at[item, pl.ds(0, SPAN)], prs.at[item], prr.at[item], "seq", after).wait_send()

    all_of(lse_send, n - 1, lss, lsr, g).wait_send()


def front(n, m, heads, second, first_cot, second_cot, order, gain, shift, wq, wv):
    tokens, part_width = second.shape
    width = wq.shape[0]
    count = order.shape[0]
    piece = tokens // n
    blocks = tokens // SPAN
    chunks = 2
    dma = pltpu.SemaphoreType.DMA
    sds = jax.ShapeDtypeStruct
    outs = (
        sds((tokens, width), BF16),
        sds((1, m, tokens, part_width), BF16),
        sds((count, SPAN + tokens, 2 * DH), BF16),
        sds((count, tokens, DH), BF16),
        sds((tokens, 128), F32),
        sds((tokens, heads * DH), BF16),
        sds((tokens, heads * DH), F32),
        sds((count, tokens), F32),
        sds((count, tokens), F32),
        sds((count, tokens), F32),
        sds((blocks, count, 2 * SPAN), F32),
        sds((m, chunks, tokens // chunks, part_width), BF16),
    )
    scratch = [
        pltpu.VMEM((heads, tokens, 2 * DH), BF16),
        pltpu.VMEM((count, tokens, 2 * DH), BF16),
        pltpu.VMEM((count, tokens, 2 * DH), BF16),
        pltpu.VMEM((count, tokens, DH), BF16),
        pltpu.VMEM((count, tokens, DH), BF16),
        pltpu.VMEM((SPAN + tokens, DH), BF16),
        pltpu.VMEM((count, tokens + 128), F32),
        pltpu.VMEM((count, tokens, 1), F32),
        pltpu.VMEM((count, tokens, 1), F32),
        pltpu.VMEM((count, tokens, 1), F32),
        pltpu.VMEM((count, tokens, 1), F32),
        pltpu.VMEM((n, count, 128), F32),
        pltpu.VMEM((n, count, 128), F32),
        dma((2, m, chunks)),
        dma((2, m, chunks)),
        dma((2, m)),
        dma((2, m)),
        dma((count,)),
        dma((count,)),
        dma((count,)),
        dma((count,)),
        dma((count,)),
        dma((count,)),
        dma,
        dma,
    ]
    return pl.pallas_call(
        functools.partial(front_kernel, n, m, heads, piece),
        out_shape=outs,
        in_specs=[VMEM] * 8,
        out_specs=[VMEM] * len(outs),
        scratch_shapes=scratch,
        compiler_params=pltpu.CompilerParams(
            collective_id=0, has_side_effects=True, vmem_limit_bytes=56 << 20
        ),
        name="front",
    )(second, first_cot, second_cot, order, gain, shift, wq, wv)


def reduce_start(me, m, own, got, send, recv, chunk):
    @pl.when(me == 0)
    def _():
        for s in range(m - 1, 0, -1):
            remote(own.at[s, chunk], got.at[0, s, chunk], send.at[0, s, chunk], recv.at[0, s, chunk], "mp", me + 1).start()

    @pl.when(me == m - 1)
    def _():
        for s in range(m - 1):
            remote(own.at[s, chunk], got.at[1, s, chunk], send.at[1, s, chunk], recv.at[1, s, chunk], "mp", me - 1).start()


def reduce_step(me, m, own, got, passing, total, send, recv, chunk):
    def way(direction, s, inside, peer):
        place = (direction, s, chunk)
        hop = remote(passing.at[place], got.at[place], send.at[place], recv.at[place], "mp", peer)

        @pl.when(inside)
        def _():
            hop.wait_recv()
            passing[place] = (own[s, chunk].astype(F32) + got[place].astype(F32)).astype(BF16)
            hop.start()

    for i in range(m):
        s = m - 1 - i
        way(0, s, (me > 0) & (me < s), me + 1)
        way(1, i, (me < m - 1) & (me > i), me - 1)
    total[...] = own[me, chunk].astype(F32)

    @pl.when(me > 0)
    def _():
        remote(own.at[me, chunk], got.at[0, me, chunk], send.at[0, me, chunk], recv.at[0, me, chunk], "mp", me - 1).wait_recv()
        total[...] += got[0, me, chunk].astype(F32)

    @pl.when(me < m - 1)
    def _():
        remote(own.at[me, chunk], got.at[1, me, chunk], send.at[1, me, chunk], recv.at[1, me, chunk], "mp", me + 1).wait_recv()
        total[...] += got[1, me, chunk].astype(F32)


def reduce_drain(me, m, own, got, send, recv, chunk):
    for s in range(m):
        for direction, sent in ((0, me < s), (1, me > s)):
            place = (direction, s, chunk)

            @pl.when(sent)
            def _():
                remote(own.at[s, chunk], got.at[place], send.at[place], recv.at[place], "mp", me).wait_send()


def pack_stats(a, b):
    lane = iota((a.shape[0], 128), 1)
    return jnp.transpose(jnp.where(lane == 0, a, jnp.where(lane == 1, b, 0.0)))[0:8]


def stats_start(me, m, stats, send, recv, chunk):
    @pl.loop(1, m)
    def _(i):
        remote(stats.at[me, chunk], stats.at[me, chunk], send.at[i, chunk], recv.at[me, chunk], "mp", lax.rem(me + i, m)).start()


def stats_wait(me, m, stats, send, recv, chunk):
    @pl.loop(1, m)
    def _(i):
        src = lax.rem(me + i, m)
        remote(stats.at[src, chunk], stats.at[src, chunk], send.at[i, chunk], recv.at[src, chunk], "mp", src).wait()

    return jnp.transpose(sum(stats[s, chunk] for s in range(m)))


def middle_kernel(
    n, m, heads, chunks,
    mixed, mixing, first, first_cot, cot_full, gain, shift, expand, expand_bias, contract,
    out_first, grad_first, gm_out, fo_out, pe_out, pc_out, pm_out, vec_out,
    part_a, got_a, pass_a, full_a, part_b, got_b, pass_b, full_b, total, stats,
    gact, feed, active, gpre, grad_feed, grad_att, mean_scr, rstd_scr,
    ras, rar, gas, gar, rbs, rbr, gbs, gbr, sts, str_,
):
    g = lax.axis_index("seq")
    me = lax.axis_index("mp")
    tokens, part_width = first.shape
    width = mixing.shape[1]
    rows = tokens // chunks
    greet(1, m, g, me)

    def scatter(part, value, chunk):
        for s in range(m):
            part[s, chunk] = value[:, s * part_width : (s + 1) * part_width].astype(BF16)

    def gather(full, chunk):
        return jnp.concatenate([full[s, chunk] for s in range(m)], axis=1)

    for chunk in range(chunks):
        scatter(part_a, dot(mixed[chunk * rows : (chunk + 1) * rows, :], mixing[...]), chunk)
        reduce_start(me, m, part_a, got_a, ras, rar, chunk)
    for chunk in range(chunks):
        part = slice(chunk * rows, (chunk + 1) * rows)
        cot = jnp.concatenate([cot_full[0, s, part, :] for s in range(m)], axis=1)
        grad_feed[part, :] = cot
        gact[part, :] = dot_nt(cot, contract[...])
    own_cols = pl.multiple_of(me * part_width, part_width)
    gain_own = gain[:, pl.ds(own_cols, part_width)]
    vec_out[...] = jnp.zeros_like(vec_out)

    @pl.loop(0, chunks + 3)
    def _(tick):
        @pl.when(tick < chunks)
        def _():
            chunk = tick
            part = pl.ds(pl.multiple_of(chunk * rows, rows), rows)
            reduce_step(me, m, part_a, got_a, pass_a, total, ras, rar, chunk)
            stream = first[part, :] + total[...]
            out_first[part, :] = stream
            full_a[me, chunk] = stream.astype(BF16)
            line_start(me, m, full_a, gas, gar, chunk)

        @pl.when((tick >= 1) & (tick < chunks + 1))
        def _():
            chunk = tick - 1
            part = pl.ds(pl.multiple_of(chunk * rows, rows), rows)
            for hop in range(1, m):
                line_step(me, m, full_a, gas, gar, chunk, hop)
            x = gather(full_a, chunk).astype(F32)
            mean = jnp.mean(x, axis=1, keepdims=True)
            center = x - mean
            rstd = lax.rsqrt(jnp.mean(center * center, axis=1, keepdims=True) + EPSILON)
            mean_scr[part, :] = mean
            rstd_scr[part, :] = rstd
            xhat = center * rstd
            normed = (xhat * gain[...] + shift[...]).astype(BF16)
            feed[part, :] = normed
            pre = dot(normed, expand[...]) + expand_bias[...]
            gate = 0.5 * (1.0 + lax.erf(pre * (1.0 / math.sqrt(2.0))))
            active[part, :] = (pre * gate).astype(BF16)
            slope = gate + pre * jnp.exp(-0.5 * pre * pre) * (1.0 / math.sqrt(2.0 * math.pi))
            back = (gact[part, :] * slope).astype(BF16)
            gpre[part, :] = back
            term = dot_nt(back, expand[...])
            scatter(part_b, term, chunk)
            reduce_start(me, m, part_b, got_b, rbs, rbr, chunk)
            e = term * gain[...]
            stats[me, chunk] = pack_stats(
                jnp.sum(e, axis=1, keepdims=True), jnp.sum(e * xhat, axis=1, keepdims=True)
            )
            stats_start(me, m, stats, sts, str_, chunk)
            vec_out[0:1, :] += jnp.sum(term * xhat, axis=0, keepdims=True)
            vec_out[1:2, :] += jnp.sum(term, axis=0, keepdims=True)
            vec_out[2:3, :] += jnp.sum(grad_feed[part, :].astype(F32), axis=0, keepdims=True)
            vec_out[3:4, :] += jnp.sum(back.astype(F32), axis=0, keepdims=True)

        @pl.when((tick >= 2) & (tick < chunks + 2))
        def _():
            chunk = tick - 2
            part = pl.ds(pl.multiple_of(chunk * rows, rows), rows)
            reduce_step(me, m, part_b, got_b, pass_b, total, rbs, rbr, chunk)
            sums = stats_wait(me, m, stats, sts, str_, chunk) * (1.0 / width)
            rstd = rstd_scr[part, :]
            xhat = (full_a[me, chunk].astype(F32) - mean_scr[part, :]) * rstd
            stream = first_cot[part, :] + rstd * (
                total[...] * gain_own - sums[:, 0:1] - xhat * sums[:, 1:2]
            )
            grad_first[part, :] = stream
            full_b[me, chunk] = stream.astype(BF16)
            line_start(me, m, full_b, gbs, gbr, chunk)

        @pl.when(tick >= 3)
        def _():
            chunk = tick - 3
            part = pl.ds(pl.multiple_of(chunk * rows, rows), rows)
            for hop in range(1, m):
                line_step(me, m, full_b, gbs, gbr, chunk, hop)
            att = gather(full_b, chunk)
            grad_att[part, :] = att
            gm_out[part, :] = dot_nt(att, mixing[...])

    tile = 256

    @pl.loop(0, width // tile)
    def _(k):
        cols = pl.ds(pl.multiple_of(k * tile, tile), tile)
        pe_out[cols, :] = dot_tn(feed[:, cols], gpre[...]).astype(BF16)
        pc_out[cols, :] = dot_tn(grad_feed[:, cols], active[...]).astype(BF16)
        pm_out[cols, :] = dot_tn(grad_att[:, cols], mixed[...]).astype(BF16)

    for s in range(m):
        fo_out[s] = dot(active[...], contract[:, s * part_width : (s + 1) * part_width]).astype(BF16)

    for chunk in range(chunks):
        reduce_drain(me, m, part_a, got_a, ras, rar, chunk)
        reduce_drain(me, m, part_b, got_b, rbs, rbr, chunk)
        line_drain(me, m, full_a, gas, gar, chunk)
        line_drain(me, m, full_b, gbs, gbr, chunk)


def middle(n, m, heads, mixed, mixing, first, first_cot, cot_full, gain, shift, expand, expand_bias, contract):
    tokens, part_width = first.shape
    width = mixing.shape[1]
    hidden = expand.shape[1]
    chunks = 4
    rows = tokens // chunks
    dma = pltpu.SemaphoreType.DMA
    sds = jax.ShapeDtypeStruct
    outs = (
        sds((tokens, part_width), F32),
        sds((tokens, part_width), F32),
        sds((tokens, heads * DH), F32),
        sds((m, tokens, part_width), BF16),
        sds((width, hidden), BF16),
        sds((width, hidden), BF16),
        sds((width, heads * DH), BF16),
        sds((8, width), F32),
    )
    shards = pltpu.VMEM((m, chunks, rows, part_width), BF16)
    both = pltpu.VMEM((2, m, chunks, rows, part_width), BF16)
    scratch = [
        shards, both, both, shards, shards, both, both, shards,
        pltpu.VMEM((rows, part_width), F32),
        pltpu.VMEM((m, chunks, 8, rows), F32),
        pltpu.VMEM((tokens, hidden), F32),
        pltpu.VMEM((tokens, width), BF16),
        pltpu.VMEM((tokens, hidden), BF16),
        pltpu.VMEM((tokens, hidden), BF16),
        pltpu.VMEM((tokens, width), BF16),
        pltpu.VMEM((tokens, width), BF16),
        pltpu.VMEM((tokens, 1), F32),
        pltpu.VMEM((tokens, 1), F32),
    ] + [dma((2, m, chunks))] * 8 + [dma((m, chunks))] * 2
    return pl.pallas_call(
        functools.partial(middle_kernel, n, m, heads, chunks),
        out_shape=outs,
        in_specs=[VMEM] * 10,
        out_specs=[VMEM] * len(outs),
        scratch_shapes=scratch,
        compiler_params=pltpu.CompilerParams(
            collective_id=1, has_side_effects=True, vmem_limit_bytes=56 << 20
        ),
        name="middle",
    )(mixed, mixing, first, first_cot, cot_full, gain, shift, expand, expand_bias, contract)


def back_kernel(
    n, m, heads, piece, chunks,
    gm, merged, wts, ro, ext, rank, sendp, pos, kpos, normed, gathered, wq, wv, second, second_cot, fo, gain, bias,
    out_second, grad_second, pq_out, pv_out, vec_out,
    outgoing, arrived, returning, back, unit, poscol, rankcol, sendcol, gl_send, gl_recv, gl_rows, gradk, gradq, grads, wsel,
    prior, incoming, gpair, fo_recv, part_c, got_c, pass_c, total, stats, mean_scr, rstd_scr,
    ins, inr, prs, prr, bks, bkr, gls, glr, fos, fore, rcs, rcr, sts, str_,
):
    g = lax.axis_index("seq")
    me = lax.axis_index("mp")
    tokens, width = normed.shape
    part_width = second.shape[1]
    count = ro.shape[0]
    rounds = count // heads
    blocks = tokens // SPAN
    rows = tokens // chunks
    scaling = 1.0 / math.sqrt(DH)
    greet(n, m, g, me)

    @pl.loop(1, m)
    def _(i):
        peer = lax.rem(me + i, m)
        remote(fo.at[peer], fo_recv.at[me], fos.at[i], fore.at[me], "mp", peer).start()

    pos_col = jnp.transpose(pos[...])
    send_col = jnp.transpose(sendp[...])
    rank_col = jnp.transpose(rank[...])
    for item in range(count):
        poscol[item] = pos_col[:, item : item + 1]
        sendcol[item] = send_col[:, item : item + 1]
        rankcol[item] = rank_col[:, item : item + 1]

    lane = iota((tokens, 128), 1)

    for h in range(heads):
        cols = slice(h * DH, (h + 1) * DH)
        gmh = gm[:, cols]
        inner = jnp.sum(gmh * merged[:, cols], axis=1, keepdims=True)
        for r in range(rounds):
            item = r * heads + h
            w = jnp.sum(jnp.where(lane == item, wts[...], 0.0), axis=1, keepdims=True)
            select = onehot_rows(sendp[item : item + 1, :], tokens)
            outgoing[item] = dot(select, (w * gmh).astype(BF16)).astype(BF16)
            spread(n, g, outgoing.at[item], arrived.at[item], piece, ins.at[item], inr.at[item])
            gs = w * (jnp.sum(gmh * ro[item].astype(F32), axis=1, keepdims=True) - inner)
            row = column_to_row(gs, select)
            for d in range(n):
                gl_send[d, item : item + 1, 0:piece] = row[:, d * piece : (d + 1) * piece]

    gl_recv[g] = gl_send[g]

    @pl.loop(1, n)
    def _(i):
        d = lax.rem(g + i, n)
        remote(gl_send.at[d], gl_recv.at[g], gls, glr, "seq", d).start()

    all_of(gl_recv, n - 1, gls, glr, g).wait_recv()
    gl_rows[...] = jnp.concatenate([gl_recv[d][:, 0:piece] for d in range(n)], axis=1)
    peers_rows = (n - 1) * piece
    before = lax.rem(g + n - 1, n)

    @pl.loop(0, count + 1)
    def _(step):
        @pl.when(step < count)
        def _():
            item = step
            slot = lax.rem(item, 2)
            all_of(arrived.at[item], peers_rows, ins.at[item], inr.at[item], g).wait_recv()
            select = onehot_columns(rankcol[item], tokens)
            grads[...] = dot(select, arrived[item]).astype(BF16)
            wsel[...] = row_to_column(gl_rows[pl.ds(item, 1), :], select)
            w = ext[item, :, 0:DH].astype(F32)
            unit[...] = (w * lax.rsqrt(jnp.sum(w * w, axis=1, keepdims=True) + EPSILON)).astype(BF16)
            for block in range(blocks):
                lo = block * SPAN
                q = ext[item, lo + SPAN : lo + 2 * SPAN, 0:DH]
                keys = unit[lo : lo + 2 * SPAN]
                vals = ext[item, lo : lo + 2 * SPAN, DH : 2 * DH]
                raw = dot_nt(q, keys) * scaling
                key_pos = kpos[block, pl.ds(item, 1), :]
                query_pos = poscol[item, lo : lo + SPAN]
                earlier = key_pos < query_pos
                scores = jnp.where(earlier, raw, jnp.where(key_pos == query_pos, SELF_SCORE, MASKED))
                peak = jnp.max(scores, axis=1, keepdims=True)
                lse = peak + jnp.log(jnp.sum(jnp.exp(scores - peak), axis=1, keepdims=True))
                probs = jnp.exp(scores - lse)
                go = grads[lo : lo + SPAN]
                gp = dot_nt(go, vals)
                inner = jnp.sum(probs * gp, axis=1, keepdims=True)
                gs = jnp.where(earlier, probs * (gp - inner + wsel[lo : lo + SPAN]), 0.0).astype(BF16)
                gradq[slot, lo : lo + SPAN] = dot(gs, keys) * scaling
                gk = dot_tn(gs, q) * scaling
                gv = dot_tn(probs.astype(BF16), go)
                if block == 0:
                    prior[item, :, 0:DH] = gk[0:SPAN].astype(BF16)
                    prior[item, :, DH : 2 * DH] = gv[0:SPAN].astype(BF16)
                else:
                    gradk[slot, lo - SPAN : lo, 0:DH] += gk[0:SPAN]
                    gradk[slot, lo - SPAN : lo, DH : 2 * DH] += gv[0:SPAN]
                gradk[slot, lo : lo + SPAN, 0:DH] = gk[SPAN : 2 * SPAN]
                gradk[slot, lo : lo + SPAN, DH : 2 * DH] = gv[SPAN : 2 * SPAN]
            remote(prior.at[item], incoming.at[item], prs.at[item], prr.at[item], "seq", before).start()

        @pl.when(step > 0)
        def _():
            item = step - 1
            slot = lax.rem(item, 2)
            remote(prior.at[item], incoming.at[item], prs.at[item], prr.at[item], "seq", before).wait_recv()
            gradk[slot, tokens - SPAN :, :] += incoming[item].astype(F32)
            w = ext[item, SPAN:, 0:DH].astype(F32)
            inv = lax.rsqrt(jnp.sum(w * w, axis=1, keepdims=True) + EPSILON)
            gk = gradk[slot, :, 0:DH]
            along = jnp.sum(w * gk, axis=1, keepdims=True)
            gq = gradq[slot] + inv * gk - (inv * inv * inv * along) * w
            done = jnp.concatenate([gq.astype(BF16), gradk[slot, :, DH : 2 * DH].astype(BF16)], axis=1)
            select = onehot_rows(rank[pl.ds(item, 1), :], tokens)
            returning[item] = dot(select, done).astype(BF16)
            spread(n, g, returning.at[item], back.at[item], piece, bks.at[item], bkr.at[item])

    for chunk in range(gathered.shape[1]):
        high = gathered.shape[2]
        x = jnp.concatenate([gathered[s, chunk].astype(F32) for s in range(m)], axis=1)
        mean = jnp.mean(x, axis=1, keepdims=True)
        center = x - mean
        mean_scr[chunk * high : (chunk + 1) * high] = mean
        rstd_scr[chunk * high : (chunk + 1) * high] = lax.rsqrt(
            jnp.mean(center * center, axis=1, keepdims=True) + EPSILON
        )

    gpair[...] = jnp.zeros_like(gpair)

    @pl.loop(0, count)
    def _(item):
        all_of(back.at[item], peers_rows, bks.at[item], bkr.at[item], g).wait_recv()
        select = onehot_columns(sendcol[item], tokens)
        gpair[lax.rem(item, heads)] += dot(select, back[item])

    gq = jnp.concatenate([gpair[h][:, 0:DH] for h in range(heads)], axis=1).astype(BF16)
    gv = jnp.concatenate([gpair[h][:, DH : 2 * DH] for h in range(heads)], axis=1).astype(BF16)
    vec_out[...] = jnp.zeros_like(vec_out)
    sub = gathered.shape[2] // rows
    for chunk in range(chunks):
        part = slice(chunk * rows, (chunk + 1) * rows)
        inside = slice((chunk % sub) * rows, (chunk % sub + 1) * rows)
        term = dot_nt(gq[part], wq[...]) + dot_nt(gv[part], wv[...])
        for s in range(m):
            part_c[s, chunk] = term[:, s * part_width : (s + 1) * part_width].astype(BF16)
        reduce_start(me, m, part_c, got_c, rcs, rcr, chunk)
        x = jnp.concatenate([gathered[s, chunk // sub, inside, :].astype(F32) for s in range(m)], axis=1)
        xhat = (x - mean_scr[part]) * rstd_scr[part]
        e = term * gain[...]
        stats[me, chunk] = pack_stats(
            jnp.sum(e, axis=1, keepdims=True), jnp.sum(e * xhat, axis=1, keepdims=True)
        )
        stats_start(me, m, stats, sts, str_, chunk)
        vec_out[0:1, :] += jnp.sum(term * xhat, axis=0, keepdims=True)
        vec_out[1:2, :] += jnp.sum(term, axis=0, keepdims=True)

    tile = 256

    @pl.loop(0, width // tile)
    def _(k):
        cols = pl.ds(pl.multiple_of(k * tile, tile), tile)
        pq_out[cols, :] = dot_tn(normed[:, cols], gq).astype(BF16)
        pv_out[cols, :] = dot_tn(normed[:, cols], gv).astype(BF16)

    own_cols = pl.multiple_of(me * part_width, part_width)
    gain_own = gain[:, pl.ds(own_cols, part_width)]
    for chunk in range(chunks):
        part = slice(chunk * rows, (chunk + 1) * rows)
        inside = slice((chunk % sub) * rows, (chunk % sub + 1) * rows)
        reduce_step(me, m, part_c, got_c, pass_c, total, rcs, rcr, chunk)
        sums = stats_wait(me, m, stats, sts, str_, chunk) * (1.0 / width)
        xhat = (gathered[me, chunk // sub, inside, :].astype(F32) - mean_scr[part]) * rstd_scr[part]
        grad_second[part, :] = second_cot[part, :] + rstd_scr[part] * (
            total[...] * gain_own - sums[:, 0:1] - xhat * sums[:, 1:2]
        )

    fo_recv[me] = fo[me]

    @pl.loop(1, m)
    def _(i):
        src = lax.rem(me + i, m)
        remote(fo.at[src], fo_recv.at[src], fos.at[i], fore.at[src], "mp", src).wait()

    out_second[...] = (
        second[...]
        + sum(fo_recv[s].astype(F32) for s in range(m))
        + bias[:, pl.ds(own_cols, part_width)]
    )
    for chunk in range(chunks):
        reduce_drain(me, m, part_c, got_c, rcs, rcr, chunk)

    @pl.loop(0, count)
    def _(item):
        all_of(outgoing.at[item], peers_rows, ins.at[item], inr.at[item], g).wait_send()
        all_of(returning.at[item], peers_rows, bks.at[item], bkr.at[item], g).wait_send()
        remote(prior.at[item], incoming.at[item], prs.at[item], prr.at[item], "seq", before).wait_send()

    all_of(gl_send, n - 1, gls, glr, g).wait_send()


def behind(n, m, heads, gm, merged, wts, ro, ext, rank, sendp, pos, kpos, normed, gathered, wq, wv, second, second_cot, fo, gain, bias):
    tokens, part_width = second.shape
    width = normed.shape[1]
    count = ro.shape[0]
    piece = tokens // n
    chunks = 4
    rows = tokens // chunks
    dma = pltpu.SemaphoreType.DMA
    sds = jax.ShapeDtypeStruct
    outs = (
        sds((tokens, part_width), F32),
        sds((tokens, part_width), F32),
        sds((width, heads * DH), BF16),
        sds((width, heads * DH), BF16),
        sds((8, width), F32),
    )
    both = pltpu.VMEM((2, m, chunks, rows, part_width), BF16)
    column = pltpu.VMEM((count, tokens, 1), F32)
    scratch = [
        pltpu.VMEM((count, tokens, DH), BF16),
        pltpu.VMEM((count, tokens, DH), BF16),
        pltpu.VMEM((count, tokens, 2 * DH), BF16),
        pltpu.VMEM((count, tokens, 2 * DH), BF16),
        pltpu.VMEM((SPAN + tokens, DH), BF16),
        column, column, column,
        pltpu.VMEM((n, count, 128), F32),
        pltpu.VMEM((n, count, 128), F32),
        pltpu.VMEM((count, tokens), F32),
        pltpu.VMEM((2, tokens, 2 * DH), F32),
        pltpu.VMEM((2, tokens, DH), F32),
        pltpu.VMEM((tokens, DH), BF16),
        pltpu.VMEM((tokens, 1), F32),
        pltpu.VMEM((count, SPAN, 2 * DH), BF16),
        pltpu.VMEM((count, SPAN, 2 * DH), BF16),
        pltpu.VMEM((heads, tokens, 2 * DH), F32),
        pltpu.VMEM((m, tokens, part_width), BF16),
        pltpu.VMEM((m, chunks, rows, part_width), BF16),
        both, both,
        pltpu.VMEM((rows, part_width), F32),
        pltpu.VMEM((m, chunks, 8, rows), F32),
        pltpu.VMEM((tokens, 1), F32),
        pltpu.VMEM((tokens, 1), F32),
    ] + [dma((count,))] * 6 + [dma, dma, dma((m,)), dma((m,))] + [dma((2, m, chunks))] * 2 + [dma((m, chunks))] * 2
    return pl.pallas_call(
        functools.partial(back_kernel, n, m, heads, piece, chunks),
        out_shape=outs,
        in_specs=[VMEM] * 18,
        out_specs=[VMEM] * len(outs),
        scratch_shapes=scratch,
        compiler_params=pltpu.CompilerParams(
            collective_id=2, has_side_effects=True, vmem_limit_bytes=56 << 20
        ),
        name="back",
    )(gm, merged, wts, ro, ext, rank, sendp, pos, kpos, normed, gathered, wq, wv, second, second_cot, fo, gain, bias)


def local(
    first_half,
    second_half,
    bucket_order,
    attend_gain,
    attend_shift,
    queries,
    values,
    mixing,
    feed_gain,
    feed_shift,
    expand,
    expand_bias,
    contract,
    contract_bias,
    cot_first,
    cot_second,
):
    n = lax.axis_size("seq")
    m = lax.axis_size("mp")
    heads = bucket_order.shape[1]
    order = bucket_order.reshape(-1, bucket_order.shape[2])
    normed, cot_full, ext, ro, wts, mixed, merged, rank, sendp, pos, kpos, gathered = front(
        n, m, heads, second_half, cot_first, cot_second, order,
        attend_gain[None], attend_shift[None], queries, values,
    )
    out_first, grad_first, gm, fo, pe, pc, pm, vec_feed = middle(
        n, m, heads, mixed, mixing, first_half, cot_first, cot_full,
        feed_gain[None], feed_shift[None], expand, expand_bias[None], contract,
    )
    out_second, grad_second, pq, pv, vec_attend = behind(
        n, m, heads, gm, merged, wts, ro, ext, rank, sendp, pos, kpos, normed, gathered,
        queries, values, second_half, cot_second, fo, attend_gain[None], contract_bias[None],
    )

    def summed(part, dim):
        return lax.psum_scatter(part, "seq", scatter_dimension=dim, tiled=True).astype(F32)

    gains = lax.psum(jnp.concatenate([vec_attend[0:2], vec_feed[0:2]]), "mp")
    vectors = summed(jnp.concatenate([gains, vec_feed[2:4]]), 1)
    return (
        out_first,
        out_second,
        grad_first,
        grad_second,
        vectors[0],
        vectors[1],
        summed(pq, 0),
        summed(pv, 0),
        summed(pm, 0).T,
        vectors[2],
        vectors[3],
        summed(pe, 0),
        vectors[5],
        summed(pc, 0).T,
        vectors[4],
    )


def solution(mesh):
    in_specs = (
        P("seq", "mp"),
        P("seq", "mp"),
        P(None, "mp", None),
        P(),
        P(),
        P(None, "mp"),
        P(None, "mp"),
        P("mp", None),
        P(),
        P(),
        P(None, "mp"),
        P("mp"),
        P("mp", None),
        P(),
        P("seq", "mp"),
        P("seq", "mp"),
    )
    out_specs = (
        P("seq", "mp"),
        P("seq", "mp"),
        P("seq", "mp"),
        P("seq", "mp"),
        P("seq"),
        P("seq"),
        P("seq", "mp"),
        P("seq", "mp"),
        P("mp", "seq"),
        P("seq"),
        P("seq"),
        P("seq", "mp"),
        P(("mp", "seq")),
        P("mp", "seq"),
        P("seq"),
    )
    return jax.shard_map(local, mesh=mesh, in_specs=in_specs, out_specs=out_specs, check_vma=False)
```

```python
import functools
import math

import jax
import jax.numpy as jnp
from jax import lax
from jax.experimental import pallas as pl
from jax.experimental.pallas import tpu as pltpu
from jax.sharding import PartitionSpec as P

DH = 128
SPAN = 64
EPSILON = 1e-06
SELF_SCORE = -100000.0
MASKED = -1000000000.0
F32 = jnp.float32
BF16 = jnp.bfloat16
MESH = pl.DeviceIdType.MESH
VMEM = pl.BlockSpec(memory_space=pltpu.VMEM)
ROW = (((1,), (1,)), ((), ()))
COL = (((0,), (0,)), ((), ()))


def dot(a, b):
    return jnp.dot(a, b, preferred_element_type=F32)


def dot_nt(a, b):
    return lax.dot_general(a, b, ROW, preferred_element_type=F32)


def dot_tn(a, b):
    return lax.dot_general(a, b, COL, preferred_element_type=F32)


def remote(src, dst, send_sem, recv_sem, axis, index):
    return pltpu.make_async_remote_copy(
        src_ref=src,
        dst_ref=dst,
        send_sem=send_sem,
        recv_sem=recv_sem,
        device_id={axis: index},
        device_id_type=MESH,
    )


def greet(n, m, g, me):
    barrier = pltpu.get_barrier_semaphore()

    @pl.loop(1, n)
    def _(i):
        pl.semaphore_signal(
            barrier, inc=1, device_id={"seq": lax.rem(g + i, n)}, device_id_type=MESH
        )

    @pl.loop(1, m)
    def _(i):
        pl.semaphore_signal(
            barrier, inc=1, device_id={"mp": lax.rem(me + i, m)}, device_id_type=MESH
        )

    pl.semaphore_wait(barrier, n + m - 2)


def iota(shape, dim):
    return lax.broadcasted_iota(jnp.int32, shape, dim)


def fiota(shape, dim):
    return iota(shape, dim).astype(F32)


def split3(x):
    hi = x.astype(BF16).astype(F32)
    rest = x - hi
    mid = rest.astype(BF16).astype(F32)
    return hi, mid, rest - mid


def columns3(x):
    hi, mid, low = split3(x)
    lane = iota((x.shape[0], 128), 1)
    return jnp.where(lane == 0, hi, jnp.where(lane == 1, mid, jnp.where(lane == 2, low, 0.0)))


def rows3(x):
    hi, mid, low = split3(x)
    part = iota((16, x.shape[1]), 0)
    return jnp.where(part == 0, hi, jnp.where(part == 1, mid, jnp.where(part == 2, low, 0.0)))


def column_to_row(x, onehot):
    packed = jnp.transpose(columns3(x))[0:16].astype(BF16)
    return jnp.sum(dot_nt(packed, onehot), axis=0, keepdims=True)


def row_to_column(x, onehot):
    return jnp.sum(dot_nt(onehot, rows3(x).astype(BF16)), axis=1, keepdims=True)


def onehot_rows(row, count):
    return jnp.where(fiota((count, row.shape[1]), 0) == row, 1.0, 0.0).astype(BF16)


def onehot_columns(column, count):
    return jnp.where(fiota((column.shape[0], count), 1) == column, 1.0, 0.0).astype(BF16)


def line_start(me, m, buf, send, recv, chunk):
    @pl.when(me < m - 1)
    def _():
        remote(buf.at[me, chunk], buf.at[me, chunk], send.at[0, me, chunk], recv.at[0, me, chunk], "mp", me + 1).start()

    @pl.when(me > 0)
    def _():
        remote(buf.at[me, chunk], buf.at[me, chunk], send.at[1, me, chunk], recv.at[1, me, chunk], "mp", me - 1).start()


def line_step(me, m, buf, send, recv, chunk, hop):
    @pl.when(me - hop >= 0)
    def _():
        src = me - hop
        part = buf.at[src, chunk]
        remote(part, part, send.at[0, src, chunk], recv.at[0, src, chunk], "mp", me - 1).wait_recv()

        @pl.when(me < m - 1)
        def _():
            remote(part, part, send.at[0, src, chunk], recv.at[0, src, chunk], "mp", me + 1).start()

    @pl.when(me + hop < m)
    def _():
        src = me + hop
        part = buf.at[src, chunk]
        remote(part, part, send.at[1, src, chunk], recv.at[1, src, chunk], "mp", me + 1).wait_recv()

        @pl.when(me > 0)
        def _():
            remote(part, part, send.at[1, src, chunk], recv.at[1, src, chunk], "mp", me - 1).start()


def line_drain(me, m, buf, send, recv, chunk):
    for hop in range(m):

        @pl.when((me - hop >= 0) & (me < m - 1))
        def _():
            part = buf.at[me - hop, chunk]
            remote(part, part, send.at[0, me - hop, chunk], recv.at[0, me - hop, chunk], "mp", me + 1).wait_send()

        @pl.when((me + hop < m) & (me > 0))
        def _():
            part = buf.at[me + hop, chunk]
            remote(part, part, send.at[1, me + hop, chunk], recv.at[1, me + hop, chunk], "mp", me - 1).wait_send()


def spread(n, g, src, dst, piece, send_sem, recv_sem):
    own = pl.multiple_of(g * piece, piece)
    dst[pl.ds(own, piece)] = src[pl.ds(own, piece)]

    @pl.loop(1, n)
    def _(i):
        d = lax.rem(g + i, n)
        there = pl.multiple_of(d * piece, piece)
        remote(src.at[pl.ds(there, piece)], dst.at[pl.ds(own, piece)], send_sem, recv_sem, "seq", d).start()


def all_of(buf, rows, send_sem, recv_sem, g):
    part = buf.at[pl.ds(0, rows)]
    return remote(part, part, send_sem, recv_sem, "seq", g)


def rank_rows(keys_row, keys_col):
    return jnp.sum(jnp.where(keys_col < keys_row, 1.0, 0.0), axis=0, keepdims=True)


def masked(raw, kpos, poscol, item, blocks):
    keys = jnp.concatenate(
        [jnp.broadcast_to(kpos[b, pl.ds(item, 1), :], (SPAN, 2 * SPAN)) for b in range(blocks)], axis=0
    )
    query = poscol[item]
    earlier = keys < query
    return jnp.where(earlier, raw, jnp.where(keys == query, SELF_SCORE, MASKED)), earlier


def front_kernel(
    n, m, heads, piece,
    second, first_cot, second_cot, order, gain, shift, wq, wv,
    rows_out, cot_out, ext, ro_out, wts_out, mixed_out, merged_out, rank_out, send_out, pos_out, kpos_out, slots_out, zbuf,
    paired, outgoing, arrived, returning, back, unit, pos_ext, poscol, rankcol, sendcol, lsecol, lse_send, lse_recv,
    zs, zr, cs, cr, ins, inr, prs, prr, bks, bkr, lss, lsr,
):
    g = lax.axis_index("seq")
    me = lax.axis_index("mp")
    tokens, width = rows_out.shape
    part_width = second.shape[1]
    count = order.shape[0]
    rounds = count // heads
    blocks = tokens // SPAN
    chunks = zbuf.shape[1]
    chunk_rows = tokens // chunks
    greet(n, m, g, me)

    for chunk in range(chunks):
        zbuf[me, chunk] = second[chunk * chunk_rows : (chunk + 1) * chunk_rows].astype(BF16)
        line_start(me, m, zbuf, zs, zr, chunk)

    start = pl.multiple_of(g * tokens, tokens)
    before = pl.multiple_of(lax.rem(g + n - 1, n) * tokens + tokens - 128, 128)
    own_pos = order[:, pl.ds(start, tokens)].astype(F32)
    pos_ext[:, 0:SPAN] = order[:, pl.ds(before, 128)][:, 128 - SPAN :].astype(F32)
    pos_ext[:, SPAN : SPAN + tokens] = own_pos
    for block in range(blocks):
        kpos_out[block] = pos_ext[:, block * SPAN : (block + 2) * SPAN]
    pos_out[...] = own_pos
    total = order.shape[1]
    place = jnp.right_shift(iota((1, total), 1), tokens.bit_length() - 1).astype(F32)
    high = jnp.right_shift(iota((32, tokens), 1), 4) == iota((32, tokens), 0)
    low = jnp.where(jnp.bitwise_and(iota((16, tokens), 1), 15) == iota((16, tokens), 0), 1.0, 0.0).astype(BF16)
    token = fiota((1, tokens), 1)
    for item in range(count):
        local = order[item : item + 1, :] - g * tokens
        a = jnp.where(jnp.right_shift(local, 4) == iota((32, total), 0), place, 0.0).astype(BF16)
        b = jnp.where(jnp.bitwise_and(local, 15) == iota((16, total), 0), 1.0, 0.0).astype(BF16)
        table = dot_nt(a, b).astype(BF16)
        target = jnp.sum(jnp.where(high, dot(table, low), 0.0), axis=0, keepdims=True)
        send_out[item : item + 1, :] = target * tokens + token
    keys_row = send_out[...]
    keys_col = jnp.transpose(keys_row)
    pos_col = jnp.transpose(own_pos)
    hops = [(hop, chunk) for hop in range(1, m) for chunk in range(chunks)]
    for item in range(count):
        poscol[item] = pos_col[:, item : item + 1]
        send_out[item : item + 1, :] = rank_rows(keys_row[item : item + 1], keys_col[:, item : item + 1])
        rank_out[item : item + 1, :] = rank_rows(own_pos[item : item + 1], pos_col[:, item : item + 1])
        if item < len(hops):
            line_step(me, m, zbuf, zs, zr, hops[item][1], hops[item][0])
    for hop, chunk in hops[count:]:
        line_step(me, m, zbuf, zs, zr, chunk, hop)
    send_col = jnp.transpose(send_out[...])
    rank_col = jnp.transpose(rank_out[...])
    for item in range(count):
        sendcol[item] = send_col[:, item : item + 1]
        rankcol[item] = rank_col[:, item : item + 1]

    for chunk in range(chunks):
        part = slice(chunk * chunk_rows, (chunk + 1) * chunk_rows)
        rows = jnp.concatenate([zbuf[s, chunk].astype(F32) for s in range(m)], axis=1)
        center = rows - jnp.mean(rows, axis=1, keepdims=True)
        var = jnp.mean(center * center, axis=1, keepdims=True)
        normed = (center * lax.rsqrt(var + EPSILON) * gain[...] + shift[...]).astype(BF16)
        rows_out[part, :] = normed
        q = dot(normed, wq[...]).astype(BF16)
        v = dot(normed, wv[...]).astype(BF16)
        for h in range(heads):
            paired[h, part, 0:DH] = q[:, h * DH : (h + 1) * DH]
            paired[h, part, DH : 2 * DH] = v[:, h * DH : (h + 1) * DH]

    for k, cot in enumerate((second_cot, first_cot)[: cot_out.shape[0]]):
        cot_out[k, me] = cot[...].astype(BF16)

        @pl.loop(1, m)
        def _(i):
            peer = lax.rem(me + i, m)
            remote(cot_out.at[k, me], cot_out.at[k, me], cs.at[k, i], cr.at[k, me], "mp", peer).start()

    @pl.loop(0, count)
    def _(item):
        select = onehot_rows(send_out[pl.ds(item, 1), :], tokens)
        outgoing[item] = dot(select, paired[lax.rem(item, heads)]).astype(BF16)
        spread(n, g, outgoing.at[item], arrived.at[item], piece, ins.at[item], inr.at[item])

    peers_rows = (n - 1) * piece
    after = lax.rem(g + 1, n)

    @pl.loop(0, count + 1)
    def _(step):
        @pl.when(step < count)
        def _():
            item = step
            all_of(arrived.at[item], peers_rows, ins.at[item], inr.at[item], g).wait_recv()
            select = onehot_columns(rankcol[item], tokens)
            ext[item, SPAN:, :] = dot(select, arrived[item]).astype(BF16)
            remote(ext.at[item, pl.ds(tokens, SPAN)], ext.at[item, pl.ds(0, SPAN)], prs.at[item], prr.at[item], "seq", after).start()

        @pl.when(step > 0)
        def _():
            item = step - 1
            remote(ext.at[item, pl.ds(tokens, SPAN)], ext.at[item, pl.ds(0, SPAN)], prs.at[item], prr.at[item], "seq", after).wait_recv()
            w = ext[item, :, 0:DH].astype(F32)
            unit[...] = (w * lax.rsqrt(jnp.sum(w * w, axis=1, keepdims=True) + EPSILON)).astype(BF16)
            spans = [slice(block * SPAN, (block + 2) * SPAN) for block in range(blocks)]
            raw = jnp.concatenate(
                [dot_nt(ext[item, span.start + SPAN : span.stop, 0:DH], unit[span]) for span in spans], axis=0
            ) * (1.0 / math.sqrt(DH))
            scores = masked(raw, kpos_out, poscol, item, blocks)[0]
            peak = jnp.max(scores, axis=1, keepdims=True)
            lse = peak + jnp.log(jnp.sum(jnp.exp(scores - peak), axis=1, keepdims=True))
            probs = jnp.exp(scores - lse).astype(BF16)
            outs = jnp.concatenate(
                [dot(probs[span.start : span.start + SPAN], ext[item, span, DH : 2 * DH]) for span in spans], axis=0
            ).astype(BF16)
            select = onehot_rows(rank_out[pl.ds(item, 1), :], tokens)
            returning[item] = dot(select, outs).astype(BF16)
            spread(n, g, returning.at[item], back.at[item], piece, bks.at[item], bkr.at[item])
            packed = jnp.transpose(columns3(lse))[0:16]
            slots_out[pl.ds(item, 1), :] = jnp.sum(packed, axis=0, keepdims=True)
            lse_row = jnp.sum(dot_nt(packed.astype(BF16), select), axis=0, keepdims=True)
            for d in range(n):
                lse_send[d, pl.ds(item, 1), 0:piece] = lse_row[:, d * piece : (d + 1) * piece]

    lse_recv[g] = lse_send[g]

    @pl.loop(1, n)
    def _(i):
        d = lax.rem(g + i, n)
        remote(lse_send.at[d], lse_recv.at[g], lss, lsr, "seq", d).start()

    all_of(lse_recv, n - 1, lss, lsr, g).wait_recv()
    lse_rows = jnp.concatenate([lse_recv[d][:, 0:piece] for d in range(n)], axis=1)
    pos_ext[:, 0:tokens] = lse_rows

    @pl.loop(0, count)
    def _(item):
        all_of(back.at[item], peers_rows, bks.at[item], bkr.at[item], g).wait_recv()
        select = onehot_columns(sendcol[item], tokens)
        ro_out[item] = dot(select, back[item]).astype(BF16)
        lsecol[item] = row_to_column(pos_ext[pl.ds(item, 1), 0:tokens], select)

    lane = iota((tokens, 128), 1)
    weights = jnp.zeros((tokens, 128), F32)
    for h in range(heads):
        logs = [lsecol[r * heads + h] for r in range(rounds)]
        peak = functools.reduce(jnp.maximum, logs)
        full = peak + jnp.log(sum(jnp.exp(x - peak) for x in logs))
        merged = jnp.zeros((tokens, DH), F32)
        for r in range(rounds):
            w = jnp.exp(logs[r] - full)
            weights = jnp.where(lane == r * heads + h, w, weights)
            merged = merged + w * ro_out[r * heads + h].astype(F32)
        merged_out[:, h * DH : (h + 1) * DH] = merged
        mixed_out[:, h * DH : (h + 1) * DH] = merged.astype(BF16)
    wts_out[...] = weights

    for chunk in range(chunks):
        line_drain(me, m, zbuf, zs, zr, chunk)
    for k in range(cot_out.shape[0]):

        @pl.loop(1, m)
        def _(i):
            src = lax.rem(me + i, m)
            remote(cot_out.at[k, src], cot_out.at[k, src], cs.at[k, i], cr.at[k, src], "mp", src).wait()

    @pl.loop(0, count)
    def _(item):
        all_of(outgoing.at[item], peers_rows, ins.at[item], inr.at[item], g).wait_send()
        all_of(returning.at[item], peers_rows, bks.at[item], bkr.at[item], g).wait_send()
        remote(ext.at[item, pl.ds(tokens, SPAN)], ext.at[item, pl.ds(0, SPAN)], prs.at[item], prr.at[item], "seq", after).wait_send()

    all_of(lse_send, n - 1, lss, lsr, g).wait_send()


def front(n, m, heads, second, first_cot, second_cot, order, gain, shift, wq, wv):
    tokens, part_width = second.shape
    width = wq.shape[0]
    count = order.shape[0]
    piece = tokens // n
    blocks = tokens // SPAN
    chunks = 2
    dma = pltpu.SemaphoreType.DMA
    sds = jax.ShapeDtypeStruct
    outs = (
        sds((tokens, width), BF16),
        sds((1, m, tokens, part_width), BF16),
        sds((count, SPAN + tokens, 2 * DH), BF16),
        sds((count, tokens, DH), BF16),
        sds((tokens, 128), F32),
        sds((tokens, heads * DH), BF16),
        sds((tokens, heads * DH), F32),
        sds((count, tokens), F32),
        sds((count, tokens), F32),
        sds((count, tokens), F32),
        sds((blocks, count, 2 * SPAN), F32),
        sds((count, tokens), F32),
        sds((m, chunks, tokens // chunks, part_width), BF16),
    )
    scratch = [
        pltpu.VMEM((heads, tokens, 2 * DH), BF16),
        pltpu.VMEM((count, tokens, 2 * DH), BF16),
        pltpu.VMEM((count, tokens, 2 * DH), BF16),
        pltpu.VMEM((count, tokens, DH), BF16),
        pltpu.VMEM((count, tokens, DH), BF16),
        pltpu.VMEM((SPAN + tokens, DH), BF16),
        pltpu.VMEM((count, tokens + 128), F32),
        pltpu.VMEM((count, tokens, 1), F32),
        pltpu.VMEM((count, tokens, 1), F32),
        pltpu.VMEM((count, tokens, 1), F32),
        pltpu.VMEM((count, tokens, 1), F32),
        pltpu.VMEM((n, count, max(128, piece)), F32),
        pltpu.VMEM((n, count, max(128, piece)), F32),
        dma((2, m, chunks)),
        dma((2, m, chunks)),
        dma((2, m)),
        dma((2, m)),
        dma((count,)),
        dma((count,)),
        dma((count,)),
        dma((count,)),
        dma((count,)),
        dma((count,)),
        dma,
        dma,
    ]
    return pl.pallas_call(
        functools.partial(front_kernel, n, m, heads, piece),
        out_shape=outs,
        in_specs=[VMEM] * 8,
        out_specs=[VMEM] * len(outs),
        scratch_shapes=scratch,
        compiler_params=pltpu.CompilerParams(
            collective_id=0, has_side_effects=True, vmem_limit_bytes=56 << 20
        ),
        name="front",
    )(second, first_cot, second_cot, order, gain, shift, wq, wv)


def reduce_start(me, m, own, got, send, recv, chunk):
    @pl.when(me == 0)
    def _():
        for s in range(m - 1, 0, -1):
            remote(own.at[s, chunk], got.at[0, s, chunk], send.at[0, s, chunk], recv.at[0, s, chunk], "mp", me + 1).start()

    @pl.when(me == m - 1)
    def _():
        for s in range(m - 1):
            remote(own.at[s, chunk], got.at[1, s, chunk], send.at[1, s, chunk], recv.at[1, s, chunk], "mp", me - 1).start()


def reduce_forward(me, m, own, got, passing, send, recv, tick, chunks):
    for direction, chunk, peer in ((0, tick - me, me + 1), (1, tick - (m - 1 - me), me - 1)):

        @pl.when((me > 0) & (me < m - 1) & (chunk >= 0) & (chunk < chunks))
        def _():
            for i in range(m - 1):
                s = m - 1 - i if direction == 0 else i

                @pl.when(s > me if direction == 0 else s < me)
                def _():
                    place = (direction, s, chunk)
                    hop = remote(passing.at[place], got.at[place], send.at[place], recv.at[place], "mp", peer)
                    hop.wait_recv()
                    passing[place] = (own[s, chunk].astype(F32) + got[place].astype(F32)).astype(BF16)
                    hop.start()


def reduce_final(me, m, own, got, total, send, recv, chunk):
    total[...] = own[me, chunk].astype(F32)
    for direction, expected in ((0, me > 0), (1, me < m - 1)):

        @pl.when(expected)
        def _():
            place = (direction, me, chunk)
            remote(own.at[me, chunk], got.at[place], send.at[place], recv.at[place], "mp", me).wait_recv()
            total[...] += got[place].astype(F32)


def reduce_drain(me, m, own, got, send, recv, chunk):
    for s in range(m):
        for direction, sent in ((0, me < s), (1, me > s)):
            place = (direction, s, chunk)

            @pl.when(sent)
            def _():
                remote(own.at[s, chunk], got.at[place], send.at[place], recv.at[place], "mp", me).wait_send()


def pack_stats(a, b):
    lane = iota((a.shape[0], 128), 1)
    return jnp.transpose(jnp.where(lane == 0, a, jnp.where(lane == 1, b, 0.0)))[0:8]


def stats_start(me, m, stats, send, recv, chunk):
    @pl.loop(1, m)
    def _(i):
        remote(stats.at[me, chunk], stats.at[me, chunk], send.at[i, chunk], recv.at[me, chunk], "mp", lax.rem(me + i, m)).start()


def stats_wait(me, m, stats, send, recv, chunk):
    @pl.loop(1, m)
    def _(i):
        src = lax.rem(me + i, m)
        remote(stats.at[src, chunk], stats.at[src, chunk], send.at[i, chunk], recv.at[src, chunk], "mp", src).wait()

    return jnp.transpose(sum(stats[s, chunk] for s in range(m)))


def pair_send(g, q, own, got, send, recv):
    odd = lax.rem(g, 2)
    return remote(own.at[2 * q + 1 - odd], got.at[q], send.at[q], recv.at[q], "seq", g + 1 - 2 * odd)


def pair_pass(g, q, own, got, passing, fin, send1, recv1, send2, recv2):
    odd = lax.rem(g, 2)
    home = g // 2
    pair_send(g, q, own, got, send1, recv1).wait_recv()
    passing[q] = (own[2 * q + odd].astype(F32) + got[q].astype(F32)).astype(BF16)

    @pl.when(q != home)
    def _():
        remote(passing.at[q], fin.at[home], send2.at[q], recv2.at[home], "seq", 2 * q + odd).start()


def pair_total(g, pairs, own, got, fin, send2, recv2):
    home = g // 2

    @pl.loop(1, pairs)
    def _(i):
        q = lax.rem(home + i, pairs)
        remote(fin.at[q], fin.at[q], send2.at[q], recv2.at[q], "seq", g).wait_recv()

    fin[home] = (own[2 * home + lax.rem(g, 2)].astype(F32) + got[home].astype(F32)).astype(BF16)


def pair_drain(g, pairs, own, got, passing, fin, send1, recv1, send2, recv2):
    home = g // 2

    @pl.loop(0, pairs)
    def _(q):
        pair_send(g, q, own, got, send1, recv1).wait_send()

        @pl.when(q != home)
        def _():
            remote(passing.at[q], fin.at[home], send2.at[q], recv2.at[home], "seq", g).wait_send()


def middle_kernel(
    n, m, heads, chunks,
    mixed, mixing, first, first_cot, cot_full, gain, shift, expand, expand_bias, contract,
    out_first, grad_first, gm_out, fo_out, pe_out, pc_out, pm_out, vec_out,
    part_a, got_a, pass_a, full_a, part_b, got_b, pass_b, full_b, total, stats,
    gact, feed, active, gpre, grad_feed, grad_att, mean_scr, rstd_scr, w_own, w_got, w_pass, w_fin,
    ras, rar, gas, gar, rbs, rbr, gbs, gbr, sts, str_, w1s, w1r, w2s, w2r,
):
    g = lax.axis_index("seq")
    me = lax.axis_index("mp")
    tokens, part_width = first.shape
    width = mixing.shape[1]
    hidden = expand.shape[1]
    rows = tokens // chunks
    hops = m - 1
    pairs = n // 2
    slice_rows = width // n
    tile = max(256, 2 * slice_rows)
    tiles = width // tile
    tile_pairs = tile // slice_rows // 2
    greet(n, m, g, me)

    def scatter(part, value, chunk):
        for s in range(m):
            part[s, chunk] = value[:, s * part_width : (s + 1) * part_width].astype(BF16)

    def gather(full, chunk):
        return jnp.concatenate([full[s, chunk] for s in range(m)], axis=1)

    def rows_of(chunk):
        return pl.ds(pl.multiple_of(chunk * rows, rows), rows)

    def during(tick, delay, body, length=chunks):
        @pl.when((tick >= delay) & (tick < delay + length))
        def _():
            body(tick - delay)

    for chunk in range(chunks):
        scatter(part_a, dot(mixed[chunk * rows : (chunk + 1) * rows, :], mixing[...]), chunk)
        reduce_start(me, m, part_a, got_a, ras, rar, chunk)
    own_cols = pl.multiple_of(me * part_width, part_width)
    gain_own = gain[:, pl.ds(own_cols, part_width)]
    vec_out[...] = jnp.zeros_like(vec_out)

    def finish_first(chunk):
        part = rows_of(chunk)
        reduce_final(me, m, part_a, got_a, total, ras, rar, chunk)
        stream = first[part, :] + total[...]
        out_first[part, :] = stream
        full_a[me, chunk] = stream.astype(BF16)
        line_start(me, m, full_a, gas, gar, chunk)

    def back_of_feed(chunk):
        part = rows_of(chunk)
        cot = jnp.concatenate([cot_full[0, s, part, :] for s in range(m)], axis=1)
        grad_feed[part, :] = cot
        gact[part, :] = dot_nt(cot, contract[...])

    def feed_forward(chunk):
        part = rows_of(chunk)
        x = gather(full_a, chunk).astype(F32)
        mean = jnp.mean(x, axis=1, keepdims=True)
        center = x - mean
        rstd = lax.rsqrt(jnp.mean(center * center, axis=1, keepdims=True) + EPSILON)
        mean_scr[part, :] = mean
        rstd_scr[part, :] = rstd
        xhat = center * rstd
        normed = (xhat * gain[...] + shift[...]).astype(BF16)
        feed[part, :] = normed
        pre = dot(normed, expand[...]) + expand_bias[...]
        gate = 0.5 * (1.0 + lax.erf(pre * (1.0 / math.sqrt(2.0))))
        active[part, :] = (pre * gate).astype(BF16)
        slope = gate + pre * jnp.exp(-0.5 * pre * pre) * (1.0 / math.sqrt(2.0 * math.pi))
        back = (gact[part, :] * slope).astype(BF16)
        gpre[part, :] = back
        term = dot_nt(back, expand[...])
        scatter(part_b, term, chunk)
        reduce_start(me, m, part_b, got_b, rbs, rbr, chunk)
        e = term * gain[...]
        stats[me, chunk] = pack_stats(
            jnp.sum(e, axis=1, keepdims=True), jnp.sum(e * xhat, axis=1, keepdims=True)
        )
        stats_start(me, m, stats, sts, str_, chunk)
        vec_out[0:1, :] += jnp.sum(term * xhat, axis=0, keepdims=True)
        vec_out[1:2, :] += jnp.sum(term, axis=0, keepdims=True)
        vec_out[2:3, :] += jnp.sum(grad_feed[part, :].astype(F32), axis=0, keepdims=True)
        vec_out[3:4, :] += jnp.sum(back.astype(F32), axis=0, keepdims=True)

    def finish_grad(chunk):
        part = rows_of(chunk)
        reduce_final(me, m, part_b, got_b, total, rbs, rbr, chunk)
        sums = stats_wait(me, m, stats, sts, str_, chunk) * (1.0 / width)
        rstd = rstd_scr[part, :]
        xhat = (full_a[me, chunk].astype(F32) - mean_scr[part, :]) * rstd
        stream = first_cot[part, :] + rstd * (
            total[...] * gain_own - sums[:, 0:1] - xhat * sums[:, 1:2]
        )
        grad_first[part, :] = stream
        full_b[me, chunk] = stream.astype(BF16)
        line_start(me, m, full_b, gbs, gbr, chunk)

    def merged_grad(chunk):
        part = rows_of(chunk)
        att = gather(full_b, chunk)
        grad_att[part, :] = att
        gm_out[part, :] = dot_nt(att, mixing[...])

    def weight_tile(k):
        cols = pl.ds(pl.multiple_of(k * tile, tile), tile)
        for lanes, left, right in (
            (slice(0, hidden), feed, gpre),
            (slice(hidden, 2 * hidden), grad_feed, active),
        ):
            product = dot_tn(left[:, cols], right[...]).astype(BF16)
            for i in range(2 * tile_pairs):
                w_own[k * 2 * tile_pairs + i, :, lanes] = product[i * slice_rows : (i + 1) * slice_rows]
        for i in range(tile_pairs):
            pair_send(g, k * tile_pairs + i, w_own, w_got, w1s, w1r).start()

    def weight_pass(k):
        for i in range(tile_pairs):
            pair_pass(g, k * tile_pairs + i, w_own, w_got, w_pass, w_fin, w1s, w1r, w2s, w2r)

    def feed_out(k):
        s = k
        fo_out[s] = dot(active[...], contract[:, pl.ds(pl.multiple_of(s * part_width, part_width), part_width)]).astype(BF16)

    @pl.loop(0, chunks + 4 * hops)
    def _(tick):
        reduce_forward(me, m, part_a, got_a, pass_a, ras, rar, tick, chunks)
        reduce_forward(me, m, part_b, got_b, pass_b, rbs, rbr, tick - 2 * hops, chunks)
        for hop in range(hops, 0, -1):
            during(tick, hops + hop, lambda chunk: line_step(me, m, full_a, gas, gar, chunk, hop))
            during(tick, 3 * hops + hop, lambda chunk: line_step(me, m, full_b, gbs, gbr, chunk, hop))
        during(tick, hops, finish_first)
        during(tick, 3 * hops, finish_grad)
        during(tick, 4 * hops, merged_grad)
        during(tick, 0, back_of_feed)
        during(tick, 2 * hops, feed_forward)
        during(tick, chunks + 2 * hops + 1, weight_pass, tiles)
        during(tick, chunks + 2 * hops, weight_tile, tiles)

    @pl.loop(0, m)
    def _(s):
        feed_out(s)

    for k in range(2 * hops, tiles):
        weight_tile(k)
    for k in range(tiles):
        if k + 1 >= 2 * hops:
            weight_pass(k)

    @pl.loop(0, width // 256)
    def _(k):
        cols = pl.ds(pl.multiple_of(k * 256, 256), 256)
        pm_out[cols, :] = dot_tn(grad_att[:, cols], mixed[...]).astype(BF16)

    pair_total(g, pairs, w_own, w_got, w_fin, w2s, w2r)
    pe_out[...] = sum(w_fin[q, :, 0:hidden].astype(F32) for q in range(pairs))
    pc_out[...] = jnp.transpose(sum(w_fin[q, :, hidden : 2 * hidden].astype(F32) for q in range(pairs)))

    for chunk in range(chunks):
        reduce_drain(me, m, part_a, got_a, ras, rar, chunk)
        reduce_drain(me, m, part_b, got_b, rbs, rbr, chunk)
        line_drain(me, m, full_a, gas, gar, chunk)
        line_drain(me, m, full_b, gbs, gbr, chunk)
    pair_drain(g, pairs, w_own, w_got, w_pass, w_fin, w1s, w1r, w2s, w2r)


def middle(n, m, heads, mixed, mixing, first, first_cot, cot_full, gain, shift, expand, expand_bias, contract):
    tokens, part_width = first.shape
    width = mixing.shape[1]
    hidden = expand.shape[1]
    chunks = 4
    rows = tokens // chunks
    slice_rows = width // n
    dma = pltpu.SemaphoreType.DMA
    sds = jax.ShapeDtypeStruct
    outs = (
        sds((tokens, part_width), F32),
        sds((tokens, part_width), F32),
        sds((tokens, heads * DH), F32),
        sds((m, tokens, part_width), BF16),
        sds((slice_rows, hidden), F32),
        sds((hidden, slice_rows), F32),
        sds((width, heads * DH), BF16),
        sds((8, width), F32),
    )
    shards = pltpu.VMEM((m, chunks, rows, part_width), BF16)
    both = pltpu.VMEM((2, m, chunks, rows, part_width), BF16)
    pieces = pltpu.VMEM((n // 2, slice_rows, 2 * hidden), BF16)
    scratch = [
        shards, both, both, shards, shards, both, both, shards,
        pltpu.VMEM((rows, part_width), F32),
        pltpu.VMEM((m, chunks, 8, rows), F32),
        pltpu.VMEM((tokens, hidden), F32),
        pltpu.VMEM((tokens, width), BF16),
        pltpu.VMEM((tokens, hidden), BF16),
        pltpu.VMEM((tokens, hidden), BF16),
        pltpu.VMEM((tokens, width), BF16),
        pltpu.VMEM((tokens, width), BF16),
        pltpu.VMEM((tokens, 1), F32),
        pltpu.VMEM((tokens, 1), F32),
        pltpu.VMEM((n, slice_rows, 2 * hidden), BF16),
        pieces, pieces, pieces,
    ] + [dma((2, m, chunks))] * 8 + [dma((m, chunks))] * 2 + [dma((n // 2,))] * 4
    return pl.pallas_call(
        functools.partial(middle_kernel, n, m, heads, chunks),
        out_shape=outs,
        in_specs=[VMEM] * 10,
        out_specs=[VMEM] * len(outs),
        scratch_shapes=scratch,
        compiler_params=pltpu.CompilerParams(
            collective_id=1, has_side_effects=True, vmem_limit_bytes=60 << 20
        ),
        name="middle",
    )(mixed, mixing, first, first_cot, cot_full, gain, shift, expand, expand_bias, contract)


def back_kernel(
    n, m, heads, piece, chunks,
    gm, merged, wts, ro, ext, rank, sendp, pos, kpos, slots, normed, gathered, wq, wv, second, second_cot, fo, pm, vec_feed, gain, bias,
    out_second, grad_second, pq_out, pv_out, pm_out, vec_out,
    outgoing, arrived, returning, back, unit, poscol, rankcol, sendcol, lsecol, gl_send, gl_recv, gl_rows, gradk, gradq, grads, wsel,
    prior, incoming, gpair, fo_recv, part_c, got_c, pass_c, total, stats, mean_scr, rstd_scr, w_own, w_got, w_pass, w_fin, vec, vec_send, vec_recv, vec_all,
    ins, inr, prs, prr, bks, bkr, gls, glr, fos, fore, rcs, rcr, sts, str_, w1s, w1r, w2s, w2r, vs, vr, vzs, vzr,
):
    g = lax.axis_index("seq")
    me = lax.axis_index("mp")
    tokens, width = normed.shape
    part_width = second.shape[1]
    count = ro.shape[0]
    rounds = count // heads
    blocks = tokens // SPAN
    rows = tokens // chunks
    scaling = 1.0 / math.sqrt(DH)
    greet(n, m, g, me)

    @pl.loop(1, m)
    def _(i):
        peer = lax.rem(me + i, m)
        remote(fo.at[peer], fo_recv.at[me], fos.at[i], fore.at[me], "mp", peer).start()

    pos_col = jnp.transpose(pos[...])
    send_col = jnp.transpose(sendp[...])
    rank_col = jnp.transpose(rank[...])
    lse_col = jnp.transpose(slots[...])
    for item in range(count):
        poscol[item] = pos_col[:, item : item + 1]
        lsecol[item] = lse_col[:, item : item + 1]
        sendcol[item] = send_col[:, item : item + 1]
        rankcol[item] = rank_col[:, item : item + 1]

    lane = iota((tokens, 128), 1)

    for h in range(heads):
        cols = slice(h * DH, (h + 1) * DH)
        gmh = gm[:, cols]
        inner = jnp.sum(gmh * merged[:, cols], axis=1, keepdims=True)
        for r in range(rounds):
            item = r * heads + h
            w = jnp.sum(jnp.where(lane == item, wts[...], 0.0), axis=1, keepdims=True)
            select = onehot_rows(sendp[item : item + 1, :], tokens)
            outgoing[item] = dot(select, (w * gmh).astype(BF16)).astype(BF16)
            spread(n, g, outgoing.at[item], arrived.at[item], piece, ins.at[item], inr.at[item])
            gs = w * (jnp.sum(gmh * ro[item].astype(F32), axis=1, keepdims=True) - inner)
            row = column_to_row(gs, select)
            for d in range(n):
                gl_send[d, item : item + 1, 0:piece] = row[:, d * piece : (d + 1) * piece]

    gl_recv[g] = gl_send[g]

    @pl.loop(1, n)
    def _(i):
        d = lax.rem(g + i, n)
        remote(gl_send.at[d], gl_recv.at[g], gls, glr, "seq", d).start()

    all_of(gl_recv, n - 1, gls, glr, g).wait_recv()
    gl_rows[...] = jnp.concatenate([gl_recv[d][:, 0:piece] for d in range(n)], axis=1)
    peers_rows = (n - 1) * piece
    before = lax.rem(g + n - 1, n)

    @pl.loop(0, count + 1)
    def _(step):
        @pl.when(step < count)
        def _():
            item = step
            slot = lax.rem(item, 2)
            all_of(arrived.at[item], peers_rows, ins.at[item], inr.at[item], g).wait_recv()
            select = onehot_columns(rankcol[item], tokens)
            grads[...] = dot(select, arrived[item]).astype(BF16)
            wsel[...] = row_to_column(gl_rows[pl.ds(item, 1), :], select)
            w = ext[item, :, 0:DH].astype(F32)
            unit[...] = (w * lax.rsqrt(jnp.sum(w * w, axis=1, keepdims=True) + EPSILON)).astype(BF16)
            spans = [slice(block * SPAN, (block + 2) * SPAN) for block in range(blocks)]
            queries = [ext[item, span.start + SPAN : span.stop, 0:DH] for span in spans]
            raw = jnp.concatenate([dot_nt(q, unit[span]) for q, span in zip(queries, spans)], axis=0) * scaling
            gp = jnp.concatenate(
                [dot_nt(grads[span.start : span.start + SPAN], ext[item, span, DH : 2 * DH]) for span in spans], axis=0
            )
            scores, earlier = masked(raw, kpos, poscol, item, blocks)
            probs = jnp.exp(scores - lsecol[item])
            inner = jnp.sum(probs * gp, axis=1, keepdims=True)
            gs = (jnp.where(earlier, probs * (gp - inner + wsel[...]), 0.0) * scaling).astype(BF16)
            low = probs.astype(BF16)
            gradq[slot] = jnp.concatenate(
                [dot(gs[span.start : span.start + SPAN], unit[span]) for span in spans], axis=0
            )
            gk = [dot_tn(gs[span.start : span.start + SPAN], q) for q, span in zip(queries, spans)]
            gv = [
                dot_tn(low[span.start : span.start + SPAN], grads[span.start : span.start + SPAN])
                for span in spans
            ]
            for lanes, slots in ((slice(0, DH), gk), (slice(DH, 2 * DH), gv)):
                prior[item, :, lanes] = slots[0][0:SPAN].astype(BF16)
                for block in range(blocks):
                    lo = block * SPAN
                    own = slots[block][SPAN : 2 * SPAN]
                    if block + 1 < blocks:
                        own = own + slots[block + 1][0:SPAN]
                    gradk[slot, lo : lo + SPAN, lanes] = own
            remote(prior.at[item], incoming.at[item], prs.at[item], prr.at[item], "seq", before).start()

        @pl.when(step > 0)
        def _():
            item = step - 1
            slot = lax.rem(item, 2)
            remote(prior.at[item], incoming.at[item], prs.at[item], prr.at[item], "seq", before).wait_recv()
            gradk[slot, tokens - SPAN :, :] += incoming[item].astype(F32)
            w = ext[item, SPAN:, 0:DH].astype(F32)
            inv = lax.rsqrt(jnp.sum(w * w, axis=1, keepdims=True) + EPSILON)
            gk = gradk[slot, :, 0:DH]
            along = jnp.sum(w * gk, axis=1, keepdims=True)
            gq = gradq[slot] + inv * gk - (inv * inv * inv * along) * w
            done = jnp.concatenate([gq.astype(BF16), gradk[slot, :, DH : 2 * DH].astype(BF16)], axis=1)
            select = onehot_rows(rank[pl.ds(item, 1), :], tokens)
            returning[item] = dot(select, done).astype(BF16)
            spread(n, g, returning.at[item], back.at[item], piece, bks.at[item], bkr.at[item])

    for chunk in range(gathered.shape[1]):
        high = gathered.shape[2]
        x = jnp.concatenate([gathered[s, chunk].astype(F32) for s in range(m)], axis=1)
        mean = jnp.mean(x, axis=1, keepdims=True)
        center = x - mean
        mean_scr[chunk * high : (chunk + 1) * high] = mean
        rstd_scr[chunk * high : (chunk + 1) * high] = lax.rsqrt(
            jnp.mean(center * center, axis=1, keepdims=True) + EPSILON
        )

    gpair[...] = jnp.zeros_like(gpair)

    @pl.loop(0, count)
    def _(item):
        all_of(back.at[item], peers_rows, bks.at[item], bkr.at[item], g).wait_recv()
        select = onehot_columns(sendcol[item], tokens)
        gpair[lax.rem(item, heads)] += dot(select, back[item])

    gq = jnp.concatenate([gpair[h][:, 0:DH] for h in range(heads)], axis=1).astype(BF16)
    gv = jnp.concatenate([gpair[h][:, DH : 2 * DH] for h in range(heads)], axis=1).astype(BF16)
    vec[0:2, :] = jnp.zeros((2, width), F32)
    vec[2:6, :] = vec_feed[0:4, :]
    vec[6:8, :] = jnp.zeros((2, width), F32)
    sub = gathered.shape[2] // rows
    for chunk in range(chunks):
        part = slice(chunk * rows, (chunk + 1) * rows)
        inside = slice((chunk % sub) * rows, (chunk % sub + 1) * rows)
        term = dot_nt(gq[part], wq[...]) + dot_nt(gv[part], wv[...])
        for s in range(m):
            part_c[s, chunk] = term[:, s * part_width : (s + 1) * part_width].astype(BF16)
        reduce_start(me, m, part_c, got_c, rcs, rcr, chunk)
        x = jnp.concatenate([gathered[s, chunk // sub, inside, :].astype(F32) for s in range(m)], axis=1)
        xhat = (x - mean_scr[part]) * rstd_scr[part]
        e = term * gain[...]
        stats[me, chunk] = pack_stats(
            jnp.sum(e, axis=1, keepdims=True), jnp.sum(e * xhat, axis=1, keepdims=True)
        )
        stats_start(me, m, stats, sts, str_, chunk)
        vec[0:1, :] += jnp.sum(term * xhat, axis=0, keepdims=True)
        vec[1:2, :] += jnp.sum(term, axis=0, keepdims=True)

    pairs = n // 2
    slice_rows = width // n
    for d in range(n):
        vec_send[d, :, 0:slice_rows] = vec[:, d * slice_rows : (d + 1) * slice_rows]
    vec_recv[g] = vec_send[g]

    @pl.loop(1, n)
    def _(i):
        d = lax.rem(g + i, n)
        remote(vec_send.at[d], vec_recv.at[g], vs, vr, "seq", d).start()

    tile = max(256, 2 * slice_rows)
    tile_pairs = tile // slice_rows // 2
    own_heads = heads * DH

    @pl.loop(0, width // tile)
    def _(k):
        cols = pl.ds(pl.multiple_of(k * tile, tile), tile)
        products = (
            dot_tn(normed[:, cols], gq).astype(BF16),
            dot_tn(normed[:, cols], gv).astype(BF16),
            pm[cols, :],
        )
        for j, product in enumerate(products):
            for i in range(2 * tile_pairs):
                w_own[k * 2 * tile_pairs + i, :, j * own_heads : (j + 1) * own_heads] = product[
                    i * slice_rows : (i + 1) * slice_rows
                ]
        for i in range(tile_pairs):
            pair_send(g, k * tile_pairs + i, w_own, w_got, w1s, w1r).start()

    own_cols = pl.multiple_of(me * part_width, part_width)
    gain_own = gain[:, pl.ds(own_cols, part_width)]
    hops = m - 1

    def finish(chunk):
        part = pl.ds(pl.multiple_of(chunk * rows, rows), rows)
        inside = pl.ds(pl.multiple_of(lax.rem(chunk, sub) * rows, rows), rows)
        reduce_final(me, m, part_c, got_c, total, rcs, rcr, chunk)
        sums = stats_wait(me, m, stats, sts, str_, chunk) * (1.0 / width)
        rstd = rstd_scr[part, :]
        xhat = (gathered[me, chunk // sub, inside, :].astype(F32) - mean_scr[part, :]) * rstd
        grad_second[part, :] = second_cot[part, :] + rstd * (
            total[...] * gain_own - sums[:, 0:1] - xhat * sums[:, 1:2]
        )

    @pl.loop(0, pairs)
    def _(q):
        pair_pass(g, q, w_own, w_got, w_pass, w_fin, w1s, w1r, w2s, w2r)

    all_of(vec_recv, n - 1, vs, vr, g).wait_recv()
    vec_all[me] = sum(vec_recv[d] for d in range(n))

    @pl.loop(1, m)
    def _(i):
        peer = lax.rem(me + i, m)
        remote(vec_all.at[me], vec_all.at[me], vzs.at[i], vzr.at[me], "mp", peer).start()

    @pl.loop(0, chunks + hops)
    def _(tick):
        reduce_forward(me, m, part_c, got_c, pass_c, rcs, rcr, tick, chunks)

        @pl.when(tick >= hops)
        def _():
            finish(tick - hops)

    fo_recv[me] = fo[me]

    @pl.loop(1, m)
    def _(i):
        src = lax.rem(me + i, m)
        remote(fo.at[src], fo_recv.at[src], fos.at[i], fore.at[src], "mp", src).wait()

    out_second[...] = (
        second[...]
        + sum(fo_recv[s].astype(F32) for s in range(m))
        + bias[:, pl.ds(own_cols, part_width)]
    )
    @pl.loop(1, m)
    def _(i):
        src = lax.rem(me + i, m)
        remote(vec_all.at[src], vec_all.at[src], vzs.at[i], vzr.at[src], "mp", src).wait()

    row = iota((8, vec_all.shape[2]), 0)
    vec_out[...] = jnp.where(row < 4, sum(vec_all[s] for s in range(m)), vec_all[me])
    pair_total(g, pairs, w_own, w_got, w_fin, w2s, w2r)
    for j, out in enumerate((pq_out, pv_out)):
        out[...] = sum(w_fin[q, :, j * own_heads : (j + 1) * own_heads].astype(F32) for q in range(pairs))
    pm_out[...] = jnp.transpose(
        sum(w_fin[q, :, 2 * own_heads : 3 * own_heads].astype(F32) for q in range(pairs))
    )
    for chunk in range(chunks):
        reduce_drain(me, m, part_c, got_c, rcs, rcr, chunk)
    pair_drain(g, pairs, w_own, w_got, w_pass, w_fin, w1s, w1r, w2s, w2r)
    all_of(vec_send, n - 1, vs, vr, g).wait_send()

    @pl.loop(0, count)
    def _(item):
        all_of(outgoing.at[item], peers_rows, ins.at[item], inr.at[item], g).wait_send()
        all_of(returning.at[item], peers_rows, bks.at[item], bkr.at[item], g).wait_send()
        remote(prior.at[item], incoming.at[item], prs.at[item], prr.at[item], "seq", before).wait_send()

    all_of(gl_send, n - 1, gls, glr, g).wait_send()


def behind(n, m, heads, gm, merged, wts, ro, ext, rank, sendp, pos, kpos, slots, normed, gathered, wq, wv, second, second_cot, fo, pm, vec_feed, gain, bias):
    tokens, part_width = second.shape
    width = normed.shape[1]
    count = ro.shape[0]
    piece = tokens // n
    chunks = 4
    rows = tokens // chunks
    slice_rows = width // n
    dma = pltpu.SemaphoreType.DMA
    sds = jax.ShapeDtypeStruct
    outs = (
        sds((tokens, part_width), F32),
        sds((tokens, part_width), F32),
        sds((slice_rows, heads * DH), F32),
        sds((slice_rows, heads * DH), F32),
        sds((heads * DH, slice_rows), F32),
        sds((8, max(128, slice_rows)), F32),
    )
    both = pltpu.VMEM((2, m, chunks, rows, part_width), BF16)
    column = pltpu.VMEM((count, tokens, 1), F32)
    pieces = pltpu.VMEM((n // 2, slice_rows, 3 * heads * DH), BF16)
    scratch = [
        pltpu.VMEM((count, tokens, DH), BF16),
        pltpu.VMEM((count, tokens, DH), BF16),
        pltpu.VMEM((count, tokens, 2 * DH), BF16),
        pltpu.VMEM((count, tokens, 2 * DH), BF16),
        pltpu.VMEM((SPAN + tokens, DH), BF16),
        column, column, column, column,
        pltpu.VMEM((n, count, max(128, piece)), F32),
        pltpu.VMEM((n, count, max(128, piece)), F32),
        pltpu.VMEM((count, tokens), F32),
        pltpu.VMEM((2, tokens, 2 * DH), F32),
        pltpu.VMEM((2, tokens, DH), F32),
        pltpu.VMEM((tokens, DH), BF16),
        pltpu.VMEM((tokens, 1), F32),
        pltpu.VMEM((count, SPAN, 2 * DH), BF16),
        pltpu.VMEM((count, SPAN, 2 * DH), BF16),
        pltpu.VMEM((heads, tokens, 2 * DH), F32),
        pltpu.VMEM((m, tokens, part_width), BF16),
        pltpu.VMEM((m, chunks, rows, part_width), BF16),
        both, both,
        pltpu.VMEM((rows, part_width), F32),
        pltpu.VMEM((m, chunks, 8, rows), F32),
        pltpu.VMEM((tokens, 1), F32),
        pltpu.VMEM((tokens, 1), F32),
        pltpu.VMEM((n, slice_rows, 3 * heads * DH), BF16),
        pieces, pieces, pieces,
        pltpu.VMEM((8, width), F32),
        pltpu.VMEM((n, 8, max(128, slice_rows)), F32),
        pltpu.VMEM((n, 8, max(128, slice_rows)), F32),
        pltpu.VMEM((m, 8, max(128, slice_rows)), F32),
    ] + [dma((count,))] * 6 + [dma, dma, dma((m,)), dma((m,))] + [dma((2, m, chunks))] * 2 + [dma((m, chunks))] * 2 + [dma((n // 2,))] * 4 + [dma, dma, dma((m,)), dma((m,))]
    return pl.pallas_call(
        functools.partial(back_kernel, n, m, heads, piece, chunks),
        out_shape=outs,
        in_specs=[VMEM] * 21,
        out_specs=[VMEM] * len(outs),
        scratch_shapes=scratch,
        compiler_params=pltpu.CompilerParams(
            collective_id=2, has_side_effects=True, vmem_limit_bytes=60 << 20
        ),
        name="back",
    )(gm, merged, wts, ro, ext, rank, sendp, pos, kpos, slots, normed, gathered, wq, wv, second, second_cot, fo, pm, vec_feed, gain, bias)


def local(
    first_half,
    second_half,
    bucket_order,
    attend_gain,
    attend_shift,
    queries,
    values,
    mixing,
    feed_gain,
    feed_shift,
    expand,
    expand_bias,
    contract,
    contract_bias,
    cot_first,
    cot_second,
):
    n = lax.axis_size("seq")
    m = lax.axis_size("mp")
    heads = bucket_order.shape[1]
    order = bucket_order.reshape(-1, bucket_order.shape[2])
    normed, cot_full, ext, ro, wts, mixed, merged, rank, sendp, pos, kpos, slots, gathered = front(
        n, m, heads, second_half, cot_first, cot_second, order,
        attend_gain[None], attend_shift[None], queries, values,
    )
    out_first, grad_first, gm, fo, pe, pc, pm, vec_feed = middle(
        n, m, heads, mixed, mixing, first_half, cot_first, cot_full,
        feed_gain[None], feed_shift[None], expand, expand_bias[None], contract,
    )
    out_second, grad_second, pq, pv, pm, vectors = behind(
        n, m, heads, gm, merged, wts, ro, ext, rank, sendp, pos, kpos, slots, normed, gathered,
        queries, values, second_half, cot_second, fo, pm, vec_feed, attend_gain[None], contract_bias[None],
    )
    vectors = vectors[:, 0 : pq.shape[0]]
    return (
        out_first,
        out_second,
        grad_first,
        grad_second,
        vectors[0],
        vectors[1],
        pq,
        pv,
        pm,
        vectors[2],
        vectors[3],
        pe,
        vectors[5],
        pc,
        vectors[4],
    )


def solution(mesh):
    in_specs = (
        P("seq", "mp"),
        P("seq", "mp"),
        P(None, "mp", None),
        P(),
        P(),
        P(None, "mp"),
        P(None, "mp"),
        P("mp", None),
        P(),
        P(),
        P(None, "mp"),
        P("mp"),
        P("mp", None),
        P(),
        P("seq", "mp"),
        P("seq", "mp"),
    )
    out_specs = (
        P("seq", "mp"),
        P("seq", "mp"),
        P("seq", "mp"),
        P("seq", "mp"),
        P("seq"),
        P("seq"),
        P("seq", "mp"),
        P("seq", "mp"),
        P("mp", "seq"),
        P("seq"),
        P("seq"),
        P("seq", "mp"),
        P(("mp", "seq")),
        P("mp", "seq"),
        P("seq"),
    )
    return jax.shard_map(local, mesh=mesh, in_specs=in_specs, out_specs=out_specs, check_vma=False)
```

```python
import functools
import math

import jax
import jax.numpy as jnp
from jax import lax
from jax.experimental import pallas as pl
from jax.experimental.pallas import tpu as pltpu
from jax.sharding import PartitionSpec as P

DH = 128
SPAN = 64
EPSILON = 1e-06
SELF_SCORE = -100000.0
MASKED = -1000000000.0
F32 = jnp.float32
BF16 = jnp.bfloat16
MESH = pl.DeviceIdType.MESH
VMEM = pl.BlockSpec(memory_space=pltpu.VMEM)
HBM = pl.BlockSpec(memory_space=pltpu.HBM)
ROW = (((1,), (1,)), ((), ()))
COL = (((0,), (0,)), ((), ()))


def dot(a, b):
    return jnp.dot(a, b, preferred_element_type=F32)


def dot_nt(a, b):
    return lax.dot_general(a, b, ROW, preferred_element_type=F32)


def dot_tn(a, b):
    return lax.dot_general(a, b, COL, preferred_element_type=F32)


def remote(src, dst, send_sem, recv_sem, axis, index):
    return pltpu.make_async_remote_copy(
        src_ref=src,
        dst_ref=dst,
        send_sem=send_sem,
        recv_sem=recv_sem,
        device_id={axis: index},
        device_id_type=MESH,
    )


def greet(n, m, g, me):
    barrier = pltpu.get_barrier_semaphore()

    @pl.loop(1, n)
    def _(i):
        pl.semaphore_signal(
            barrier, inc=1, device_id={"seq": lax.rem(g + i, n)}, device_id_type=MESH
        )

    @pl.loop(1, m)
    def _(i):
        pl.semaphore_signal(
            barrier, inc=1, device_id={"mp": lax.rem(me + i, m)}, device_id_type=MESH
        )

    pl.semaphore_wait(barrier, n + m - 2)


def iota(shape, dim):
    return lax.broadcasted_iota(jnp.int32, shape, dim)


def fiota(shape, dim):
    return iota(shape, dim).astype(F32)


def split3(x):
    hi = x.astype(BF16).astype(F32)
    rest = x - hi
    mid = rest.astype(BF16).astype(F32)
    return hi, mid, rest - mid


def columns3(x):
    hi, mid, low = split3(x)
    lane = iota((x.shape[0], 128), 1)
    return jnp.where(lane == 0, hi, jnp.where(lane == 1, mid, jnp.where(lane == 2, low, 0.0)))


def rows3(x):
    hi, mid, low = split3(x)
    part = iota((16, x.shape[1]), 0)
    return jnp.where(part == 0, hi, jnp.where(part == 1, mid, jnp.where(part == 2, low, 0.0)))


def column_to_row(x, onehot):
    packed = jnp.transpose(columns3(x))[0:16].astype(BF16)
    return jnp.sum(dot_nt(packed, onehot), axis=0, keepdims=True)


def row_to_column(x, onehot):
    return jnp.sum(dot_nt(onehot, rows3(x).astype(BF16)), axis=1, keepdims=True)


def onehot_rows(row, count):
    return jnp.where(fiota((count, row.shape[1]), 0) == row, 1.0, 0.0).astype(BF16)


def onehot_columns(column, count):
    return jnp.where(fiota((column.shape[0], count), 1) == column, 1.0, 0.0).astype(BF16)


def line_start(me, m, buf, send, recv, chunk):
    @pl.when(me < m - 1)
    def _():
        remote(buf.at[me, chunk], buf.at[me, chunk], send.at[0, me, chunk], recv.at[0, me, chunk], "mp", me + 1).start()

    @pl.when(me > 0)
    def _():
        remote(buf.at[me, chunk], buf.at[me, chunk], send.at[1, me, chunk], recv.at[1, me, chunk], "mp", me - 1).start()


def line_step(me, m, buf, send, recv, chunk, hop):
    @pl.when(me - hop >= 0)
    def _():
        src = me - hop
        part = buf.at[src, chunk]
        remote(part, part, send.at[0, src, chunk], recv.at[0, src, chunk], "mp", me - 1).wait_recv()

        @pl.when(me < m - 1)
        def _():
            remote(part, part, send.at[0, src, chunk], recv.at[0, src, chunk], "mp", me + 1).start()

    @pl.when(me + hop < m)
    def _():
        src = me + hop
        part = buf.at[src, chunk]
        remote(part, part, send.at[1, src, chunk], recv.at[1, src, chunk], "mp", me + 1).wait_recv()

        @pl.when(me > 0)
        def _():
            remote(part, part, send.at[1, src, chunk], recv.at[1, src, chunk], "mp", me - 1).start()


def line_drain(me, m, buf, send, recv, chunk):
    for hop in range(m):

        @pl.when((me - hop >= 0) & (me < m - 1))
        def _():
            part = buf.at[me - hop, chunk]
            remote(part, part, send.at[0, me - hop, chunk], recv.at[0, me - hop, chunk], "mp", me + 1).wait_send()

        @pl.when((me + hop < m) & (me > 0))
        def _():
            part = buf.at[me + hop, chunk]
            remote(part, part, send.at[1, me + hop, chunk], recv.at[1, me + hop, chunk], "mp", me - 1).wait_send()


def spread(n, g, src, dst, piece, send_sem, recv_sem):
    own = pl.multiple_of(g * piece, piece)
    dst[pl.ds(own, piece)] = src[pl.ds(own, piece)]

    @pl.loop(1, n)
    def _(i):
        d = lax.rem(g + i, n)
        there = pl.multiple_of(d * piece, piece)
        remote(src.at[pl.ds(there, piece)], dst.at[pl.ds(own, piece)], send_sem, recv_sem, "seq", d).start()


def all_of(buf, rows, send_sem, recv_sem, g):
    part = buf.at[pl.ds(0, rows)]
    return remote(part, part, send_sem, recv_sem, "seq", g)


def rank_rows(keys_row, keys_col):
    return jnp.sum(jnp.where(keys_col < keys_row, 1.0, 0.0), axis=0, keepdims=True)


def masked(raw, kpos, poscol, item, blocks):
    keys = jnp.concatenate(
        [jnp.broadcast_to(kpos[b, pl.ds(item, 1), :], (SPAN, 2 * SPAN)) for b in range(blocks)], axis=0
    )
    query = poscol[item]
    earlier = keys < query
    return jnp.where(earlier, raw, jnp.where(keys == query, SELF_SCORE, MASKED)), earlier


def share_start(g, n, buf, chunk, send, recv):
    odd = lax.rem(g, 2)
    block = buf.at[g, chunk]
    remote(block, block, send.at[0, chunk], recv.at[g, chunk], "seq", g + 1 - 2 * odd).start()

    @pl.loop(1, n // 2)
    def _(i):
        remote(block, block, send.at[i, chunk], recv.at[g, chunk], "seq", lax.rem(g + 2 * i, n)).start()


def share_forward(g, n, buf, chunk, send, recv):
    odd = lax.rem(g, 2)

    @pl.loop(1, n // 2)
    def _(i):
        src = lax.rem(g + 2 * i, n)
        block = buf.at[src, chunk]
        hop = remote(block, block, send.at[n // 2 + i, chunk], recv.at[src, chunk], "seq", g + 1 - 2 * odd)
        hop.wait_recv()
        hop.start()


def share_wait(g, n, buf, chunk, send, recv):
    sibling = g + 1 - 2 * lax.rem(g, 2)

    @pl.loop(0, n // 2)
    def _(i):
        src = lax.rem(sibling + 2 * i, n)
        block = buf.at[src, chunk]
        remote(block, block, send.at[0, chunk], recv.at[src, chunk], "seq", g).wait_recv()


def share_drain(g, n, buf, chunk, send, recv):
    block = buf.at[g, chunk]

    @pl.loop(0, n // 2)
    def _(i):
        remote(block, block, send.at[i, chunk], recv.at[g, chunk], "seq", g).wait_send()

    @pl.loop(1, n // 2)
    def _(i):
        remote(block, block, send.at[n // 2 + i, chunk], recv.at[g, chunk], "seq", g).wait_send()


def pick(n, piece, tokens, rounds, heads, h, tokcol, table, arrived):
    @pl.loop(0, n)
    def _(s):
        place = pl.ds(pl.multiple_of(s * piece, piece), piece)
        wanted = jnp.concatenate([tokcol[r * heads + h, place, :] for r in range(rounds)], axis=0)
        select = onehot_columns(wanted - (s * tokens).astype(F32), tokens)
        rows = dot(select, table(s)).astype(BF16)
        for r in range(rounds):
            arrived[r * heads + h, place, :] = rows[r * piece : (r + 1) * piece]


def fetch(pairs, sems):
    copies = [pltpu.make_async_copy(src, dst, sems.at[k]) for k, (src, dst) in enumerate(pairs)]
    for copy in copies:
        copy.start()
    return copies


def front_kernel(
    n, m, heads, piece,
    second_in, second_cot_in, order_in, gain_in, shift_in, wq_in, wv_in,
    rows_out, cot_out, ext, ro_out, wts_out, mixed_out, merged_out, rank_out, send_out, pos_out, kpos_out, slots_out, tok_out, zbuf,
    table, arrived, returning, back, unit, pos_ext, poscol, rankcol, sendcol, tokcol, lsecol, lse_send, lse_recv, lse_rows, second, second_cot, order, order_parts, gain, shift, wq, wv,
    zs, zr, cs, cr, xs, xr, prs, prr, bks, bkr, lss, lsr, fs,
):
    g = lax.axis_index("seq")
    me = lax.axis_index("mp")
    tokens, width = rows_out.shape
    part_width = second.shape[1]
    count = order.shape[0]
    rounds = count // heads
    blocks = tokens // SPAN
    chunks = zbuf.shape[1]
    chunk_rows = tokens // chunks
    loads = fetch(
        (
            (second_in, second), (order_in, order_parts), (gain_in, gain), (shift_in, shift),
            (wq_in, wq), (wv_in, wv), (second_cot_in, second_cot),
        ),
        fs,
    )
    greet(n, m, g, me)
    loads[0].wait()

    for chunk in range(chunks):
        zbuf[me, chunk] = second[chunk * chunk_rows : (chunk + 1) * chunk_rows].astype(BF16)
        line_start(me, m, zbuf, zs, zr, chunk)

    for load in loads[1:]:
        load.wait()
    for r in range(rounds):
        order[r * heads : (r + 1) * heads, :] = order_parts[r]
    start = pl.multiple_of(g * tokens, tokens)
    before = pl.multiple_of(lax.rem(g + n - 1, n) * tokens + tokens - 128, 128)
    own_pos = order[:, pl.ds(start, tokens)].astype(F32)
    pos_ext[:, 0:SPAN] = order[:, pl.ds(before, 128)][:, 128 - SPAN :].astype(F32)
    pos_ext[:, SPAN : SPAN + tokens] = own_pos
    for block in range(blocks):
        kpos_out[block] = pos_ext[:, block * SPAN : (block + 2) * SPAN]
    pos_out[...] = own_pos
    total = order.shape[1]
    place = jnp.right_shift(iota((1, total), 1), tokens.bit_length() - 1).astype(F32)
    high = jnp.right_shift(iota((32, tokens), 1), 4) == iota((32, tokens), 0)
    low = jnp.where(jnp.bitwise_and(iota((16, tokens), 1), 15) == iota((16, tokens), 0), 1.0, 0.0).astype(BF16)
    token = fiota((1, tokens), 1)
    for item in range(count):
        local = order[item : item + 1, :] - g * tokens
        a = jnp.where(jnp.right_shift(local, 4) == iota((32, total), 0), place, 0.0).astype(BF16)
        b = jnp.where(jnp.bitwise_and(local, 15) == iota((16, total), 0), 1.0, 0.0).astype(BF16)
        spot = dot_nt(a, b).astype(BF16)
        target = jnp.sum(jnp.where(high, dot(spot, low), 0.0), axis=0, keepdims=True)
        send_out[item : item + 1, :] = target * tokens + token
    keys_row = send_out[...]
    keys_col = jnp.transpose(keys_row)
    pos_col = jnp.transpose(own_pos)
    lane = iota((tokens, 128), 1)

    def tables(item):
        poscol[item] = pos_col[:, item : item + 1]
        send_out[item : item + 1, :] = rank_rows(keys_row[item : item + 1], keys_col[:, item : item + 1])
        rank = rank_rows(own_pos[item : item + 1], pos_col[:, item : item + 1])
        rank_out[item : item + 1, :] = rank
        tokcol[item] = row_to_column(own_pos[item : item + 1], onehot_rows(rank, tokens))

    def project(chunk):
        part = slice(chunk * chunk_rows, (chunk + 1) * chunk_rows)
        rows = jnp.concatenate([zbuf[s, chunk].astype(F32) for s in range(m)], axis=1)
        center = rows - jnp.mean(rows, axis=1, keepdims=True)
        var = jnp.mean(center * center, axis=1, keepdims=True)
        normed = (center * lax.rsqrt(var + EPSILON) * gain[...] + shift[...]).astype(BF16)
        rows_out[part, :] = normed
        q = dot(normed, wq[...]).astype(BF16)
        v = dot(normed, wv[...]).astype(BF16)
        for h in range(heads):
            table[g, h * chunks + chunk, :, 0:DH] = q[:, h * DH : (h + 1) * DH]
            table[g, h * chunks + chunk, :, DH : 2 * DH] = v[:, h * DH : (h + 1) * DH]
        share_start(g, n, table, chunk, xs, xr)

    todo = list(range(count))
    for wave in range(1, chunks + m - 1):
        for hop in range(m - 1, 0, -1):
            chunk = wave - hop
            if 0 <= chunk < chunks:
                line_step(me, m, zbuf, zs, zr, chunk, hop)
                if hop == m - 1:
                    project(chunk)
                    if chunk > 0:
                        share_forward(g, n, table, chunk - 1, xs, xr)
        for item in todo[:2]:
            tables(item)
        todo = todo[2:]
    for item in todo:
        tables(item)
    send_col = jnp.transpose(send_out[...])
    rank_col = jnp.transpose(rank_out[...])
    sorted_pos = jnp.zeros((tokens, 128), F32)
    for item in range(count):
        sendcol[item] = send_col[:, item : item + 1]
        rankcol[item] = rank_col[:, item : item + 1]
        sorted_pos = jnp.where(lane == item, tokcol[item], sorted_pos)
    tok_out[...] = jnp.transpose(sorted_pos)[0:count]

    for k, cot in enumerate((second_cot,)):
        cot_out[k, me] = cot[...].astype(BF16)

        @pl.loop(1, m)
        def _(i):
            peer = lax.rem(me + i, m)
            remote(cot_out.at[k, me], cot_out.at[k, me], cs.at[k, i], cr.at[k, me], "mp", peer).start()

    for block in range(chunks, heads * chunks):
        share_start(g, n, table, block, xs, xr)
    share_forward(g, n, table, chunks - 1, xs, xr)
    peers_rows = (n - 1) * piece
    after = lax.rem(g + 1, n)
    for h in range(heads):
        blocks_of = range(h * chunks, (h + 1) * chunks)
        for block in blocks_of:
            share_wait(g, n, table, block, xs, xr)
        pick(
            n, piece, tokens, rounds, heads, h, tokcol,
            lambda s: jnp.concatenate([table[s, block] for block in blocks_of], axis=0), arrived,
        )

        @pl.loop(0, rounds)
        def _(r):
            item = r * heads + h
            select = onehot_columns(rankcol[item], tokens)
            ext[item, SPAN:, :] = dot(select, arrived[item]).astype(BF16)
            remote(ext.at[item, pl.ds(tokens, SPAN)], ext.at[item, pl.ds(0, SPAN)], prs.at[item], prr.at[item], "seq", after).start()

        if h + 1 < heads:
            for block in range((h + 1) * chunks, (h + 2) * chunks):
                share_forward(g, n, table, block, xs, xr)

        @pl.loop(0, rounds)
        def _(r):
            item = r * heads + h
            remote(ext.at[item, pl.ds(tokens, SPAN)], ext.at[item, pl.ds(0, SPAN)], prs.at[item], prr.at[item], "seq", after).wait_recv()
            w = ext[item, :, 0:DH].astype(F32)
            unit[...] = (w * lax.rsqrt(jnp.sum(w * w, axis=1, keepdims=True) + EPSILON)).astype(BF16)
            spans = [slice(block * SPAN, (block + 2) * SPAN) for block in range(blocks)]
            raw = jnp.concatenate(
                [dot_nt(ext[item, span.start + SPAN : span.stop, 0:DH], unit[span]) for span in spans], axis=0
            ) * (1.0 / math.sqrt(DH))
            scores = masked(raw, kpos_out, poscol, item, blocks)[0]
            peak = jnp.max(scores, axis=1, keepdims=True)
            lse = peak + jnp.log(jnp.sum(jnp.exp(scores - peak), axis=1, keepdims=True))
            probs = jnp.exp(scores - lse).astype(BF16)
            outs = jnp.concatenate(
                [dot(probs[span.start : span.start + SPAN], ext[item, span, DH : 2 * DH]) for span in spans], axis=0
            ).astype(BF16)
            select = onehot_rows(rank_out[pl.ds(item, 1), :], tokens)
            returning[item] = dot(select, outs).astype(BF16)
            spread(n, g, returning.at[item], back.at[item], piece, bks.at[item], bkr.at[item])
            packed = jnp.transpose(columns3(lse))[0:16]
            slots_out[pl.ds(item, 1), :] = jnp.sum(packed, axis=0, keepdims=True)
            lse_row = jnp.sum(dot_nt(packed.astype(BF16), select), axis=0, keepdims=True)
            for d in range(n):
                lse_send[h, d, pl.ds(r, 1), 0:piece] = lse_row[:, d * piece : (d + 1) * piece]

        lse_recv[h, g] = lse_send[h, g]

        @pl.loop(1, n)
        def _(i):
            d = lax.rem(g + i, n)
            remote(lse_send.at[h, d], lse_recv.at[h, g], lss.at[h], lsr.at[h], "seq", d).start()

    for h in range(heads):
        all_of(lse_recv.at[h], n - 1, lss.at[h], lsr.at[h], g).wait_recv()
        lse_rows[h] = jnp.concatenate([lse_recv[h, d][:, 0:piece] for d in range(n)], axis=1)

        @pl.loop(0, rounds)
        def _(r):
            item = r * heads + h
            all_of(back.at[item], peers_rows, bks.at[item], bkr.at[item], g).wait_recv()
            select = onehot_columns(sendcol[item], tokens)
            ro_out[item] = dot(select, back[item]).astype(BF16)
            lsecol[item] = row_to_column(lse_rows[h, pl.ds(r, 1), :], select)

    weights = jnp.zeros((tokens, 128), F32)
    for h in range(heads):
        logs = [lsecol[r * heads + h] for r in range(rounds)]
        peak = functools.reduce(jnp.maximum, logs)
        full = peak + jnp.log(sum(jnp.exp(x - peak) for x in logs))
        merged = jnp.zeros((tokens, DH), F32)
        for r in range(rounds):
            w = jnp.exp(logs[r] - full)
            weights = jnp.where(lane == r * heads + h, w, weights)
            merged = merged + w * ro_out[r * heads + h].astype(F32)
        merged_out[:, h * DH : (h + 1) * DH] = merged
        mixed_out[:, h * DH : (h + 1) * DH] = merged.astype(BF16)
    wts_out[...] = weights

    for chunk in range(chunks):
        line_drain(me, m, zbuf, zs, zr, chunk)
    for block in range(heads * chunks):
        share_drain(g, n, table, block, xs, xr)
    for k in range(cot_out.shape[0]):

        @pl.loop(1, m)
        def _(i):
            src = lax.rem(me + i, m)
            remote(cot_out.at[k, src], cot_out.at[k, src], cs.at[k, i], cr.at[k, src], "mp", src).wait()

    @pl.loop(0, count)
    def _(item):
        all_of(returning.at[item], peers_rows, bks.at[item], bkr.at[item], g).wait_send()
        remote(ext.at[item, pl.ds(tokens, SPAN)], ext.at[item, pl.ds(0, SPAN)], prs.at[item], prr.at[item], "seq", after).wait_send()

    for h in range(heads):
        all_of(lse_send.at[h], n - 1, lss.at[h], lsr.at[h], g).wait_send()


def front(n, m, heads, second, second_cot, order, gain, shift, wq, wv):
    tokens, part_width = second.shape
    width = wq.shape[0]
    rounds = order.shape[0]
    count = rounds * heads
    piece = tokens // n
    blocks = tokens // SPAN
    chunks = 4
    dma = pltpu.SemaphoreType.DMA
    sds = jax.ShapeDtypeStruct
    outs = (
        sds((tokens, width), BF16),
        sds((1, m, tokens, part_width), BF16),
        sds((count, SPAN + tokens, 2 * DH), BF16),
        sds((count, tokens, DH), BF16),
        sds((tokens, 128), F32),
        sds((tokens, heads * DH), BF16),
        sds((tokens, heads * DH), F32),
        sds((count, tokens), F32),
        sds((count, tokens), F32),
        sds((count, tokens), F32),
        sds((blocks, count, 2 * SPAN), F32),
        sds((count, tokens), F32),
        sds((count, tokens), F32),
        sds((m, chunks, tokens // chunks, part_width), BF16),
    )
    scratch = [
        pltpu.VMEM((n, heads * chunks, tokens // chunks, 2 * DH), BF16),
        pltpu.VMEM((count, tokens, 2 * DH), BF16),
        pltpu.VMEM((count, tokens, DH), BF16),
        pltpu.VMEM((count, tokens, DH), BF16),
        pltpu.VMEM((SPAN + tokens, DH), BF16),
        pltpu.VMEM((count, tokens + 128), F32),
        pltpu.VMEM((count, tokens, 1), F32),
        pltpu.VMEM((count, tokens, 1), F32),
        pltpu.VMEM((count, tokens, 1), F32),
        pltpu.VMEM((count, tokens, 1), F32),
        pltpu.VMEM((count, tokens, 1), F32),
        pltpu.VMEM((heads, n, 8, max(128, piece)), F32),
        pltpu.VMEM((heads, n, 8, max(128, piece)), F32),
        pltpu.VMEM((heads, 8, tokens), F32),
        pltpu.VMEM((tokens, part_width), F32),
        pltpu.VMEM((tokens, part_width), F32),
        pltpu.VMEM((count, order.shape[2]), jnp.int32),
        pltpu.VMEM(order.shape, jnp.int32),
        pltpu.VMEM((1, width), F32),
        pltpu.VMEM((1, width), F32),
        pltpu.VMEM(wq.shape, BF16),
        pltpu.VMEM(wv.shape, BF16),
        dma((2, m, chunks)),
        dma((2, m, chunks)),
        dma((2, m)),
        dma((2, m)),
        dma((n, heads * chunks)),
        dma((n, heads * chunks)),
        dma((count,)),
        dma((count,)),
        dma((count,)),
        dma((count,)),
        dma((heads,)),
        dma((heads,)),
        dma((7,)),
    ]
    return pl.pallas_call(
        functools.partial(front_kernel, n, m, heads, piece),
        out_shape=outs,
        in_specs=[HBM] * 7,
        out_specs=[VMEM] * len(outs),
        scratch_shapes=scratch,
        compiler_params=pltpu.CompilerParams(
            collective_id=0, has_side_effects=True, vmem_limit_bytes=38 << 20
        ),
        name="front",
    )(*(pltpu.with_memory_space_constraint(x, pltpu.HBM) for x in (second, second_cot, order, gain, shift, wq, wv)))


def reduce_start(me, m, own, got, send, recv, chunk):
    @pl.when(me == 0)
    def _():
        for s in range(m - 1, 0, -1):
            remote(own.at[s, chunk], got.at[0, s, chunk], send.at[0, s, chunk], recv.at[0, s, chunk], "mp", me + 1).start()

    @pl.when(me == m - 1)
    def _():
        for s in range(m - 1):
            remote(own.at[s, chunk], got.at[1, s, chunk], send.at[1, s, chunk], recv.at[1, s, chunk], "mp", me - 1).start()


def reduce_forward(me, m, own, got, passing, send, recv, tick, chunks):
    for direction, chunk, peer in ((0, tick - me, me + 1), (1, tick - (m - 1 - me), me - 1)):

        @pl.when((me > 0) & (me < m - 1) & (chunk >= 0) & (chunk < chunks))
        def _():
            for i in range(m - 1):
                s = m - 1 - i if direction == 0 else i

                @pl.when(s > me if direction == 0 else s < me)
                def _():
                    place = (direction, s, chunk)
                    hop = remote(passing.at[place], got.at[place], send.at[place], recv.at[place], "mp", peer)
                    hop.wait_recv()
                    passing[place] = (own[s, chunk].astype(F32) + got[place].astype(F32)).astype(BF16)
                    hop.start()


def reduce_final(me, m, own, got, total, send, recv, chunk):
    total[...] = own[me, chunk].astype(F32)
    for direction, expected in ((0, me > 0), (1, me < m - 1)):

        @pl.when(expected)
        def _():
            place = (direction, me, chunk)
            remote(own.at[me, chunk], got.at[place], send.at[place], recv.at[place], "mp", me).wait_recv()
            total[...] += got[place].astype(F32)


def reduce_drain(me, m, own, got, send, recv, chunk):
    for s in range(m):
        for direction, sent in ((0, me < s), (1, me > s)):
            place = (direction, s, chunk)

            @pl.when(sent)
            def _():
                remote(own.at[s, chunk], got.at[place], send.at[place], recv.at[place], "mp", me).wait_send()


def pack_stats(a, b):
    lane = iota((a.shape[0], 128), 1)
    return jnp.transpose(jnp.where(lane == 0, a, jnp.where(lane == 1, b, 0.0)))[0:8]


def stats_start(me, m, stats, send, recv, chunk):
    @pl.loop(1, m)
    def _(i):
        remote(stats.at[me, chunk], stats.at[me, chunk], send.at[i, chunk], recv.at[me, chunk], "mp", lax.rem(me + i, m)).start()


def stats_wait(me, m, stats, send, recv, chunk):
    @pl.loop(1, m)
    def _(i):
        src = lax.rem(me + i, m)
        remote(stats.at[src, chunk], stats.at[src, chunk], send.at[i, chunk], recv.at[src, chunk], "mp", src).wait()

    return jnp.transpose(sum(stats[s, chunk] for s in range(m)))


def pair_send(g, q, own, got, send, recv):
    odd = lax.rem(g, 2)
    return remote(own.at[2 * q + 1 - odd], got.at[q], send.at[q], recv.at[q], "seq", g + 1 - 2 * odd)


def pair_pass(g, q, own, got, passing, part, fin, send1, recv1, send2, recv2):
    odd = lax.rem(g, 2)
    home = g // 2
    pair_send(g, q, own, got, send1, recv1).wait_recv()
    passing[q] = (own[2 * q + odd].astype(F32) + got[q].astype(F32)).astype(BF16)

    @pl.when(q != home)
    def _():
        remote(passing.at[(q,) + part], fin.at[home], send2.at[q], recv2.at[home], "seq", 2 * q + odd).start()


def pair_total(g, pairs, passing, part, fin, send2, recv2):
    home = g // 2

    @pl.loop(1, pairs)
    def _(i):
        q = lax.rem(home + i, pairs)
        remote(fin.at[q], fin.at[q], send2.at[q], recv2.at[q], "seq", g).wait_recv()

    fin[home] = passing[(home,) + part]


def pair_drain(g, pairs, own, got, passing, part, fin, send1, recv1, send2, recv2):
    home = g // 2

    @pl.loop(0, pairs)
    def _(q):
        pair_send(g, q, own, got, send1, recv1).wait_send()

        @pl.when(q != home)
        def _():
            remote(passing.at[(q,) + part], fin.at[home], send2.at[q], recv2.at[home], "seq", g).wait_send()


def middle_kernel(
    n, m, heads, chunks,
    mixed, mixing_in, first_in, first_cot_in, cot_full, gain, shift, expand_in, expand_bias, contract_in,
    out_first, grad_first, gm_out, fo_out, pe_out, pc_out, pm_out, vec_out,
    part_a, got_a, pass_a, full_a, part_b, got_b, pass_b, full_b, total, stats,
    gact, feed, active, gpre, grad_feed, grad_att, mean_scr, rstd_scr, w_own, w_got, w_pass, w_fin, mixing, first, first_cot, expand, contract,
    ras, rar, gas, gar, rbs, rbr, gbs, gbr, sts, str_, w1s, w1r, w2s, w2r, fs,
):
    g = lax.axis_index("seq")
    me = lax.axis_index("mp")
    tokens, part_width = first.shape
    width = mixing.shape[1]
    hidden = expand.shape[1]
    rows = tokens // chunks
    loads = fetch(
        (
            (mixing_in, mixing), (contract_in, contract), (first_in, first),
            (expand_in, expand), (first_cot_in, first_cot),
        ),
        fs,
    )
    hops = m - 1
    pairs = n // 2
    slice_rows = width // n
    tile = max(256, 2 * slice_rows)
    tiles = width // tile
    tile_pairs = tile // slice_rows // 2
    greet(n, m, g, me)
    loads[0].wait()

    def scatter(part, value, chunk):
        for s in range(m):
            part[s, chunk] = value[:, s * part_width : (s + 1) * part_width].astype(BF16)

    def gather(full, chunk):
        return jnp.concatenate([full[s, chunk] for s in range(m)], axis=1)

    def rows_of(chunk):
        return pl.ds(pl.multiple_of(chunk * rows, rows), rows)

    def during(tick, delay, body, length=chunks):
        @pl.when((tick >= delay) & (tick < delay + length))
        def _():
            body(tick - delay)

    for chunk in range(chunks):
        scatter(part_a, dot(mixed[chunk * rows : (chunk + 1) * rows, :], mixing[...]), chunk)
        reduce_start(me, m, part_a, got_a, ras, rar, chunk)
    for load in loads[1:]:
        load.wait()
    own_cols = pl.multiple_of(me * part_width, part_width)
    gain_own = gain[:, pl.ds(own_cols, part_width)]
    vec_out[...] = jnp.zeros_like(vec_out)

    def finish_first(chunk):
        part = rows_of(chunk)
        reduce_final(me, m, part_a, got_a, total, ras, rar, chunk)
        stream = first[part, :] + total[...]
        out_first[part, :] = stream
        full_a[me, chunk] = stream.astype(BF16)
        line_start(me, m, full_a, gas, gar, chunk)

    def back_of_feed(chunk):
        part = rows_of(chunk)
        cot = jnp.concatenate([cot_full[0, s, part, :] for s in range(m)], axis=1)
        grad_feed[part, :] = cot
        gact[part, :] = dot_nt(cot, contract[...])

    def feed_forward(chunk):
        part = rows_of(chunk)
        x = gather(full_a, chunk).astype(F32)
        mean = jnp.mean(x, axis=1, keepdims=True)
        center = x - mean
        rstd = lax.rsqrt(jnp.mean(center * center, axis=1, keepdims=True) + EPSILON)
        mean_scr[part, :] = mean
        rstd_scr[part, :] = rstd
        xhat = center * rstd
        normed = (xhat * gain[...] + shift[...]).astype(BF16)
        feed[part, :] = normed
        pre = dot(normed, expand[...]) + expand_bias[...]
        gate = 0.5 * (1.0 + lax.erf(pre * (1.0 / math.sqrt(2.0))))
        active[part, :] = (pre * gate).astype(BF16)
        slope = gate + pre * jnp.exp(-0.5 * pre * pre) * (1.0 / math.sqrt(2.0 * math.pi))
        back = (gact[part, :] * slope).astype(BF16)
        gpre[part, :] = back
        term = dot_nt(back, expand[...])
        scatter(part_b, term, chunk)
        reduce_start(me, m, part_b, got_b, rbs, rbr, chunk)
        e = term * gain[...]
        stats[me, chunk] = pack_stats(
            jnp.sum(e, axis=1, keepdims=True), jnp.sum(e * xhat, axis=1, keepdims=True)
        )
        stats_start(me, m, stats, sts, str_, chunk)
        vec_out[0:1, :] += jnp.sum(term * xhat, axis=0, keepdims=True)
        vec_out[1:2, :] += jnp.sum(term, axis=0, keepdims=True)
        vec_out[2:3, :] += jnp.sum(grad_feed[part, :].astype(F32), axis=0, keepdims=True)
        vec_out[3:4, :] += jnp.sum(back.astype(F32), axis=0, keepdims=True)

    def finish_grad(chunk):
        part = rows_of(chunk)
        reduce_final(me, m, part_b, got_b, total, rbs, rbr, chunk)
        sums = stats_wait(me, m, stats, sts, str_, chunk) * (1.0 / width)
        rstd = rstd_scr[part, :]
        xhat = (full_a[me, chunk].astype(F32) - mean_scr[part, :]) * rstd
        stream = first_cot[part, :] + rstd * (
            total[...] * gain_own - sums[:, 0:1] - xhat * sums[:, 1:2]
        )
        grad_first[part, :] = stream
        full_b[me, chunk] = stream.astype(BF16)
        line_start(me, m, full_b, gbs, gbr, chunk)

    def merged_grad(chunk):
        part = rows_of(chunk)
        att = gather(full_b, chunk)
        grad_att[part, :] = att
        gm_out[part, :] = dot_nt(att, mixing[...])

    def weight_tile(k):
        cols = pl.ds(pl.multiple_of(k * tile, tile), tile)
        for lanes, left, right in (
            (slice(0, hidden), feed, gpre),
            (slice(hidden, 2 * hidden), grad_feed, active),
        ):
            product = dot_tn(left[:, cols], right[...]).astype(BF16)
            for i in range(2 * tile_pairs):
                w_own[k * 2 * tile_pairs + i, :, lanes] = product[i * slice_rows : (i + 1) * slice_rows]
        for i in range(tile_pairs):
            pair_send(g, k * tile_pairs + i, w_own, w_got, w1s, w1r).start()

    second_part = (slice(None), pl.ds(hidden, hidden))

    def weight_pass(k):
        for i in range(tile_pairs):
            pair_pass(g, k * tile_pairs + i, w_own, w_got, w_pass, second_part, w_fin, w1s, w1r, w2s, w2r)

    def feed_out(k):
        s = k
        fo_out[s] = dot(active[...], contract[:, pl.ds(pl.multiple_of(s * part_width, part_width), part_width)]).astype(BF16)

    @pl.loop(0, chunks + 4 * hops)
    def _(tick):
        reduce_forward(me, m, part_a, got_a, pass_a, ras, rar, tick, chunks)
        reduce_forward(me, m, part_b, got_b, pass_b, rbs, rbr, tick - 2 * hops, chunks)
        for hop in range(hops, 0, -1):
            during(tick, hops + hop, lambda chunk: line_step(me, m, full_a, gas, gar, chunk, hop))
            during(tick, 3 * hops + hop, lambda chunk: line_step(me, m, full_b, gbs, gbr, chunk, hop))
        during(tick, hops, finish_first)
        during(tick, 3 * hops, finish_grad)
        during(tick, 4 * hops, merged_grad)
        during(tick, 0, back_of_feed)
        during(tick, 2 * hops, feed_forward)
        during(tick, chunks + 2 * hops + 1, weight_pass, tiles)
        during(tick, chunks + 2 * hops, weight_tile, tiles)

    @pl.loop(0, m)
    def _(s):
        feed_out(s)

    for k in range(2 * hops, tiles):
        weight_tile(k)
    for k in range(tiles):
        if k + 1 >= 2 * hops:
            weight_pass(k)

    @pl.loop(0, width // 256)
    def _(k):
        cols = pl.ds(pl.multiple_of(k * 256, 256), 256)
        pm_out[cols, :] = dot_tn(grad_att[:, cols], mixed[...]).astype(BF16)

    pe_out[...] = w_pass[:, :, 0:hidden]
    pair_total(g, pairs, w_pass, second_part, w_fin, w2s, w2r)
    pc_out[...] = jnp.transpose(sum(w_fin[q].astype(F32) for q in range(pairs)))

    for chunk in range(chunks):
        reduce_drain(me, m, part_a, got_a, ras, rar, chunk)
        reduce_drain(me, m, part_b, got_b, rbs, rbr, chunk)
        line_drain(me, m, full_a, gas, gar, chunk)
        line_drain(me, m, full_b, gbs, gbr, chunk)
    pair_drain(g, pairs, w_own, w_got, w_pass, second_part, w_fin, w1s, w1r, w2s, w2r)


def middle(n, m, heads, mixed, mixing, first, first_cot, cot_full, gain, shift, expand, expand_bias, contract):
    tokens, part_width = first.shape
    width = mixing.shape[1]
    hidden = expand.shape[1]
    chunks = 4
    rows = tokens // chunks
    slice_rows = width // n
    dma = pltpu.SemaphoreType.DMA
    sds = jax.ShapeDtypeStruct
    outs = (
        sds((tokens, part_width), F32),
        sds((tokens, part_width), F32),
        sds((tokens, heads * DH), F32),
        sds((m, tokens, part_width), BF16),
        sds((n // 2, slice_rows, hidden), BF16),
        sds((hidden, slice_rows), F32),
        sds((width, heads * DH), BF16),
        sds((8, width), F32),
    )
    shards = pltpu.VMEM((m, chunks, rows, part_width), BF16)
    both = pltpu.VMEM((2, m, chunks, rows, part_width), BF16)
    pieces = pltpu.VMEM((n // 2, slice_rows, 2 * hidden), BF16)
    scratch = [
        shards, both, both, shards, shards, both, both, shards,
        pltpu.VMEM((rows, part_width), F32),
        pltpu.VMEM((m, chunks, 8, rows), F32),
        pltpu.VMEM((tokens, hidden), F32),
        pltpu.VMEM((tokens, width), BF16),
        pltpu.VMEM((tokens, hidden), BF16),
        pltpu.VMEM((tokens, hidden), BF16),
        pltpu.VMEM((tokens, width), BF16),
        pltpu.VMEM((tokens, width), BF16),
        pltpu.VMEM((tokens, 1), F32),
        pltpu.VMEM((tokens, 1), F32),
        pltpu.VMEM((n, slice_rows, 2 * hidden), BF16),
        pieces, pieces,
        pltpu.VMEM((n // 2, slice_rows, hidden), BF16),
        pltpu.VMEM(mixing.shape, BF16),
        pltpu.VMEM(first.shape, F32),
        pltpu.VMEM(first.shape, F32),
        pltpu.VMEM(expand.shape, BF16),
        pltpu.VMEM(contract.shape, BF16),
    ] + [dma((2, m, chunks))] * 8 + [dma((m, chunks))] * 2 + [dma((n // 2,))] * 4 + [dma((5,))]
    return pl.pallas_call(
        functools.partial(middle_kernel, n, m, heads, chunks),
        out_shape=outs,
        in_specs=[VMEM, HBM, HBM, HBM, VMEM, VMEM, VMEM, HBM, VMEM, HBM],
        out_specs=[VMEM] * len(outs),
        scratch_shapes=scratch,
        compiler_params=pltpu.CompilerParams(
            collective_id=1, has_side_effects=True, vmem_limit_bytes=46 << 20
        ),
        name="middle",
    )(mixed, mixing, first, first_cot, cot_full, gain, shift, expand, expand_bias, contract)


def back_kernel(
    n, m, heads, piece, chunks,
    gm, merged, wts, ro, ext, rank, sendp, pos, kpos, slots, pe, normed, gathered, wq, wv, second, second_cot, fo, pm, vec_feed, gain, bias,
    out_second, grad_second, pe_out, pq_out, pv_out, pm_out, vec_out,
    outgoing, arrived, returning, back, unit, poscol, rankcol, sendcol, lsecol, gl_send, gl_recv, gl_rows, gradk, gradq, grads, wsel,
    prior, incoming, gpair, fo_recv, part_c, got_c, pass_c, total, stats, mean_scr, rstd_scr, w_own, w_got, w_pass, w_fin, e_fin, vec, vec_send, vec_recv, vec_all,
    ins, inr, prs, prr, bks, bkr, gls, glr, es, er, fos, fore, rcs, rcr, sts, str_, w1s, w1r, w2s, w2r, vs, vr, vzs, vzr,
):
    g = lax.axis_index("seq")
    me = lax.axis_index("mp")
    tokens, width = normed.shape
    part_width = second.shape[1]
    count = ro.shape[0]
    rounds = count // heads
    blocks = tokens // SPAN
    rows = tokens // chunks
    scaling = 1.0 / math.sqrt(DH)
    greet(n, m, g, me)

    @pl.loop(1, m)
    def _(i):
        peer = lax.rem(me + i, m)
        remote(fo.at[peer], fo_recv.at[me], fos.at[i], fore.at[me], "mp", peer).start()

    pos_col = jnp.transpose(pos[...])
    send_col = jnp.transpose(sendp[...])
    rank_col = jnp.transpose(rank[...])
    lse_col = jnp.transpose(slots[...])
    for item in range(count):
        poscol[item] = pos_col[:, item : item + 1]
        lsecol[item] = lse_col[:, item : item + 1]
        sendcol[item] = send_col[:, item : item + 1]
        rankcol[item] = rank_col[:, item : item + 1]

    lane = iota((tokens, 128), 1)

    for h in range(heads):
        cols = slice(h * DH, (h + 1) * DH)
        gmh = gm[:, cols]
        inner = jnp.sum(gmh * merged[:, cols], axis=1, keepdims=True)
        for r in range(rounds):
            item = r * heads + h
            w = jnp.sum(jnp.where(lane == item, wts[...], 0.0), axis=1, keepdims=True)
            select = onehot_rows(sendp[item : item + 1, :], tokens)
            outgoing[item] = dot(select, (w * gmh).astype(BF16)).astype(BF16)
            spread(n, g, outgoing.at[item], arrived.at[item], piece, ins.at[item], inr.at[item])
            gs = w * (jnp.sum(gmh * ro[item].astype(F32), axis=1, keepdims=True) - inner)
            row = column_to_row(gs, select)
            for d in range(n):
                gl_send[d, item : item + 1, 0:piece] = row[:, d * piece : (d + 1) * piece]

    gl_recv[g] = gl_send[g]

    @pl.loop(1, n)
    def _(i):
        d = lax.rem(g + i, n)
        remote(gl_send.at[d], gl_recv.at[g], gls, glr, "seq", d).start()

    all_of(gl_recv, n - 1, gls, glr, g).wait_recv()
    gl_rows[...] = jnp.concatenate([gl_recv[d][:, 0:piece] for d in range(n)], axis=1)
    peers_rows = (n - 1) * piece
    before = lax.rem(g + n - 1, n)

    @pl.loop(0, count + 2)
    def _(step):
        @pl.when(step < count)
        def _():
            item = step
            slot = lax.rem(item, 3)
            all_of(arrived.at[item], peers_rows, ins.at[item], inr.at[item], g).wait_recv()
            select = onehot_columns(rankcol[item], tokens)
            grads[...] = dot(select, arrived[item]).astype(BF16)
            wsel[...] = row_to_column(gl_rows[pl.ds(item, 1), :], select)
            w = ext[item, :, 0:DH].astype(F32)
            unit[...] = (w * lax.rsqrt(jnp.sum(w * w, axis=1, keepdims=True) + EPSILON)).astype(BF16)
            spans = [slice(block * SPAN, (block + 2) * SPAN) for block in range(blocks)]
            queries = [ext[item, span.start + SPAN : span.stop, 0:DH] for span in spans]
            raw = jnp.concatenate([dot_nt(q, unit[span]) for q, span in zip(queries, spans)], axis=0) * scaling
            gp = jnp.concatenate(
                [dot_nt(grads[span.start : span.start + SPAN], ext[item, span, DH : 2 * DH]) for span in spans], axis=0
            )
            scores, earlier = masked(raw, kpos, poscol, item, blocks)
            probs = jnp.exp(scores - lsecol[item])
            inner = jnp.sum(probs * gp, axis=1, keepdims=True)
            gs = (jnp.where(earlier, probs * (gp - inner + wsel[...]), 0.0) * scaling).astype(BF16)
            low = probs.astype(BF16)
            gradq[slot] = jnp.concatenate(
                [dot(gs[span.start : span.start + SPAN], unit[span]) for span in spans], axis=0
            )
            gk = [dot_tn(gs[span.start : span.start + SPAN], q) for q, span in zip(queries, spans)]
            gv = [
                dot_tn(low[span.start : span.start + SPAN], grads[span.start : span.start + SPAN])
                for span in spans
            ]
            for lanes, slots in ((slice(0, DH), gk), (slice(DH, 2 * DH), gv)):
                prior[item, :, lanes] = slots[0][0:SPAN].astype(BF16)
                for block in range(blocks):
                    lo = block * SPAN
                    own = slots[block][SPAN : 2 * SPAN]
                    if block + 1 < blocks:
                        own = own + slots[block + 1][0:SPAN]
                    gradk[slot, lo : lo + SPAN, lanes] = own
            remote(prior.at[item], incoming.at[item], prs.at[item], prr.at[item], "seq", before).start()

        @pl.when(step > 1)
        def _():
            item = step - 2
            slot = lax.rem(item, 3)
            remote(prior.at[item], incoming.at[item], prs.at[item], prr.at[item], "seq", before).wait_recv()
            gradk[slot, tokens - SPAN :, :] += incoming[item].astype(F32)
            w = ext[item, SPAN:, 0:DH].astype(F32)
            inv = lax.rsqrt(jnp.sum(w * w, axis=1, keepdims=True) + EPSILON)
            gk = gradk[slot, :, 0:DH]
            along = jnp.sum(w * gk, axis=1, keepdims=True)
            gq = gradq[slot] + inv * gk - (inv * inv * inv * along) * w
            done = jnp.concatenate([gq.astype(BF16), gradk[slot, :, DH : 2 * DH].astype(BF16)], axis=1)
            select = onehot_rows(rank[pl.ds(item, 1), :], tokens)
            returning[item] = dot(select, done).astype(BF16)
            spread(n, g, returning.at[item], back.at[item], piece, bks.at[item], bkr.at[item])

    home = g // 2
    pairs = n // 2

    @pl.loop(1, pairs)
    def _(i):
        q = lax.rem(home + i, pairs)
        remote(pe.at[q], e_fin.at[home], es.at[q], er.at[home], "seq", 2 * q + lax.rem(g, 2)).start()

    for chunk in range(gathered.shape[1]):
        high = gathered.shape[2]
        x = jnp.concatenate([gathered[s, chunk].astype(F32) for s in range(m)], axis=1)
        mean = jnp.mean(x, axis=1, keepdims=True)
        center = x - mean
        mean_scr[chunk * high : (chunk + 1) * high] = mean
        rstd_scr[chunk * high : (chunk + 1) * high] = lax.rsqrt(
            jnp.mean(center * center, axis=1, keepdims=True) + EPSILON
        )

    gpair[...] = jnp.zeros_like(gpair)

    @pl.loop(0, count)
    def _(item):
        all_of(back.at[item], peers_rows, bks.at[item], bkr.at[item], g).wait_recv()
        select = onehot_columns(sendcol[item], tokens)
        gpair[lax.rem(item, heads)] += dot(select, back[item])

    gq = jnp.concatenate([gpair[h][:, 0:DH] for h in range(heads)], axis=1).astype(BF16)
    gv = jnp.concatenate([gpair[h][:, DH : 2 * DH] for h in range(heads)], axis=1).astype(BF16)
    vec[0:2, :] = jnp.zeros((2, width), F32)
    vec[2:6, :] = vec_feed[0:4, :]
    vec[6:8, :] = jnp.zeros((2, width), F32)
    sub = gathered.shape[2] // rows
    for chunk in range(chunks):
        part = slice(chunk * rows, (chunk + 1) * rows)
        inside = slice((chunk % sub) * rows, (chunk % sub + 1) * rows)
        term = dot_nt(gq[part], wq[...]) + dot_nt(gv[part], wv[...])
        for s in range(m):
            part_c[s, chunk] = term[:, s * part_width : (s + 1) * part_width].astype(BF16)
        reduce_start(me, m, part_c, got_c, rcs, rcr, chunk)
        x = jnp.concatenate([gathered[s, chunk // sub, inside, :].astype(F32) for s in range(m)], axis=1)
        xhat = (x - mean_scr[part]) * rstd_scr[part]
        e = term * gain[...]
        stats[me, chunk] = pack_stats(
            jnp.sum(e, axis=1, keepdims=True), jnp.sum(e * xhat, axis=1, keepdims=True)
        )
        stats_start(me, m, stats, sts, str_, chunk)
        vec[0:1, :] += jnp.sum(term * xhat, axis=0, keepdims=True)
        vec[1:2, :] += jnp.sum(term, axis=0, keepdims=True)

    slice_rows = width // n
    for d in range(n):
        vec_send[d, :, 0:slice_rows] = vec[:, d * slice_rows : (d + 1) * slice_rows]
    vec_recv[g] = vec_send[g]

    @pl.loop(1, n)
    def _(i):
        d = lax.rem(g + i, n)
        remote(vec_send.at[d], vec_recv.at[g], vs, vr, "seq", d).start()

    tile = max(256, 2 * slice_rows)
    tile_pairs = tile // slice_rows // 2
    own_heads = heads * DH

    @pl.loop(0, width // tile)
    def _(k):
        cols = pl.ds(pl.multiple_of(k * tile, tile), tile)
        products = (
            dot_tn(normed[:, cols], gq).astype(BF16),
            dot_tn(normed[:, cols], gv).astype(BF16),
            pm[cols, :],
        )
        for j, product in enumerate(products):
            for i in range(2 * tile_pairs):
                w_own[k * 2 * tile_pairs + i, :, j * own_heads : (j + 1) * own_heads] = product[
                    i * slice_rows : (i + 1) * slice_rows
                ]
        for i in range(tile_pairs):
            pair_send(g, k * tile_pairs + i, w_own, w_got, w1s, w1r).start()

    own_cols = pl.multiple_of(me * part_width, part_width)
    gain_own = gain[:, pl.ds(own_cols, part_width)]
    hops = m - 1

    def finish(chunk):
        part = pl.ds(pl.multiple_of(chunk * rows, rows), rows)
        inside = pl.ds(pl.multiple_of(lax.rem(chunk, sub) * rows, rows), rows)
        reduce_final(me, m, part_c, got_c, total, rcs, rcr, chunk)
        sums = stats_wait(me, m, stats, sts, str_, chunk) * (1.0 / width)
        rstd = rstd_scr[part, :]
        xhat = (gathered[me, chunk // sub, inside, :].astype(F32) - mean_scr[part, :]) * rstd
        grad_second[part, :] = second_cot[part, :] + rstd * (
            total[...] * gain_own - sums[:, 0:1] - xhat * sums[:, 1:2]
        )

    @pl.loop(0, pairs)
    def _(q):
        pair_pass(g, q, w_own, w_got, w_pass, (), w_fin, w1s, w1r, w2s, w2r)

    all_of(vec_recv, n - 1, vs, vr, g).wait_recv()
    vec_all[me] = sum(vec_recv[d] for d in range(n))

    @pl.loop(1, m)
    def _(i):
        peer = lax.rem(me + i, m)
        remote(vec_all.at[me], vec_all.at[me], vzs.at[i], vzr.at[me], "mp", peer).start()

    @pl.loop(0, chunks + hops)
    def _(tick):
        reduce_forward(me, m, part_c, got_c, pass_c, rcs, rcr, tick, chunks)

        @pl.when(tick >= hops)
        def _():
            finish(tick - hops)

    fo_recv[me] = fo[me]

    @pl.loop(1, m)
    def _(i):
        src = lax.rem(me + i, m)
        remote(fo.at[src], fo_recv.at[src], fos.at[i], fore.at[src], "mp", src).wait()

    out_second[...] = (
        second[...]
        + sum(fo_recv[s].astype(F32) for s in range(m))
        + bias[:, pl.ds(own_cols, part_width)]
    )
    @pl.loop(1, m)
    def _(i):
        src = lax.rem(me + i, m)
        remote(vec_all.at[src], vec_all.at[src], vzs.at[i], vzr.at[src], "mp", src).wait()

    row = iota((8, vec_all.shape[2]), 0)
    vec_out[...] = jnp.where(row < 4, sum(vec_all[s] for s in range(m)), vec_all[me])
    pair_total(g, pairs, pe, (), e_fin, es, er)
    pe_out[...] = sum(e_fin[q].astype(F32) for q in range(pairs))
    pair_total(g, pairs, w_pass, (), w_fin, w2s, w2r)
    for j, out in enumerate((pq_out, pv_out)):
        out[...] = sum(w_fin[q, :, j * own_heads : (j + 1) * own_heads].astype(F32) for q in range(pairs))
    pm_out[...] = jnp.transpose(
        sum(w_fin[q, :, 2 * own_heads : 3 * own_heads].astype(F32) for q in range(pairs))
    )
    for chunk in range(chunks):
        reduce_drain(me, m, part_c, got_c, rcs, rcr, chunk)
    pair_drain(g, pairs, w_own, w_got, w_pass, (), w_fin, w1s, w1r, w2s, w2r)
    all_of(vec_send, n - 1, vs, vr, g).wait_send()

    @pl.loop(0, count)
    def _(item):
        all_of(outgoing.at[item], peers_rows, ins.at[item], inr.at[item], g).wait_send()
        all_of(returning.at[item], peers_rows, bks.at[item], bkr.at[item], g).wait_send()
        remote(prior.at[item], incoming.at[item], prs.at[item], prr.at[item], "seq", before).wait_send()

    all_of(gl_send, n - 1, gls, glr, g).wait_send()

    @pl.loop(1, pairs)
    def _(i):
        q = lax.rem(home + i, pairs)
        remote(pe.at[q], e_fin.at[home], es.at[q], er.at[home], "seq", g).wait_send()


def behind(n, m, heads, gm, merged, wts, ro, ext, rank, sendp, pos, kpos, slots, pe, normed, gathered, wq, wv, second, second_cot, fo, pm, vec_feed, gain, bias):
    tokens, part_width = second.shape
    width = normed.shape[1]
    count = ro.shape[0]
    piece = tokens // n
    chunks = 4
    rows = tokens // chunks
    slice_rows = width // n
    dma = pltpu.SemaphoreType.DMA
    sds = jax.ShapeDtypeStruct
    outs = (
        sds((tokens, part_width), F32),
        sds((tokens, part_width), F32),
        sds((slice_rows, pe.shape[2]), F32),
        sds((slice_rows, heads * DH), F32),
        sds((slice_rows, heads * DH), F32),
        sds((heads * DH, slice_rows), F32),
        sds((8, max(128, slice_rows)), F32),
    )
    both = pltpu.VMEM((2, m, chunks, rows, part_width), BF16)
    column = pltpu.VMEM((count, tokens, 1), F32)
    pieces = pltpu.VMEM((n // 2, slice_rows, 3 * heads * DH), BF16)
    scratch = [
        pltpu.VMEM((count, tokens, DH), BF16),
        pltpu.VMEM((count, tokens, DH), BF16),
        pltpu.VMEM((count, tokens, 2 * DH), BF16),
        pltpu.VMEM((count, tokens, 2 * DH), BF16),
        pltpu.VMEM((SPAN + tokens, DH), BF16),
        column, column, column, column,
        pltpu.VMEM((n, count, max(128, piece)), F32),
        pltpu.VMEM((n, count, max(128, piece)), F32),
        pltpu.VMEM((count, tokens), F32),
        pltpu.VMEM((3, tokens, 2 * DH), F32),
        pltpu.VMEM((3, tokens, DH), F32),
        pltpu.VMEM((tokens, DH), BF16),
        pltpu.VMEM((tokens, 1), F32),
        pltpu.VMEM((count, SPAN, 2 * DH), BF16),
        pltpu.VMEM((count, SPAN, 2 * DH), BF16),
        pltpu.VMEM((heads, tokens, 2 * DH), F32),
        pltpu.VMEM((m, tokens, part_width), BF16),
        pltpu.VMEM((m, chunks, rows, part_width), BF16),
        both, both,
        pltpu.VMEM((rows, part_width), F32),
        pltpu.VMEM((m, chunks, 8, rows), F32),
        pltpu.VMEM((tokens, 1), F32),
        pltpu.VMEM((tokens, 1), F32),
        pltpu.VMEM((n, slice_rows, 3 * heads * DH), BF16),
        pieces, pieces, pieces,
        pltpu.VMEM(pe.shape, BF16),
        pltpu.VMEM((8, width), F32),
        pltpu.VMEM((n, 8, max(128, slice_rows)), F32),
        pltpu.VMEM((n, 8, max(128, slice_rows)), F32),
        pltpu.VMEM((m, 8, max(128, slice_rows)), F32),
    ] + [dma((count,))] * 6 + [dma, dma, dma((n // 2,)), dma((n // 2,)), dma((m,)), dma((m,))] + [dma((2, m, chunks))] * 2 + [dma((m, chunks))] * 2 + [dma((n // 2,))] * 4 + [dma, dma, dma((m,)), dma((m,))]
    return pl.pallas_call(
        functools.partial(back_kernel, n, m, heads, piece, chunks),
        out_shape=outs,
        in_specs=[VMEM] * 22,
        out_specs=[VMEM] * len(outs),
        scratch_shapes=scratch,
        compiler_params=pltpu.CompilerParams(
            collective_id=2, has_side_effects=True, vmem_limit_bytes=40 << 20
        ),
        name="back",
    )(gm, merged, wts, ro, ext, rank, sendp, pos, kpos, slots, pe, normed, gathered, wq, wv, second, second_cot, fo, pm, vec_feed, gain, bias)


def local(
    first_half,
    second_half,
    bucket_order,
    attend_gain,
    attend_shift,
    queries,
    values,
    mixing,
    feed_gain,
    feed_shift,
    expand,
    expand_bias,
    contract,
    contract_bias,
    cot_first,
    cot_second,
):
    n = lax.axis_size("seq")
    m = lax.axis_size("mp")
    heads = bucket_order.shape[1]
    normed, cot_full, ext, ro, wts, mixed, merged, rank, sendp, pos, kpos, slots, _, gathered = front(
        n, m, heads, second_half, cot_second, bucket_order,
        attend_gain[None], attend_shift[None], queries, values,
    )
    out_first, grad_first, gm, fo, pe, pc, pm, vec_feed = middle(
        n, m, heads, mixed, mixing, first_half, cot_first, cot_full,
        feed_gain[None], feed_shift[None], expand, expand_bias[None], contract,
    )
    out_second, grad_second, pe, pq, pv, pm, vectors = behind(
        n, m, heads, gm, merged, wts, ro, ext, rank, sendp, pos, kpos, slots, pe, normed, gathered,
        queries, values, second_half, cot_second, fo, pm, vec_feed, attend_gain[None], contract_bias[None],
    )
    vectors = vectors[:, 0 : pq.shape[0]]
    return (
        out_first,
        out_second,
        grad_first,
        grad_second,
        vectors[0],
        vectors[1],
        pq,
        pv,
        pm,
        vectors[2],
        vectors[3],
        pe,
        vectors[5],
        pc,
        vectors[4],
    )


def solution(mesh):
    in_specs = (
        P("seq", "mp"),
        P("seq", "mp"),
        P(None, "mp", None),
        P(),
        P(),
        P(None, "mp"),
        P(None, "mp"),
        P("mp", None),
        P(),
        P(),
        P(None, "mp"),
        P("mp"),
        P("mp", None),
        P(),
        P("seq", "mp"),
        P("seq", "mp"),
    )
    out_specs = (
        P("seq", "mp"),
        P("seq", "mp"),
        P("seq", "mp"),
        P("seq", "mp"),
        P("seq"),
        P("seq"),
        P("seq", "mp"),
        P("seq", "mp"),
        P("mp", "seq"),
        P("seq"),
        P("seq"),
        P("seq", "mp"),
        P(("mp", "seq")),
        P("mp", "seq"),
        P("seq"),
    )
    return jax.shard_map(local, mesh=mesh, in_specs=in_specs, out_specs=out_specs, check_vma=False)
```

```python
import functools
import math

import jax
import jax.numpy as jnp
from jax import lax
from jax.experimental import pallas as pl
from jax.experimental.pallas import tpu as pltpu
from jax.sharding import PartitionSpec as P

DH = 128
SPAN = 64
EPSILON = 1e-06
SELF_SCORE = -100000.0
MASKED = -1000000000.0
F32 = jnp.float32
BF16 = jnp.bfloat16
MESH = pl.DeviceIdType.MESH
VMEM = pl.BlockSpec(memory_space=pltpu.VMEM)
HBM = pl.BlockSpec(memory_space=pltpu.HBM)
ROW = (((1,), (1,)), ((), ()))
COL = (((0,), (0,)), ((), ()))


def dot(a, b):
    return jnp.dot(a, b, preferred_element_type=F32)


def dot_nt(a, b):
    return lax.dot_general(a, b, ROW, preferred_element_type=F32)


def dot_tn(a, b):
    return lax.dot_general(a, b, COL, preferred_element_type=F32)


def remote(src, dst, send_sem, recv_sem, axis, index):
    return pltpu.make_async_remote_copy(
        src_ref=src,
        dst_ref=dst,
        send_sem=send_sem,
        recv_sem=recv_sem,
        device_id={axis: index},
        device_id_type=MESH,
    )


def greet(n, m, g, me):
    barrier = pltpu.get_barrier_semaphore()

    @pl.loop(1, n)
    def _(i):
        pl.semaphore_signal(
            barrier, inc=1, device_id={"seq": lax.rem(g + i, n)}, device_id_type=MESH
        )

    @pl.loop(1, m)
    def _(i):
        pl.semaphore_signal(
            barrier, inc=1, device_id={"mp": lax.rem(me + i, m)}, device_id_type=MESH
        )

    pl.semaphore_wait(barrier, n + m - 2)


def iota(shape, dim):
    return lax.broadcasted_iota(jnp.int32, shape, dim)


def fiota(shape, dim):
    return iota(shape, dim).astype(F32)


def split3(x):
    hi = x.astype(BF16).astype(F32)
    rest = x - hi
    mid = rest.astype(BF16).astype(F32)
    return hi, mid, rest - mid


def columns3(x):
    hi, mid, low = split3(x)
    lane = iota((x.shape[0], 128), 1)
    return jnp.where(lane == 0, hi, jnp.where(lane == 1, mid, jnp.where(lane == 2, low, 0.0)))


def rows3(x):
    hi, mid, low = split3(x)
    part = iota((16, x.shape[1]), 0)
    return jnp.where(part == 0, hi, jnp.where(part == 1, mid, jnp.where(part == 2, low, 0.0)))


def column_to_row(x, onehot):
    packed = jnp.transpose(columns3(x))[0:16].astype(BF16)
    return jnp.sum(dot_nt(packed, onehot), axis=0, keepdims=True)


def row_to_column(x, onehot):
    return jnp.sum(dot_nt(onehot, rows3(x).astype(BF16)), axis=1, keepdims=True)


def onehot_rows(row, count):
    return jnp.where(fiota((count, row.shape[1]), 0) == row, 1.0, 0.0).astype(BF16)


def onehot_columns(column, count):
    return jnp.where(fiota((column.shape[0], count), 1) == column, 1.0, 0.0).astype(BF16)


def line_start(me, m, buf, send, recv, chunk):
    @pl.when(me < m - 1)
    def _():
        remote(buf.at[me, chunk], buf.at[me, chunk], send.at[0, me, chunk], recv.at[0, me, chunk], "mp", me + 1).start()

    @pl.when(me > 0)
    def _():
        remote(buf.at[me, chunk], buf.at[me, chunk], send.at[1, me, chunk], recv.at[1, me, chunk], "mp", me - 1).start()


def line_step(me, m, buf, send, recv, chunk, hop):
    @pl.when(me - hop >= 0)
    def _():
        src = me - hop
        part = buf.at[src, chunk]
        remote(part, part, send.at[0, src, chunk], recv.at[0, src, chunk], "mp", me - 1).wait_recv()

        @pl.when(me < m - 1)
        def _():
            remote(part, part, send.at[0, src, chunk], recv.at[0, src, chunk], "mp", me + 1).start()

    @pl.when(me + hop < m)
    def _():
        src = me + hop
        part = buf.at[src, chunk]
        remote(part, part, send.at[1, src, chunk], recv.at[1, src, chunk], "mp", me + 1).wait_recv()

        @pl.when(me > 0)
        def _():
            remote(part, part, send.at[1, src, chunk], recv.at[1, src, chunk], "mp", me - 1).start()


def line_drain(me, m, buf, send, recv, chunk):
    for hop in range(m):

        @pl.when((me - hop >= 0) & (me < m - 1))
        def _():
            part = buf.at[me - hop, chunk]
            remote(part, part, send.at[0, me - hop, chunk], recv.at[0, me - hop, chunk], "mp", me + 1).wait_send()

        @pl.when((me + hop < m) & (me > 0))
        def _():
            part = buf.at[me + hop, chunk]
            remote(part, part, send.at[1, me + hop, chunk], recv.at[1, me + hop, chunk], "mp", me - 1).wait_send()


def spread(n, g, src, dst, piece, send_sem, recv_sem):
    own = pl.multiple_of(g * piece, piece)
    dst[pl.ds(own, piece)] = src[pl.ds(own, piece)]

    @pl.loop(1, n)
    def _(i):
        d = lax.rem(g + i, n)
        there = pl.multiple_of(d * piece, piece)
        remote(src.at[pl.ds(there, piece)], dst.at[pl.ds(own, piece)], send_sem, recv_sem, "seq", d).start()


def all_of(buf, rows, send_sem, recv_sem, g):
    part = buf.at[pl.ds(0, rows)]
    return remote(part, part, send_sem, recv_sem, "seq", g)


def rank_rows(keys_row, keys_col):
    return jnp.sum(jnp.where(keys_col < keys_row, 1.0, 0.0), axis=0, keepdims=True)


def masked(raw, kpos, poscol, item, blocks):
    keys = jnp.concatenate(
        [jnp.broadcast_to(kpos[b, pl.ds(item, 1), :], (SPAN, 2 * SPAN)) for b in range(blocks)], axis=0
    )
    query = poscol[item]
    earlier = keys < query
    return jnp.where(earlier, raw, jnp.where(keys == query, SELF_SCORE, MASKED)), earlier


def share_start(g, n, buf, chunk, send, recv):
    odd = lax.rem(g, 2)
    block = buf.at[g, chunk]
    remote(block, block, send.at[0, chunk], recv.at[g, chunk], "seq", g + 1 - 2 * odd).start()

    @pl.loop(1, n // 2)
    def _(i):
        remote(block, block, send.at[i, chunk], recv.at[g, chunk], "seq", lax.rem(g + 2 * i, n)).start()


def share_forward(g, n, buf, chunk, send, recv):
    odd = lax.rem(g, 2)

    @pl.loop(1, n // 2)
    def _(i):
        src = lax.rem(g + 2 * i, n)
        block = buf.at[src, chunk]
        hop = remote(block, block, send.at[n // 2 + i, chunk], recv.at[src, chunk], "seq", g + 1 - 2 * odd)
        hop.wait_recv()
        hop.start()


def share_wait(g, n, buf, chunk, send, recv):
    sibling = g + 1 - 2 * lax.rem(g, 2)

    @pl.loop(0, n // 2)
    def _(i):
        src = lax.rem(sibling + 2 * i, n)
        block = buf.at[src, chunk]
        remote(block, block, send.at[0, chunk], recv.at[src, chunk], "seq", g).wait_recv()


def share_drain(g, n, buf, chunk, send, recv):
    block = buf.at[g, chunk]

    @pl.loop(0, n // 2)
    def _(i):
        remote(block, block, send.at[i, chunk], recv.at[g, chunk], "seq", g).wait_send()

    @pl.loop(1, n // 2)
    def _(i):
        remote(block, block, send.at[n // 2 + i, chunk], recv.at[g, chunk], "seq", g).wait_send()


def pick(n, piece, tokens, rounds, heads, h, tokcol, table, arrived):
    @pl.loop(0, n)
    def _(s):
        place = pl.ds(pl.multiple_of(s * piece, piece), piece)
        wanted = jnp.concatenate([tokcol[r * heads + h, place, :] for r in range(rounds)], axis=0)
        select = onehot_columns(wanted - (s * tokens).astype(F32), tokens)
        rows = dot(select, table(s)).astype(BF16)
        for r in range(rounds):
            arrived[r * heads + h, place, :] = rows[r * piece : (r + 1) * piece]


def fetch(pairs, sems):
    copies = [pltpu.make_async_copy(src, dst, sems.at[k]) for k, (src, dst) in enumerate(pairs)]
    for copy in copies:
        copy.start()
    return copies


def front_kernel(
    n, m, heads, piece,
    second_in, second_cot_in, order_in, gain_in, shift_in, wq_in, wv_in,
    rows_out, cot_out, ext, ro_out, wts_out, mixed_out, merged_out, rank_out, send_out, pos_out, kpos_out, slots_out, tok_out, zbuf,
    table, arrived, returning, back, unit, pos_ext, poscol, rankcol, sendcol, tokcol, lsecol, lse_send, lse_recv, lse_rows, second, second_cot, order, order_parts, gain, shift, wq, wv,
    zs, zr, cs, cr, xs, xr, prs, prr, bks, bkr, lss, lsr, fs,
):
    g = lax.axis_index("seq")
    me = lax.axis_index("mp")
    tokens, width = rows_out.shape
    part_width = second.shape[1]
    count = order.shape[0]
    rounds = count // heads
    blocks = tokens // SPAN
    chunks = zbuf.shape[1]
    chunk_rows = tokens // chunks
    loads = fetch(
        (
            (second_in, second), (order_in, order_parts), (gain_in, gain), (shift_in, shift),
            (wq_in, wq), (wv_in, wv), (second_cot_in, second_cot),
        ),
        fs,
    )
    greet(n, m, g, me)
    loads[0].wait()

    for chunk in range(chunks):
        zbuf[me, chunk] = second[chunk * chunk_rows : (chunk + 1) * chunk_rows].astype(BF16)
        line_start(me, m, zbuf, zs, zr, chunk)

    for load in loads[1:]:
        load.wait()
    for r in range(rounds):
        order[r * heads : (r + 1) * heads, :] = order_parts[r]
    start = pl.multiple_of(g * tokens, tokens)
    before = pl.multiple_of(lax.rem(g + n - 1, n) * tokens + tokens - 128, 128)
    own_pos = order[:, pl.ds(start, tokens)].astype(F32)
    pos_ext[:, 0:SPAN] = order[:, pl.ds(before, 128)][:, 128 - SPAN :].astype(F32)
    pos_ext[:, SPAN : SPAN + tokens] = own_pos
    for block in range(blocks):
        kpos_out[block] = pos_ext[:, block * SPAN : (block + 2) * SPAN]
    pos_out[...] = own_pos
    total = order.shape[1]
    place = jnp.right_shift(iota((1, total), 1), tokens.bit_length() - 1).astype(F32)
    high = jnp.right_shift(iota((32, tokens), 1), 4) == iota((32, tokens), 0)
    low = jnp.where(jnp.bitwise_and(iota((16, tokens), 1), 15) == iota((16, tokens), 0), 1.0, 0.0).astype(BF16)
    token = fiota((1, tokens), 1)
    for item in range(count):
        local = order[item : item + 1, :] - g * tokens
        a = jnp.where(jnp.right_shift(local, 4) == iota((32, total), 0), place, 0.0).astype(BF16)
        b = jnp.where(jnp.bitwise_and(local, 15) == iota((16, total), 0), 1.0, 0.0).astype(BF16)
        spot = dot_nt(a, b).astype(BF16)
        target = jnp.sum(jnp.where(high, dot(spot, low), 0.0), axis=0, keepdims=True)
        send_out[item : item + 1, :] = target * tokens + token
    keys_row = send_out[...]
    keys_col = jnp.transpose(keys_row)
    pos_col = jnp.transpose(own_pos)
    lane = iota((tokens, 128), 1)

    def tables(item):
        poscol[item] = pos_col[:, item : item + 1]
        send_out[item : item + 1, :] = rank_rows(keys_row[item : item + 1], keys_col[:, item : item + 1])
        rank = rank_rows(own_pos[item : item + 1], pos_col[:, item : item + 1])
        rank_out[item : item + 1, :] = rank
        tokcol[item] = row_to_column(own_pos[item : item + 1], onehot_rows(rank, tokens))

    def project(chunk):
        part = slice(chunk * chunk_rows, (chunk + 1) * chunk_rows)
        rows = jnp.concatenate([zbuf[s, chunk].astype(F32) for s in range(m)], axis=1)
        center = rows - jnp.mean(rows, axis=1, keepdims=True)
        var = jnp.mean(center * center, axis=1, keepdims=True)
        normed = (center * lax.rsqrt(var + EPSILON) * gain[...] + shift[...]).astype(BF16)
        rows_out[part, :] = normed
        q = dot(normed, wq[...]).astype(BF16)
        v = dot(normed, wv[...]).astype(BF16)
        for h in range(heads):
            table[g, h * chunks + chunk, :, 0:DH] = q[:, h * DH : (h + 1) * DH]
            table[g, h * chunks + chunk, :, DH : 2 * DH] = v[:, h * DH : (h + 1) * DH]
        share_start(g, n, table, chunk, xs, xr)

    for wave in range(1, chunks + m - 1):
        for hop in range(m - 1, 0, -1):
            chunk = wave - hop
            if 0 <= chunk < chunks:
                line_step(me, m, zbuf, zs, zr, chunk, hop)
                if hop == m - 1:
                    project(chunk)
                    if chunk > 0:
                        share_forward(g, n, table, chunk - 1, xs, xr)
    for block in range(chunks, heads * chunks):
        share_start(g, n, table, block, xs, xr)
    for item in range(count):
        tables(item)
        if item == count // 2 - 1:
            share_forward(g, n, table, chunks - 1, xs, xr)
    send_col = jnp.transpose(send_out[...])
    rank_col = jnp.transpose(rank_out[...])
    sorted_pos = jnp.zeros((tokens, 128), F32)
    for item in range(count):
        sendcol[item] = send_col[:, item : item + 1]
        rankcol[item] = rank_col[:, item : item + 1]
        sorted_pos = jnp.where(lane == item, tokcol[item], sorted_pos)
    tok_out[...] = jnp.transpose(sorted_pos)[0:count]

    for k, cot in enumerate((second_cot,)):
        cot_out[k, me] = cot[...].astype(BF16)

        @pl.loop(1, m)
        def _(i):
            peer = lax.rem(me + i, m)
            remote(cot_out.at[k, me], cot_out.at[k, me], cs.at[k, i], cr.at[k, me], "mp", peer).start()

    peers_rows = (n - 1) * piece
    after = lax.rem(g + 1, n)
    for h in range(heads):
        blocks_of = range(h * chunks, (h + 1) * chunks)
        for block in blocks_of:
            share_wait(g, n, table, block, xs, xr)
        pick(
            n, piece, tokens, rounds, heads, h, tokcol,
            lambda s: jnp.concatenate([table[s, block] for block in blocks_of], axis=0), arrived,
        )

        @pl.loop(0, rounds)
        def _(r):
            item = r * heads + h
            select = onehot_columns(rankcol[item], tokens)
            ext[item, SPAN:, :] = dot(select, arrived[item]).astype(BF16)
            remote(ext.at[item, pl.ds(tokens, SPAN)], ext.at[item, pl.ds(0, SPAN)], prs.at[item], prr.at[item], "seq", after).start()

        if h + 1 < heads:
            for block in range((h + 1) * chunks, (h + 2) * chunks):
                share_forward(g, n, table, block, xs, xr)

        @pl.loop(0, rounds)
        def _(r):
            item = r * heads + h
            remote(ext.at[item, pl.ds(tokens, SPAN)], ext.at[item, pl.ds(0, SPAN)], prs.at[item], prr.at[item], "seq", after).wait_recv()
            w = ext[item, :, 0:DH].astype(F32)
            unit[...] = (w * lax.rsqrt(jnp.sum(w * w, axis=1, keepdims=True) + EPSILON)).astype(BF16)
            spans = [slice(block * SPAN, (block + 2) * SPAN) for block in range(blocks)]
            raw = jnp.concatenate(
                [dot_nt(ext[item, span.start + SPAN : span.stop, 0:DH], unit[span]) for span in spans], axis=0
            ) * (1.0 / math.sqrt(DH))
            scores = masked(raw, kpos_out, poscol, item, blocks)[0]
            peak = jnp.max(scores, axis=1, keepdims=True)
            lse = peak + jnp.log(jnp.sum(jnp.exp(scores - peak), axis=1, keepdims=True))
            probs = jnp.exp(scores - lse).astype(BF16)
            outs = jnp.concatenate(
                [dot(probs[span.start : span.start + SPAN], ext[item, span, DH : 2 * DH]) for span in spans], axis=0
            ).astype(BF16)
            select = onehot_rows(rank_out[pl.ds(item, 1), :], tokens)
            returning[item] = dot(select, outs).astype(BF16)
            spread(n, g, returning.at[item], back.at[item], piece, bks.at[item], bkr.at[item])
            packed = jnp.transpose(columns3(lse))[0:16]
            slots_out[pl.ds(item, 1), :] = jnp.sum(packed, axis=0, keepdims=True)
            lse_row = jnp.sum(dot_nt(packed.astype(BF16), select), axis=0, keepdims=True)
            for d in range(n):
                lse_send[h, d, pl.ds(r, 1), 0:piece] = lse_row[:, d * piece : (d + 1) * piece]

        lse_recv[h, g] = lse_send[h, g]

        @pl.loop(1, n)
        def _(i):
            d = lax.rem(g + i, n)
            remote(lse_send.at[h, d], lse_recv.at[h, g], lss.at[h], lsr.at[h], "seq", d).start()

    for h in range(heads):
        all_of(lse_recv.at[h], n - 1, lss.at[h], lsr.at[h], g).wait_recv()
        lse_rows[h] = jnp.concatenate([lse_recv[h, d][:, 0:piece] for d in range(n)], axis=1)

        @pl.loop(0, rounds)
        def _(r):
            item = r * heads + h
            all_of(back.at[item], peers_rows, bks.at[item], bkr.at[item], g).wait_recv()
            select = onehot_columns(sendcol[item], tokens)
            ro_out[item] = dot(select, back[item]).astype(BF16)
            lsecol[item] = row_to_column(lse_rows[h, pl.ds(r, 1), :], select)

    weights = jnp.zeros((tokens, 128), F32)
    for h in range(heads):
        logs = [lsecol[r * heads + h] for r in range(rounds)]
        peak = functools.reduce(jnp.maximum, logs)
        full = peak + jnp.log(sum(jnp.exp(x - peak) for x in logs))
        merged = jnp.zeros((tokens, DH), F32)
        for r in range(rounds):
            w = jnp.exp(logs[r] - full)
            weights = jnp.where(lane == r * heads + h, w, weights)
            merged = merged + w * ro_out[r * heads + h].astype(F32)
        merged_out[:, h * DH : (h + 1) * DH] = merged
        mixed_out[:, h * DH : (h + 1) * DH] = merged.astype(BF16)
    wts_out[...] = weights

    for chunk in range(chunks):
        line_drain(me, m, zbuf, zs, zr, chunk)
    for block in range(heads * chunks):
        share_drain(g, n, table, block, xs, xr)
    for k in range(cot_out.shape[0]):

        @pl.loop(1, m)
        def _(i):
            src = lax.rem(me + i, m)
            remote(cot_out.at[k, src], cot_out.at[k, src], cs.at[k, i], cr.at[k, src], "mp", src).wait()

    @pl.loop(0, count)
    def _(item):
        all_of(returning.at[item], peers_rows, bks.at[item], bkr.at[item], g).wait_send()
        remote(ext.at[item, pl.ds(tokens, SPAN)], ext.at[item, pl.ds(0, SPAN)], prs.at[item], prr.at[item], "seq", after).wait_send()

    for h in range(heads):
        all_of(lse_send.at[h], n - 1, lss.at[h], lsr.at[h], g).wait_send()


def front(n, m, heads, second, second_cot, order, gain, shift, wq, wv):
    tokens, part_width = second.shape
    width = wq.shape[0]
    rounds = order.shape[0]
    count = rounds * heads
    piece = tokens // n
    blocks = tokens // SPAN
    chunks = 4
    dma = pltpu.SemaphoreType.DMA
    sds = jax.ShapeDtypeStruct
    outs = (
        sds((tokens, width), BF16),
        sds((1, m, tokens, part_width), BF16),
        sds((count, SPAN + tokens, 2 * DH), BF16),
        sds((count, tokens, DH), BF16),
        sds((tokens, 128), F32),
        sds((tokens, heads * DH), BF16),
        sds((tokens, heads * DH), F32),
        sds((count, tokens), F32),
        sds((count, tokens), F32),
        sds((count, tokens), F32),
        sds((blocks, count, 2 * SPAN), F32),
        sds((count, tokens), F32),
        sds((count, tokens), F32),
        sds((m, chunks, tokens // chunks, part_width), BF16),
    )
    scratch = [
        pltpu.VMEM((n, heads * chunks, tokens // chunks, 2 * DH), BF16),
        pltpu.VMEM((count, tokens, 2 * DH), BF16),
        pltpu.VMEM((count, tokens, DH), BF16),
        pltpu.VMEM((count, tokens, DH), BF16),
        pltpu.VMEM((SPAN + tokens, DH), BF16),
        pltpu.VMEM((count, tokens + 128), F32),
        pltpu.VMEM((count, tokens, 1), F32),
        pltpu.VMEM((count, tokens, 1), F32),
        pltpu.VMEM((count, tokens, 1), F32),
        pltpu.VMEM((count, tokens, 1), F32),
        pltpu.VMEM((count, tokens, 1), F32),
        pltpu.VMEM((heads, n, 8, max(128, piece)), F32),
        pltpu.VMEM((heads, n, 8, max(128, piece)), F32),
        pltpu.VMEM((heads, 8, tokens), F32),
        pltpu.VMEM((tokens, part_width), F32),
        pltpu.VMEM((tokens, part_width), F32),
        pltpu.VMEM((count, order.shape[2]), jnp.int32),
        pltpu.VMEM(order.shape, jnp.int32),
        pltpu.VMEM((1, width), F32),
        pltpu.VMEM((1, width), F32),
        pltpu.VMEM(wq.shape, BF16),
        pltpu.VMEM(wv.shape, BF16),
        dma((2, m, chunks)),
        dma((2, m, chunks)),
        dma((2, m)),
        dma((2, m)),
        dma((n, heads * chunks)),
        dma((n, heads * chunks)),
        dma((count,)),
        dma((count,)),
        dma((count,)),
        dma((count,)),
        dma((heads,)),
        dma((heads,)),
        dma((7,)),
    ]
    return pl.pallas_call(
        functools.partial(front_kernel, n, m, heads, piece),
        out_shape=outs,
        in_specs=[HBM] * 7,
        out_specs=[VMEM] * len(outs),
        scratch_shapes=scratch,
        compiler_params=pltpu.CompilerParams(
            collective_id=0, has_side_effects=True, vmem_limit_bytes=38 << 20
        ),
        name="front",
    )(*(pltpu.with_memory_space_constraint(x, pltpu.HBM) for x in (second, second_cot, order, gain, shift, wq, wv)))


def reduce_start(me, m, own, got, send, recv, chunk):
    @pl.when(me == 0)
    def _():
        for s in range(m - 1, 0, -1):
            remote(own.at[s, chunk], got.at[0, s, chunk], send.at[0, s, chunk], recv.at[0, s, chunk], "mp", me + 1).start()

    @pl.when(me == m - 1)
    def _():
        for s in range(m - 1):
            remote(own.at[s, chunk], got.at[1, s, chunk], send.at[1, s, chunk], recv.at[1, s, chunk], "mp", me - 1).start()


def reduce_forward(me, m, own, got, passing, send, recv, tick, chunks):
    for direction, chunk, peer in ((0, tick - me, me + 1), (1, tick - (m - 1 - me), me - 1)):

        @pl.when((me > 0) & (me < m - 1) & (chunk >= 0) & (chunk < chunks))
        def _():
            for i in range(m - 1):
                s = m - 1 - i if direction == 0 else i

                @pl.when(s > me if direction == 0 else s < me)
                def _():
                    place = (direction, s, chunk)
                    hop = remote(passing.at[place], got.at[place], send.at[place], recv.at[place], "mp", peer)
                    hop.wait_recv()
                    passing[place] = (own[s, chunk].astype(F32) + got[place].astype(F32)).astype(BF16)
                    hop.start()


def reduce_final(me, m, own, got, total, send, recv, chunk):
    total[...] = own[me, chunk].astype(F32)
    for direction, expected in ((0, me > 0), (1, me < m - 1)):

        @pl.when(expected)
        def _():
            place = (direction, me, chunk)
            remote(own.at[me, chunk], got.at[place], send.at[place], recv.at[place], "mp", me).wait_recv()
            total[...] += got[place].astype(F32)


def reduce_drain(me, m, own, got, send, recv, chunk):
    for s in range(m):
        for direction, sent in ((0, me < s), (1, me > s)):
            place = (direction, s, chunk)

            @pl.when(sent)
            def _():
                remote(own.at[s, chunk], got.at[place], send.at[place], recv.at[place], "mp", me).wait_send()


def pack_stats(a, b):
    lane = iota((a.shape[0], 128), 1)
    return jnp.transpose(jnp.where(lane == 0, a, jnp.where(lane == 1, b, 0.0)))[0:8]


def stats_start(me, m, stats, send, recv, chunk):
    @pl.loop(1, m)
    def _(i):
        remote(stats.at[me, chunk], stats.at[me, chunk], send.at[i, chunk], recv.at[me, chunk], "mp", lax.rem(me + i, m)).start()


def stats_wait(me, m, stats, send, recv, chunk):
    @pl.loop(1, m)
    def _(i):
        src = lax.rem(me + i, m)
        remote(stats.at[src, chunk], stats.at[src, chunk], send.at[i, chunk], recv.at[src, chunk], "mp", src).wait()

    return jnp.transpose(sum(stats[s, chunk] for s in range(m)))


def pair_send(g, q, own, got, send, recv):
    odd = lax.rem(g, 2)
    return remote(own.at[2 * q + 1 - odd], got.at[q], send.at[q], recv.at[q], "seq", g + 1 - 2 * odd)


def pair_pass(g, q, own, got, passing, part, fin, send1, recv1, send2, recv2):
    odd = lax.rem(g, 2)
    home = g // 2
    pair_send(g, q, own, got, send1, recv1).wait_recv()
    passing[q] = (own[2 * q + odd].astype(F32) + got[q].astype(F32)).astype(BF16)

    @pl.when(q != home)
    def _():
        remote(passing.at[(q,) + part], fin.at[home], send2.at[q], recv2.at[home], "seq", 2 * q + odd).start()


def pair_total(g, pairs, passing, part, fin, send2, recv2):
    home = g // 2

    @pl.loop(1, pairs)
    def _(i):
        q = lax.rem(home + i, pairs)
        remote(fin.at[q], fin.at[q], send2.at[q], recv2.at[q], "seq", g).wait_recv()

    fin[home] = passing[(home,) + part]


def pair_drain(g, pairs, own, got, passing, part, fin, send1, recv1, send2, recv2):
    home = g // 2

    @pl.loop(0, pairs)
    def _(q):
        pair_send(g, q, own, got, send1, recv1).wait_send()

        @pl.when(q != home)
        def _():
            remote(passing.at[(q,) + part], fin.at[home], send2.at[q], recv2.at[home], "seq", g).wait_send()


def middle_kernel(
    n, m, heads, chunks,
    mixed, mixing_in, first_in, first_cot_in, cot_full, gain, shift, expand_in, expand_bias, contract_in,
    out_first, grad_first, gm_out, fo_out, pe_out, pc_out, pm_out, vec_out,
    part_a, got_a, pass_a, full_a, part_b, got_b, pass_b, full_b, total, stats,
    gact, feed, active, gpre, grad_feed, grad_att, mean_scr, rstd_scr, w_own, w_got, w_pass, w_fin, mixing, first, first_cot, expand, contract,
    ras, rar, gas, gar, rbs, rbr, gbs, gbr, sts, str_, w1s, w1r, w2s, w2r, fs,
):
    g = lax.axis_index("seq")
    me = lax.axis_index("mp")
    tokens, part_width = first.shape
    width = mixing.shape[1]
    hidden = expand.shape[1]
    rows = tokens // chunks
    loads = fetch(
        (
            (mixing_in, mixing), (contract_in, contract), (first_in, first),
            (expand_in, expand), (first_cot_in, first_cot),
        ),
        fs,
    )
    hops = m - 1
    pairs = n // 2
    slice_rows = width // n
    tile = max(256, 2 * slice_rows)
    tiles = width // tile
    tile_pairs = tile // slice_rows // 2
    greet(n, m, g, me)
    loads[0].wait()

    def scatter(part, value, chunk):
        for s in range(m):
            part[s, chunk] = value[:, s * part_width : (s + 1) * part_width].astype(BF16)

    def gather(full, chunk):
        return jnp.concatenate([full[s, chunk] for s in range(m)], axis=1)

    def rows_of(chunk):
        return pl.ds(pl.multiple_of(chunk * rows, rows), rows)

    def during(tick, delay, body, length=chunks):
        @pl.when((tick >= delay) & (tick < delay + length))
        def _():
            body(tick - delay)

    for chunk in range(chunks):
        scatter(part_a, dot(mixed[chunk * rows : (chunk + 1) * rows, :], mixing[...]), chunk)
        reduce_start(me, m, part_a, got_a, ras, rar, chunk)
    for load in loads[1:]:
        load.wait()
    own_cols = pl.multiple_of(me * part_width, part_width)
    gain_own = gain[:, pl.ds(own_cols, part_width)]
    vec_out[...] = jnp.zeros_like(vec_out)

    def finish_first(chunk):
        part = rows_of(chunk)
        reduce_final(me, m, part_a, got_a, total, ras, rar, chunk)
        stream = first[part, :] + total[...]
        out_first[part, :] = stream
        full_a[me, chunk] = stream.astype(BF16)
        line_start(me, m, full_a, gas, gar, chunk)

    def back_of_feed(chunk):
        part = rows_of(chunk)
        cot = jnp.concatenate([cot_full[0, s, part, :] for s in range(m)], axis=1)
        grad_feed[part, :] = cot
        gact[part, :] = dot_nt(cot, contract[...])

    def feed_forward(chunk):
        part = rows_of(chunk)
        x = gather(full_a, chunk).astype(F32)
        mean = jnp.mean(x, axis=1, keepdims=True)
        center = x - mean
        rstd = lax.rsqrt(jnp.mean(center * center, axis=1, keepdims=True) + EPSILON)
        mean_scr[part, :] = mean
        rstd_scr[part, :] = rstd
        xhat = center * rstd
        normed = (xhat * gain[...] + shift[...]).astype(BF16)
        feed[part, :] = normed
        pre = dot(normed, expand[...]) + expand_bias[...]
        gate = 0.5 * (1.0 + lax.erf(pre * (1.0 / math.sqrt(2.0))))
        active[part, :] = (pre * gate).astype(BF16)
        slope = gate + pre * jnp.exp(-0.5 * pre * pre) * (1.0 / math.sqrt(2.0 * math.pi))
        back = (gact[part, :] * slope).astype(BF16)
        gpre[part, :] = back
        term = dot_nt(back, expand[...])
        scatter(part_b, term, chunk)
        reduce_start(me, m, part_b, got_b, rbs, rbr, chunk)
        e = term * gain[...]
        stats[me, chunk] = pack_stats(
            jnp.sum(e, axis=1, keepdims=True), jnp.sum(e * xhat, axis=1, keepdims=True)
        )
        stats_start(me, m, stats, sts, str_, chunk)
        vec_out[0:1, :] += jnp.sum(term * xhat, axis=0, keepdims=True)
        vec_out[1:2, :] += jnp.sum(term, axis=0, keepdims=True)
        vec_out[2:3, :] += jnp.sum(grad_feed[part, :].astype(F32), axis=0, keepdims=True)
        vec_out[3:4, :] += jnp.sum(back.astype(F32), axis=0, keepdims=True)

    def finish_grad(chunk):
        part = rows_of(chunk)
        reduce_final(me, m, part_b, got_b, total, rbs, rbr, chunk)
        sums = stats_wait(me, m, stats, sts, str_, chunk) * (1.0 / width)
        rstd = rstd_scr[part, :]
        xhat = (full_a[me, chunk].astype(F32) - mean_scr[part, :]) * rstd
        stream = first_cot[part, :] + rstd * (
            total[...] * gain_own - sums[:, 0:1] - xhat * sums[:, 1:2]
        )
        grad_first[part, :] = stream
        full_b[me, chunk] = stream.astype(BF16)
        line_start(me, m, full_b, gbs, gbr, chunk)

    def merged_grad(chunk):
        part = rows_of(chunk)
        att = gather(full_b, chunk)
        grad_att[part, :] = att
        gm_out[part, :] = dot_nt(att, mixing[...])

    def weight_tile(k):
        cols = pl.ds(pl.multiple_of(k * tile, tile), tile)
        for lanes, left, right in (
            (slice(0, hidden), feed, gpre),
            (slice(hidden, 2 * hidden), grad_feed, active),
        ):
            product = dot_tn(left[:, cols], right[...]).astype(BF16)
            for i in range(2 * tile_pairs):
                w_own[k * 2 * tile_pairs + i, :, lanes] = product[i * slice_rows : (i + 1) * slice_rows]
        for i in range(tile_pairs):
            pair_send(g, k * tile_pairs + i, w_own, w_got, w1s, w1r).start()

    second_part = (slice(None), pl.ds(hidden, hidden))

    def weight_pass(k):
        for i in range(tile_pairs):
            pair_pass(g, k * tile_pairs + i, w_own, w_got, w_pass, second_part, w_fin, w1s, w1r, w2s, w2r)

    def feed_out(k):
        s = k
        fo_out[s] = dot(active[...], contract[:, pl.ds(pl.multiple_of(s * part_width, part_width), part_width)]).astype(BF16)

    @pl.loop(0, chunks + 4 * hops)
    def _(tick):
        reduce_forward(me, m, part_a, got_a, pass_a, ras, rar, tick, chunks)
        reduce_forward(me, m, part_b, got_b, pass_b, rbs, rbr, tick - 2 * hops, chunks)
        for hop in range(hops, 0, -1):
            during(tick, hops + hop, lambda chunk: line_step(me, m, full_a, gas, gar, chunk, hop))
            during(tick, 3 * hops + hop, lambda chunk: line_step(me, m, full_b, gbs, gbr, chunk, hop))
        during(tick, hops, finish_first)
        during(tick, 3 * hops, finish_grad)
        during(tick, 4 * hops, merged_grad)
        during(tick, 0, back_of_feed)
        during(tick, 2 * hops, feed_forward)
        for j in range(2):
            during(tick, chunks + 2 * hops, lambda k: weight_pass(2 * k + j), tiles // 2)
            during(tick, chunks + 2 * hops - 1, lambda k: weight_tile(2 * k + j), tiles // 2)

    @pl.loop(0, m)
    def _(s):
        feed_out(s)

    @pl.loop(0, width // 256)
    def _(k):
        cols = pl.ds(pl.multiple_of(k * 256, 256), 256)
        pm_out[cols, :] = dot_tn(grad_att[:, cols], mixed[...]).astype(BF16)

    pe_out[...] = w_pass[:, :, 0:hidden]
    pair_total(g, pairs, w_pass, second_part, w_fin, w2s, w2r)
    pc_out[...] = jnp.transpose(sum(w_fin[q].astype(F32) for q in range(pairs)))

    for chunk in range(chunks):
        reduce_drain(me, m, part_a, got_a, ras, rar, chunk)
        reduce_drain(me, m, part_b, got_b, rbs, rbr, chunk)
        line_drain(me, m, full_a, gas, gar, chunk)
        line_drain(me, m, full_b, gbs, gbr, chunk)
    pair_drain(g, pairs, w_own, w_got, w_pass, second_part, w_fin, w1s, w1r, w2s, w2r)


def middle(n, m, heads, mixed, mixing, first, first_cot, cot_full, gain, shift, expand, expand_bias, contract):
    tokens, part_width = first.shape
    width = mixing.shape[1]
    hidden = expand.shape[1]
    chunks = 4
    rows = tokens // chunks
    slice_rows = width // n
    dma = pltpu.SemaphoreType.DMA
    sds = jax.ShapeDtypeStruct
    outs = (
        sds((tokens, part_width), F32),
        sds((tokens, part_width), F32),
        sds((tokens, heads * DH), F32),
        sds((m, tokens, part_width), BF16),
        sds((n // 2, slice_rows, hidden), BF16),
        sds((hidden, slice_rows), F32),
        sds((width, heads * DH), BF16),
        sds((8, width), F32),
    )
    shards = pltpu.VMEM((m, chunks, rows, part_width), BF16)
    both = pltpu.VMEM((2, m, chunks, rows, part_width), BF16)
    pieces = pltpu.VMEM((n // 2, slice_rows, 2 * hidden), BF16)
    scratch = [
        shards, both, both, shards, shards, both, both, shards,
        pltpu.VMEM((rows, part_width), F32),
        pltpu.VMEM((m, chunks, 8, rows), F32),
        pltpu.VMEM((tokens, hidden), F32),
        pltpu.VMEM((tokens, width), BF16),
        pltpu.VMEM((tokens, hidden), BF16),
        pltpu.VMEM((tokens, hidden), BF16),
        pltpu.VMEM((tokens, width), BF16),
        pltpu.VMEM((tokens, width), BF16),
        pltpu.VMEM((tokens, 1), F32),
        pltpu.VMEM((tokens, 1), F32),
        pltpu.VMEM((n, slice_rows, 2 * hidden), BF16),
        pieces, pieces,
        pltpu.VMEM((n // 2, slice_rows, hidden), BF16),
        pltpu.VMEM(mixing.shape, BF16),
        pltpu.VMEM(first.shape, F32),
        pltpu.VMEM(first.shape, F32),
        pltpu.VMEM(expand.shape, BF16),
        pltpu.VMEM(contract.shape, BF16),
    ] + [dma((2, m, chunks))] * 8 + [dma((m, chunks))] * 2 + [dma((n // 2,))] * 4 + [dma((5,))]
    return pl.pallas_call(
        functools.partial(middle_kernel, n, m, heads, chunks),
        out_shape=outs,
        in_specs=[VMEM, HBM, HBM, HBM, VMEM, VMEM, VMEM, HBM, VMEM, HBM],
        out_specs=[VMEM] * len(outs),
        scratch_shapes=scratch,
        compiler_params=pltpu.CompilerParams(
            collective_id=1, has_side_effects=True, vmem_limit_bytes=46 << 20
        ),
        name="middle",
    )(mixed, mixing, first, first_cot, cot_full, gain, shift, expand, expand_bias, contract)


def back_kernel(
    n, m, heads, piece, chunks,
    gm, merged, wts, ro, ext, rank, sendp, pos, kpos, slots, pe, normed, gathered, wq, wv, second, second_cot, fo, pm, vec_feed, gain, bias,
    out_second, grad_second, pe_out, pq_out, pv_out, pm_out, vec_out,
    outgoing, arrived, returning, back, unit, poscol, rankcol, sendcol, lsecol, gl_send, gl_recv, gl_rows, gradk, gradq, grads, wsel,
    prior, incoming, gpair, fo_recv, part_c, got_c, pass_c, total, stats, mean_scr, rstd_scr, w_own, w_got, w_pass, w_fin, e_fin, vec, vec_send, vec_recv, vec_all,
    ins, inr, prs, prr, bks, bkr, gls, glr, es, er, fos, fore, rcs, rcr, sts, str_, w1s, w1r, w2s, w2r, vs, vr, vzs, vzr,
):
    g = lax.axis_index("seq")
    me = lax.axis_index("mp")
    tokens, width = normed.shape
    part_width = second.shape[1]
    count = ro.shape[0]
    rounds = count // heads
    blocks = tokens // SPAN
    rows = tokens // chunks
    scaling = 1.0 / math.sqrt(DH)
    greet(n, m, g, me)

    @pl.loop(1, m)
    def _(i):
        peer = lax.rem(me + i, m)
        remote(fo.at[peer], fo_recv.at[me], fos.at[i], fore.at[me], "mp", peer).start()

    pos_col = jnp.transpose(pos[...])
    send_col = jnp.transpose(sendp[...])
    rank_col = jnp.transpose(rank[...])
    lse_col = jnp.transpose(slots[...])
    for item in range(count):
        poscol[item] = pos_col[:, item : item + 1]
        lsecol[item] = lse_col[:, item : item + 1]
        sendcol[item] = send_col[:, item : item + 1]
        rankcol[item] = rank_col[:, item : item + 1]

    lane = iota((tokens, 128), 1)

    def weight_of(item):
        return jnp.sum(jnp.where(lane == item, wts[...], 0.0), axis=1, keepdims=True)

    def send_item(item):
        h = item % heads
        select = onehot_rows(sendp[item : item + 1, :], tokens)
        outgoing[item] = dot(select, (weight_of(item) * gm[:, h * DH : (h + 1) * DH]).astype(BF16)).astype(BF16)
        spread(n, g, outgoing.at[item], arrived.at[item], piece, ins.at[item], inr.at[item])

    for item in range(2):
        send_item(item)

    for h in range(heads):
        cols = slice(h * DH, (h + 1) * DH)
        gmh = gm[:, cols]
        inner = jnp.sum(gmh * merged[:, cols], axis=1, keepdims=True)
        for r in range(rounds):
            item = r * heads + h
            gs = weight_of(item) * (jnp.sum(gmh * ro[item].astype(F32), axis=1, keepdims=True) - inner)
            row = column_to_row(gs, onehot_rows(sendp[item : item + 1, :], tokens))
            for d in range(n):
                gl_send[d, item : item + 1, 0:piece] = row[:, d * piece : (d + 1) * piece]

    gl_recv[g] = gl_send[g]

    @pl.loop(1, n)
    def _(i):
        d = lax.rem(g + i, n)
        remote(gl_send.at[d], gl_recv.at[g], gls, glr, "seq", d).start()

    for item in range(2, count):
        send_item(item)

    all_of(gl_recv, n - 1, gls, glr, g).wait_recv()
    gl_rows[...] = jnp.concatenate([gl_recv[d][:, 0:piece] for d in range(n)], axis=1)
    peers_rows = (n - 1) * piece
    before = lax.rem(g + n - 1, n)

    @pl.loop(0, count + 2)
    def _(step):
        @pl.when(step < count)
        def _():
            item = step
            slot = lax.rem(item, 3)
            all_of(arrived.at[item], peers_rows, ins.at[item], inr.at[item], g).wait_recv()
            select = onehot_columns(rankcol[item], tokens)
            grads[...] = dot(select, arrived[item]).astype(BF16)
            wsel[...] = row_to_column(gl_rows[pl.ds(item, 1), :], select)
            w = ext[item, :, 0:DH].astype(F32)
            unit[...] = (w * lax.rsqrt(jnp.sum(w * w, axis=1, keepdims=True) + EPSILON)).astype(BF16)
            spans = [slice(block * SPAN, (block + 2) * SPAN) for block in range(blocks)]
            queries = [ext[item, span.start + SPAN : span.stop, 0:DH] for span in spans]
            raw = jnp.concatenate([dot_nt(q, unit[span]) for q, span in zip(queries, spans)], axis=0) * scaling
            gp = jnp.concatenate(
                [dot_nt(grads[span.start : span.start + SPAN], ext[item, span, DH : 2 * DH]) for span in spans], axis=0
            )
            scores, earlier = masked(raw, kpos, poscol, item, blocks)
            probs = jnp.exp(scores - lsecol[item])
            inner = jnp.sum(probs * gp, axis=1, keepdims=True)
            gs = (jnp.where(earlier, probs * (gp - inner + wsel[...]), 0.0) * scaling).astype(BF16)
            low = probs.astype(BF16)
            gradq[slot] = jnp.concatenate(
                [dot(gs[span.start : span.start + SPAN], unit[span]) for span in spans], axis=0
            )
            gk = [dot_tn(gs[span.start : span.start + SPAN], q) for q, span in zip(queries, spans)]
            gv = [
                dot_tn(low[span.start : span.start + SPAN], grads[span.start : span.start + SPAN])
                for span in spans
            ]
            for lanes, slots in ((slice(0, DH), gk), (slice(DH, 2 * DH), gv)):
                prior[item, :, lanes] = slots[0][0:SPAN].astype(BF16)
                for block in range(blocks):
                    lo = block * SPAN
                    own = slots[block][SPAN : 2 * SPAN]
                    if block + 1 < blocks:
                        own = own + slots[block + 1][0:SPAN]
                    gradk[slot, lo : lo + SPAN, lanes] = own
            remote(prior.at[item], incoming.at[item], prs.at[item], prr.at[item], "seq", before).start()

        @pl.when(step > 1)
        def _():
            item = step - 2
            slot = lax.rem(item, 3)
            remote(prior.at[item], incoming.at[item], prs.at[item], prr.at[item], "seq", before).wait_recv()
            gradk[slot, tokens - SPAN :, :] += incoming[item].astype(F32)
            w = ext[item, SPAN:, 0:DH].astype(F32)
            inv = lax.rsqrt(jnp.sum(w * w, axis=1, keepdims=True) + EPSILON)
            gk = gradk[slot, :, 0:DH]
            along = jnp.sum(w * gk, axis=1, keepdims=True)
            gq = gradq[slot] + inv * gk - (inv * inv * inv * along) * w
            done = jnp.concatenate([gq.astype(BF16), gradk[slot, :, DH : 2 * DH].astype(BF16)], axis=1)
            select = onehot_rows(rank[pl.ds(item, 1), :], tokens)
            returning[item] = dot(select, done).astype(BF16)
            spread(n, g, returning.at[item], back.at[item], piece, bks.at[item], bkr.at[item])

    home = g // 2
    pairs = n // 2

    @pl.loop(1, pairs)
    def _(i):
        q = lax.rem(home + i, pairs)
        remote(pe.at[q], e_fin.at[home], es.at[q], er.at[home], "seq", 2 * q + lax.rem(g, 2)).start()

    for chunk in range(gathered.shape[1]):
        high = gathered.shape[2]
        x = jnp.concatenate([gathered[s, chunk].astype(F32) for s in range(m)], axis=1)
        mean = jnp.mean(x, axis=1, keepdims=True)
        center = x - mean
        mean_scr[chunk * high : (chunk + 1) * high] = mean
        rstd_scr[chunk * high : (chunk + 1) * high] = lax.rsqrt(
            jnp.mean(center * center, axis=1, keepdims=True) + EPSILON
        )

    gpair[...] = jnp.zeros_like(gpair)

    @pl.loop(0, count)
    def _(item):
        all_of(back.at[item], peers_rows, bks.at[item], bkr.at[item], g).wait_recv()
        select = onehot_columns(sendcol[item], tokens)
        gpair[lax.rem(item, heads)] += dot(select, back[item])

    gq = jnp.concatenate([gpair[h][:, 0:DH] for h in range(heads)], axis=1).astype(BF16)
    gv = jnp.concatenate([gpair[h][:, DH : 2 * DH] for h in range(heads)], axis=1).astype(BF16)
    vec[0:2, :] = jnp.zeros((2, width), F32)
    vec[2:6, :] = vec_feed[0:4, :]
    vec[6:8, :] = jnp.zeros((2, width), F32)
    sub = gathered.shape[2] // rows
    for chunk in range(chunks):
        part = slice(chunk * rows, (chunk + 1) * rows)
        inside = slice((chunk % sub) * rows, (chunk % sub + 1) * rows)
        term = dot_nt(gq[part], wq[...]) + dot_nt(gv[part], wv[...])
        for s in range(m):
            part_c[s, chunk] = term[:, s * part_width : (s + 1) * part_width].astype(BF16)
        reduce_start(me, m, part_c, got_c, rcs, rcr, chunk)
        x = jnp.concatenate([gathered[s, chunk // sub, inside, :].astype(F32) for s in range(m)], axis=1)
        xhat = (x - mean_scr[part]) * rstd_scr[part]
        e = term * gain[...]
        stats[me, chunk] = pack_stats(
            jnp.sum(e, axis=1, keepdims=True), jnp.sum(e * xhat, axis=1, keepdims=True)
        )
        stats_start(me, m, stats, sts, str_, chunk)
        vec[0:1, :] += jnp.sum(term * xhat, axis=0, keepdims=True)
        vec[1:2, :] += jnp.sum(term, axis=0, keepdims=True)

    slice_rows = width // n
    for d in range(n):
        vec_send[d, :, 0:slice_rows] = vec[:, d * slice_rows : (d + 1) * slice_rows]
    vec_recv[g] = vec_send[g]

    @pl.loop(1, n)
    def _(i):
        d = lax.rem(g + i, n)
        remote(vec_send.at[d], vec_recv.at[g], vs, vr, "seq", d).start()

    tile = max(256, 2 * slice_rows)
    tile_pairs = tile // slice_rows // 2
    own_heads = heads * DH

    @pl.loop(0, width // tile)
    def _(k):
        cols = pl.ds(pl.multiple_of(k * tile, tile), tile)
        products = (
            dot_tn(normed[:, cols], gq).astype(BF16),
            dot_tn(normed[:, cols], gv).astype(BF16),
            pm[cols, :],
        )
        for j, product in enumerate(products):
            for i in range(2 * tile_pairs):
                w_own[k * 2 * tile_pairs + i, :, j * own_heads : (j + 1) * own_heads] = product[
                    i * slice_rows : (i + 1) * slice_rows
                ]
        for i in range(tile_pairs):
            pair_send(g, k * tile_pairs + i, w_own, w_got, w1s, w1r).start()

    own_cols = pl.multiple_of(me * part_width, part_width)
    gain_own = gain[:, pl.ds(own_cols, part_width)]
    hops = m - 1

    def finish(chunk):
        part = pl.ds(pl.multiple_of(chunk * rows, rows), rows)
        inside = pl.ds(pl.multiple_of(lax.rem(chunk, sub) * rows, rows), rows)
        reduce_final(me, m, part_c, got_c, total, rcs, rcr, chunk)
        sums = stats_wait(me, m, stats, sts, str_, chunk) * (1.0 / width)
        rstd = rstd_scr[part, :]
        xhat = (gathered[me, chunk // sub, inside, :].astype(F32) - mean_scr[part, :]) * rstd
        grad_second[part, :] = second_cot[part, :] + rstd * (
            total[...] * gain_own - sums[:, 0:1] - xhat * sums[:, 1:2]
        )

    @pl.loop(0, pairs)
    def _(q):
        pair_pass(g, q, w_own, w_got, w_pass, (), w_fin, w1s, w1r, w2s, w2r)

    all_of(vec_recv, n - 1, vs, vr, g).wait_recv()
    vec_all[me] = sum(vec_recv[d] for d in range(n))

    @pl.loop(1, m)
    def _(i):
        peer = lax.rem(me + i, m)
        remote(vec_all.at[me], vec_all.at[me], vzs.at[i], vzr.at[me], "mp", peer).start()

    @pl.loop(0, chunks + hops)
    def _(tick):
        reduce_forward(me, m, part_c, got_c, pass_c, rcs, rcr, tick, chunks)

        @pl.when(tick >= hops)
        def _():
            finish(tick - hops)

    fo_recv[me] = fo[me]

    @pl.loop(1, m)
    def _(i):
        src = lax.rem(me + i, m)
        remote(fo.at[src], fo_recv.at[src], fos.at[i], fore.at[src], "mp", src).wait()

    out_second[...] = (
        second[...]
        + sum(fo_recv[s].astype(F32) for s in range(m))
        + bias[:, pl.ds(own_cols, part_width)]
    )
    @pl.loop(1, m)
    def _(i):
        src = lax.rem(me + i, m)
        remote(vec_all.at[src], vec_all.at[src], vzs.at[i], vzr.at[src], "mp", src).wait()

    row = iota((8, vec_all.shape[2]), 0)
    vec_out[...] = jnp.where(row < 4, sum(vec_all[s] for s in range(m)), vec_all[me])
    pair_total(g, pairs, pe, (), e_fin, es, er)
    pe_out[...] = sum(e_fin[q].astype(F32) for q in range(pairs))
    pair_total(g, pairs, w_pass, (), w_fin, w2s, w2r)
    for j, out in enumerate((pq_out, pv_out)):
        out[...] = sum(w_fin[q, :, j * own_heads : (j + 1) * own_heads].astype(F32) for q in range(pairs))
    pm_out[...] = jnp.transpose(
        sum(w_fin[q, :, 2 * own_heads : 3 * own_heads].astype(F32) for q in range(pairs))
    )
    for chunk in range(chunks):
        reduce_drain(me, m, part_c, got_c, rcs, rcr, chunk)
    pair_drain(g, pairs, w_own, w_got, w_pass, (), w_fin, w1s, w1r, w2s, w2r)
    all_of(vec_send, n - 1, vs, vr, g).wait_send()

    @pl.loop(0, count)
    def _(item):
        all_of(outgoing.at[item], peers_rows, ins.at[item], inr.at[item], g).wait_send()
        all_of(returning.at[item], peers_rows, bks.at[item], bkr.at[item], g).wait_send()
        remote(prior.at[item], incoming.at[item], prs.at[item], prr.at[item], "seq", before).wait_send()

    all_of(gl_send, n - 1, gls, glr, g).wait_send()

    @pl.loop(1, pairs)
    def _(i):
        q = lax.rem(home + i, pairs)
        remote(pe.at[q], e_fin.at[home], es.at[q], er.at[home], "seq", g).wait_send()


def behind(n, m, heads, gm, merged, wts, ro, ext, rank, sendp, pos, kpos, slots, pe, normed, gathered, wq, wv, second, second_cot, fo, pm, vec_feed, gain, bias):
    tokens, part_width = second.shape
    width = normed.shape[1]
    count = ro.shape[0]
    piece = tokens // n
    chunks = 4
    rows = tokens // chunks
    slice_rows = width // n
    dma = pltpu.SemaphoreType.DMA
    sds = jax.ShapeDtypeStruct
    outs = (
        sds((tokens, part_width), F32),
        sds((tokens, part_width), F32),
        sds((slice_rows, pe.shape[2]), F32),
        sds((slice_rows, heads * DH), F32),
        sds((slice_rows, heads * DH), F32),
        sds((heads * DH, slice_rows), F32),
        sds((8, max(128, slice_rows)), F32),
    )
    both = pltpu.VMEM((2, m, chunks, rows, part_width), BF16)
    column = pltpu.VMEM((count, tokens, 1), F32)
    pieces = pltpu.VMEM((n // 2, slice_rows, 3 * heads * DH), BF16)
    scratch = [
        pltpu.VMEM((count, tokens, DH), BF16),
        pltpu.VMEM((count, tokens, DH), BF16),
        pltpu.VMEM((count, tokens, 2 * DH), BF16),
        pltpu.VMEM((count, tokens, 2 * DH), BF16),
        pltpu.VMEM((SPAN + tokens, DH), BF16),
        column, column, column, column,
        pltpu.VMEM((n, count, max(128, piece)), F32),
        pltpu.VMEM((n, count, max(128, piece)), F32),
        pltpu.VMEM((count, tokens), F32),
        pltpu.VMEM((3, tokens, 2 * DH), F32),
        pltpu.VMEM((3, tokens, DH), F32),
        pltpu.VMEM((tokens, DH), BF16),
        pltpu.VMEM((tokens, 1), F32),
        pltpu.VMEM((count, SPAN, 2 * DH), BF16),
        pltpu.VMEM((count, SPAN, 2 * DH), BF16),
        pltpu.VMEM((heads, tokens, 2 * DH), F32),
        pltpu.VMEM((m, tokens, part_width), BF16),
        pltpu.VMEM((m, chunks, rows, part_width), BF16),
        both, both,
        pltpu.VMEM((rows, part_width), F32),
        pltpu.VMEM((m, chunks, 8, rows), F32),
        pltpu.VMEM((tokens, 1), F32),
        pltpu.VMEM((tokens, 1), F32),
        pltpu.VMEM((n, slice_rows, 3 * heads * DH), BF16),
        pieces, pieces, pieces,
        pltpu.VMEM(pe.shape, BF16),
        pltpu.VMEM((8, width), F32),
        pltpu.VMEM((n, 8, max(128, slice_rows)), F32),
        pltpu.VMEM((n, 8, max(128, slice_rows)), F32),
        pltpu.VMEM((m, 8, max(128, slice_rows)), F32),
    ] + [dma((count,))] * 6 + [dma, dma, dma((n // 2,)), dma((n // 2,)), dma((m,)), dma((m,))] + [dma((2, m, chunks))] * 2 + [dma((m, chunks))] * 2 + [dma((n // 2,))] * 4 + [dma, dma, dma((m,)), dma((m,))]
    return pl.pallas_call(
        functools.partial(back_kernel, n, m, heads, piece, chunks),
        out_shape=outs,
        in_specs=[VMEM] * 22,
        out_specs=[VMEM] * len(outs),
        scratch_shapes=scratch,
        compiler_params=pltpu.CompilerParams(
            collective_id=2, has_side_effects=True, vmem_limit_bytes=40 << 20
        ),
        name="back",
    )(gm, merged, wts, ro, ext, rank, sendp, pos, kpos, slots, pe, normed, gathered, wq, wv, second, second_cot, fo, pm, vec_feed, gain, bias)


def local(
    first_half,
    second_half,
    bucket_order,
    attend_gain,
    attend_shift,
    queries,
    values,
    mixing,
    feed_gain,
    feed_shift,
    expand,
    expand_bias,
    contract,
    contract_bias,
    cot_first,
    cot_second,
):
    n = lax.axis_size("seq")
    m = lax.axis_size("mp")
    heads = bucket_order.shape[1]
    normed, cot_full, ext, ro, wts, mixed, merged, rank, sendp, pos, kpos, slots, _, gathered = front(
        n, m, heads, second_half, cot_second, bucket_order,
        attend_gain[None], attend_shift[None], queries, values,
    )
    out_first, grad_first, gm, fo, pe, pc, pm, vec_feed = middle(
        n, m, heads, mixed, mixing, first_half, cot_first, cot_full,
        feed_gain[None], feed_shift[None], expand, expand_bias[None], contract,
    )
    out_second, grad_second, pe, pq, pv, pm, vectors = behind(
        n, m, heads, gm, merged, wts, ro, ext, rank, sendp, pos, kpos, slots, pe, normed, gathered,
        queries, values, second_half, cot_second, fo, pm, vec_feed, attend_gain[None], contract_bias[None],
    )
    vectors = vectors[:, 0 : pq.shape[0]]
    return (
        out_first,
        out_second,
        grad_first,
        grad_second,
        vectors[0],
        vectors[1],
        pq,
        pv,
        pm,
        vectors[2],
        vectors[3],
        pe,
        vectors[5],
        pc,
        vectors[4],
    )


def solution(mesh):
    in_specs = (
        P("seq", "mp"),
        P("seq", "mp"),
        P(None, "mp", None),
        P(),
        P(),
        P(None, "mp"),
        P(None, "mp"),
        P("mp", None),
        P(),
        P(),
        P(None, "mp"),
        P("mp"),
        P("mp", None),
        P(),
        P("seq", "mp"),
        P("seq", "mp"),
    )
    out_specs = (
        P("seq", "mp"),
        P("seq", "mp"),
        P("seq", "mp"),
        P("seq", "mp"),
        P("seq"),
        P("seq"),
        P("seq", "mp"),
        P("seq", "mp"),
        P("mp", "seq"),
        P("seq"),
        P("seq"),
        P("seq", "mp"),
        P(("mp", "seq")),
        P("mp", "seq"),
        P("seq"),
    )
    return jax.shard_map(local, mesh=mesh, in_specs=in_specs, out_specs=out_specs, check_vma=False)
```

```python
import functools
import math

import jax
import jax.numpy as jnp
from jax import lax
from jax.experimental import pallas as pl
from jax.experimental.pallas import tpu as pltpu
from jax.sharding import PartitionSpec as P

DH = 128
SPAN = 64
EPSILON = 1e-06
SELF_SCORE = -100000.0
MASKED = -1000000000.0
F32 = jnp.float32
BF16 = jnp.bfloat16
MESH = pl.DeviceIdType.MESH
VMEM = pl.BlockSpec(memory_space=pltpu.VMEM)
HBM = pl.BlockSpec(memory_space=pltpu.HBM)
ROW = (((1,), (1,)), ((), ()))
COL = (((0,), (0,)), ((), ()))


def dot(a, b):
    return jnp.dot(a, b, preferred_element_type=F32)


def dot_nt(a, b):
    return lax.dot_general(a, b, ROW, preferred_element_type=F32)


def dot_tn(a, b):
    return lax.dot_general(a, b, COL, preferred_element_type=F32)


def remote(src, dst, send_sem, recv_sem, axis, index):
    return pltpu.make_async_remote_copy(
        src_ref=src,
        dst_ref=dst,
        send_sem=send_sem,
        recv_sem=recv_sem,
        device_id={axis: index},
        device_id_type=MESH,
    )


def greet(n, m, g, me):
    barrier = pltpu.get_barrier_semaphore()

    @pl.loop(1, n)
    def _(i):
        pl.semaphore_signal(
            barrier, inc=1, device_id={"seq": lax.rem(g + i, n)}, device_id_type=MESH
        )

    @pl.loop(1, m)
    def _(i):
        pl.semaphore_signal(
            barrier, inc=1, device_id={"mp": lax.rem(me + i, m)}, device_id_type=MESH
        )

    pl.semaphore_wait(barrier, n + m - 2)


def iota(shape, dim):
    return lax.broadcasted_iota(jnp.int32, shape, dim)


def fiota(shape, dim):
    return iota(shape, dim).astype(F32)


def split3(x):
    hi = x.astype(BF16).astype(F32)
    rest = x - hi
    mid = rest.astype(BF16).astype(F32)
    return hi, mid, rest - mid


def columns3(x):
    hi, mid, low = split3(x)
    lane = iota((x.shape[0], 128), 1)
    return jnp.where(lane == 0, hi, jnp.where(lane == 1, mid, jnp.where(lane == 2, low, 0.0)))


def rows3(x):
    hi, mid, low = split3(x)
    part = iota((16, x.shape[1]), 0)
    return jnp.where(part == 0, hi, jnp.where(part == 1, mid, jnp.where(part == 2, low, 0.0)))


def column_to_row(x, onehot):
    packed = jnp.transpose(columns3(x))[0:16].astype(BF16)
    return jnp.sum(dot_nt(packed, onehot), axis=0, keepdims=True)


def row_to_column(x, onehot):
    return jnp.sum(dot_nt(onehot, rows3(x).astype(BF16)), axis=1, keepdims=True)


def onehot_rows(row, count):
    return jnp.where(fiota((count, row.shape[1]), 0) == row, 1.0, 0.0).astype(BF16)


def onehot_columns(column, count):
    return jnp.where(fiota((column.shape[0], count), 1) == column, 1.0, 0.0).astype(BF16)


def line_start(me, m, buf, send, recv, chunk):
    @pl.when(me < m - 1)
    def _():
        remote(buf.at[me, chunk], buf.at[me, chunk], send.at[0, me, chunk], recv.at[0, me, chunk], "mp", me + 1).start()

    @pl.when(me > 0)
    def _():
        remote(buf.at[me, chunk], buf.at[me, chunk], send.at[1, me, chunk], recv.at[1, me, chunk], "mp", me - 1).start()


def line_step(me, m, buf, send, recv, chunk, hop):
    @pl.when(me - hop >= 0)
    def _():
        src = me - hop
        part = buf.at[src, chunk]
        remote(part, part, send.at[0, src, chunk], recv.at[0, src, chunk], "mp", me - 1).wait_recv()

        @pl.when(me < m - 1)
        def _():
            remote(part, part, send.at[0, src, chunk], recv.at[0, src, chunk], "mp", me + 1).start()

    @pl.when(me + hop < m)
    def _():
        src = me + hop
        part = buf.at[src, chunk]
        remote(part, part, send.at[1, src, chunk], recv.at[1, src, chunk], "mp", me + 1).wait_recv()

        @pl.when(me > 0)
        def _():
            remote(part, part, send.at[1, src, chunk], recv.at[1, src, chunk], "mp", me - 1).start()


def line_drain(me, m, buf, send, recv, chunk):
    for hop in range(m):

        @pl.when((me - hop >= 0) & (me < m - 1))
        def _():
            part = buf.at[me - hop, chunk]
            remote(part, part, send.at[0, me - hop, chunk], recv.at[0, me - hop, chunk], "mp", me + 1).wait_send()

        @pl.when((me + hop < m) & (me > 0))
        def _():
            part = buf.at[me + hop, chunk]
            remote(part, part, send.at[1, me + hop, chunk], recv.at[1, me + hop, chunk], "mp", me - 1).wait_send()


def spread(n, g, src, dst, piece, send_sem, recv_sem):
    own = pl.multiple_of(g * piece, piece)
    dst[pl.ds(own, piece)] = src[pl.ds(own, piece)]

    @pl.loop(1, n)
    def _(i):
        d = lax.rem(g + i, n)
        there = pl.multiple_of(d * piece, piece)
        remote(src.at[pl.ds(there, piece)], dst.at[pl.ds(own, piece)], send_sem, recv_sem, "seq", d).start()


def all_of(buf, rows, send_sem, recv_sem, g):
    part = buf.at[pl.ds(0, rows)]
    return remote(part, part, send_sem, recv_sem, "seq", g)


def rank_rows(keys_row, keys_col):
    return jnp.sum(jnp.where(keys_col < keys_row, 1.0, 0.0), axis=0, keepdims=True)


def masked(raw, kpos, poscol, item, blocks):
    keys = jnp.concatenate(
        [jnp.broadcast_to(kpos[b, pl.ds(item, 1), :], (SPAN, 2 * SPAN)) for b in range(blocks)], axis=0
    )
    query = poscol[item]
    earlier = keys < query
    return jnp.where(earlier, raw, jnp.where(keys == query, SELF_SCORE, MASKED)), earlier


def share_start(g, n, buf, chunk, send, recv):
    odd = lax.rem(g, 2)
    block = buf.at[g, chunk]
    remote(block, block, send.at[0, chunk], recv.at[g, chunk], "seq", g + 1 - 2 * odd).start()

    @pl.loop(1, n // 2)
    def _(i):
        remote(block, block, send.at[i, chunk], recv.at[g, chunk], "seq", lax.rem(g + 2 * i, n)).start()


def share_forward(g, n, buf, chunk, send, recv):
    odd = lax.rem(g, 2)

    @pl.loop(1, n // 2)
    def _(i):
        src = lax.rem(g + 2 * i, n)
        block = buf.at[src, chunk]
        hop = remote(block, block, send.at[n // 2 + i, chunk], recv.at[src, chunk], "seq", g + 1 - 2 * odd)
        hop.wait_recv()
        hop.start()


def share_wait(g, n, buf, chunk, send, recv):
    sibling = g + 1 - 2 * lax.rem(g, 2)

    @pl.loop(0, n // 2)
    def _(i):
        src = lax.rem(sibling + 2 * i, n)
        block = buf.at[src, chunk]
        remote(block, block, send.at[0, chunk], recv.at[src, chunk], "seq", g).wait_recv()


def share_drain(g, n, buf, chunk, send, recv):
    block = buf.at[g, chunk]

    @pl.loop(0, n // 2)
    def _(i):
        remote(block, block, send.at[i, chunk], recv.at[g, chunk], "seq", g).wait_send()

    @pl.loop(1, n // 2)
    def _(i):
        remote(block, block, send.at[n // 2 + i, chunk], recv.at[g, chunk], "seq", g).wait_send()


def pick(n, piece, tokens, rounds, heads, h, tokcol, table, arrived):
    @pl.loop(0, n)
    def _(s):
        place = pl.ds(pl.multiple_of(s * piece, piece), piece)
        wanted = jnp.concatenate([tokcol[r * heads + h, place, :] for r in range(rounds)], axis=0)
        select = onehot_columns(wanted - (s * tokens).astype(F32), tokens)
        rows = dot(select, table(s)).astype(BF16)
        for r in range(rounds):
            arrived[r * heads + h, place, :] = rows[r * piece : (r + 1) * piece]


def fetch(pairs, sems):
    copies = [pltpu.make_async_copy(src, dst, sems.at[k]) for k, (src, dst) in enumerate(pairs)]
    for copy in copies:
        copy.start()
    return copies


def front_kernel(
    n, m, heads, piece,
    second_in, second_cot_in, order_in, gain_in, shift_in, wq_in, wv_in,
    rows_out, cot_out, ext, ro_out, wts_out, mixed_out, merged_out, rank_out, send_out, pos_out, kpos_out, slots_out, tok_out, zbuf,
    table, arrived, returning, back, unit, pos_ext, poscol, rankcol, sendcol, tokcol, lsecol, lse_send, lse_recv, lse_rows, second, second_cot, order, order_parts, gain, shift, wq, wv,
    zs, zr, cs, cr, xs, xr, prs, prr, bks, bkr, lss, lsr, fs,
):
    g = lax.axis_index("seq")
    me = lax.axis_index("mp")
    tokens, width = rows_out.shape
    part_width = second.shape[1]
    count = order.shape[0]
    rounds = count // heads
    blocks = tokens // SPAN
    chunks = zbuf.shape[1]
    chunk_rows = tokens // chunks
    loads = fetch(
        (
            (second_in, second), (order_in, order_parts), (gain_in, gain), (shift_in, shift),
            (wq_in, wq), (wv_in, wv), (second_cot_in, second_cot),
        ),
        fs,
    )
    greet(n, m, g, me)
    loads[0].wait()

    for chunk in range(chunks):
        zbuf[me, chunk] = second[chunk * chunk_rows : (chunk + 1) * chunk_rows].astype(BF16)
        line_start(me, m, zbuf, zs, zr, chunk)

    for load in loads[1:]:
        load.wait()
    for r in range(rounds):
        order[r * heads : (r + 1) * heads, :] = order_parts[r]
    start = pl.multiple_of(g * tokens, tokens)
    before = pl.multiple_of(lax.rem(g + n - 1, n) * tokens + tokens - 128, 128)
    own_pos = order[:, pl.ds(start, tokens)].astype(F32)
    pos_ext[:, 0:SPAN] = order[:, pl.ds(before, 128)][:, 128 - SPAN :].astype(F32)
    pos_ext[:, SPAN : SPAN + tokens] = own_pos
    for block in range(blocks):
        kpos_out[block] = pos_ext[:, block * SPAN : (block + 2) * SPAN]
    pos_out[...] = own_pos
    total = order.shape[1]
    place = jnp.right_shift(iota((1, total), 1), tokens.bit_length() - 1).astype(F32)
    high = jnp.right_shift(iota((32, tokens), 1), 4) == iota((32, tokens), 0)
    low = jnp.where(jnp.bitwise_and(iota((16, tokens), 1), 15) == iota((16, tokens), 0), 1.0, 0.0).astype(BF16)
    token = fiota((1, tokens), 1)
    for item in range(count):
        local = order[item : item + 1, :] - g * tokens
        a = jnp.where(jnp.right_shift(local, 4) == iota((32, total), 0), place, 0.0).astype(BF16)
        b = jnp.where(jnp.bitwise_and(local, 15) == iota((16, total), 0), 1.0, 0.0).astype(BF16)
        spot = dot_nt(a, b).astype(BF16)
        target = jnp.sum(jnp.where(high, dot(spot, low), 0.0), axis=0, keepdims=True)
        send_out[item : item + 1, :] = target * tokens + token
    keys_row = send_out[...]
    keys_col = jnp.transpose(keys_row)
    pos_col = jnp.transpose(own_pos)
    lane = iota((tokens, 128), 1)

    def tables(item):
        poscol[item] = pos_col[:, item : item + 1]
        send_out[item : item + 1, :] = rank_rows(keys_row[item : item + 1], keys_col[:, item : item + 1])
        rank = rank_rows(own_pos[item : item + 1], pos_col[:, item : item + 1])
        rank_out[item : item + 1, :] = rank
        tokcol[item] = row_to_column(own_pos[item : item + 1], onehot_rows(rank, tokens))

    def project(chunk):
        part = slice(chunk * chunk_rows, (chunk + 1) * chunk_rows)
        rows = jnp.concatenate([zbuf[s, chunk].astype(F32) for s in range(m)], axis=1)
        center = rows - jnp.mean(rows, axis=1, keepdims=True)
        var = jnp.mean(center * center, axis=1, keepdims=True)
        normed = (center * lax.rsqrt(var + EPSILON) * gain[...] + shift[...]).astype(BF16)
        rows_out[part, :] = normed
        q = dot(normed, wq[...]).astype(BF16)
        v = dot(normed, wv[...]).astype(BF16)
        for h in range(heads):
            table[g, h * chunks + chunk, :, 0:DH] = q[:, h * DH : (h + 1) * DH]
            table[g, h * chunks + chunk, :, DH : 2 * DH] = v[:, h * DH : (h + 1) * DH]
        share_start(g, n, table, chunk, xs, xr)

    for wave in range(1, chunks + m - 1):
        for hop in range(m - 1, 0, -1):
            chunk = wave - hop
            if 0 <= chunk < chunks:
                line_step(me, m, zbuf, zs, zr, chunk, hop)
                if hop == m - 1:
                    project(chunk)
                    if chunk > 0:
                        share_forward(g, n, table, chunk - 1, xs, xr)
    for block in range(chunks, heads * chunks):
        share_start(g, n, table, block, xs, xr)
    for item in range(count):
        tables(item)
        if item == count // 2 - 1:
            share_forward(g, n, table, chunks - 1, xs, xr)
    send_col = jnp.transpose(send_out[...])
    rank_col = jnp.transpose(rank_out[...])
    sorted_pos = jnp.zeros((tokens, 128), F32)
    for item in range(count):
        sendcol[item] = send_col[:, item : item + 1]
        rankcol[item] = rank_col[:, item : item + 1]
        sorted_pos = jnp.where(lane == item, tokcol[item], sorted_pos)
    tok_out[...] = jnp.transpose(sorted_pos)[0:count]

    for k, cot in enumerate((second_cot,)):
        cot_out[k, me] = cot[...].astype(BF16)

        @pl.loop(1, m)
        def _(i):
            peer = lax.rem(me + i, m)
            remote(cot_out.at[k, me], cot_out.at[k, me], cs.at[k, i], cr.at[k, me], "mp", peer).start()

    peers_rows = (n - 1) * piece
    after = lax.rem(g + 1, n)
    for h in range(heads):
        blocks_of = range(h * chunks, (h + 1) * chunks)
        for block in blocks_of:
            share_wait(g, n, table, block, xs, xr)
        pick(
            n, piece, tokens, rounds, heads, h, tokcol,
            lambda s: jnp.concatenate([table[s, block] for block in blocks_of], axis=0), arrived,
        )

        @pl.loop(0, rounds)
        def _(r):
            item = r * heads + h
            select = onehot_columns(rankcol[item], tokens)
            ext[item, SPAN:, :] = dot(select, arrived[item]).astype(BF16)
            remote(ext.at[item, pl.ds(tokens, SPAN)], ext.at[item, pl.ds(0, SPAN)], prs.at[item], prr.at[item], "seq", after).start()

        if h + 1 < heads:
            for block in range((h + 1) * chunks, (h + 2) * chunks):
                share_forward(g, n, table, block, xs, xr)

        @pl.loop(0, rounds)
        def _(r):
            item = r * heads + h
            remote(ext.at[item, pl.ds(tokens, SPAN)], ext.at[item, pl.ds(0, SPAN)], prs.at[item], prr.at[item], "seq", after).wait_recv()
            w = ext[item, :, 0:DH].astype(F32)
            unit[...] = (w * lax.rsqrt(jnp.sum(w * w, axis=1, keepdims=True) + EPSILON)).astype(BF16)
            spans = [slice(block * SPAN, (block + 2) * SPAN) for block in range(blocks)]
            raw = jnp.concatenate(
                [dot_nt(ext[item, span.start + SPAN : span.stop, 0:DH], unit[span]) for span in spans], axis=0
            ) * (1.0 / math.sqrt(DH))
            scores = masked(raw, kpos_out, poscol, item, blocks)[0]
            peak = jnp.max(scores, axis=1, keepdims=True)
            lse = peak + jnp.log(jnp.sum(jnp.exp(scores - peak), axis=1, keepdims=True))
            probs = jnp.exp(scores - lse).astype(BF16)
            outs = jnp.concatenate(
                [dot(probs[span.start : span.start + SPAN], ext[item, span, DH : 2 * DH]) for span in spans], axis=0
            ).astype(BF16)
            select = onehot_rows(rank_out[pl.ds(item, 1), :], tokens)
            returning[item] = dot(select, outs).astype(BF16)
            spread(n, g, returning.at[item], back.at[item], piece, bks.at[item], bkr.at[item])
            packed = jnp.transpose(columns3(lse))[0:16]
            slots_out[pl.ds(item, 1), :] = jnp.sum(packed, axis=0, keepdims=True)
            lse_row = jnp.sum(dot_nt(packed.astype(BF16), select), axis=0, keepdims=True)
            for d in range(n):
                lse_send[h, d, pl.ds(r, 1), 0:piece] = lse_row[:, d * piece : (d + 1) * piece]

        lse_recv[h, g] = lse_send[h, g]

        @pl.loop(1, n)
        def _(i):
            d = lax.rem(g + i, n)
            remote(lse_send.at[h, d], lse_recv.at[h, g], lss.at[h], lsr.at[h], "seq", d).start()

    for h in range(heads):
        all_of(lse_recv.at[h], n - 1, lss.at[h], lsr.at[h], g).wait_recv()
        lse_rows[h] = jnp.concatenate([lse_recv[h, d][:, 0:piece] for d in range(n)], axis=1)

        @pl.loop(0, rounds)
        def _(r):
            item = r * heads + h
            all_of(back.at[item], peers_rows, bks.at[item], bkr.at[item], g).wait_recv()
            select = onehot_columns(sendcol[item], tokens)
            ro_out[item] = dot(select, back[item]).astype(BF16)
            lsecol[item] = row_to_column(lse_rows[h, pl.ds(r, 1), :], select)

    weights = jnp.zeros((tokens, 128), F32)
    for h in range(heads):
        logs = [lsecol[r * heads + h] for r in range(rounds)]
        peak = functools.reduce(jnp.maximum, logs)
        full = peak + jnp.log(sum(jnp.exp(x - peak) for x in logs))
        merged = jnp.zeros((tokens, DH), F32)
        for r in range(rounds):
            w = jnp.exp(logs[r] - full)
            weights = jnp.where(lane == r * heads + h, w, weights)
            merged = merged + w * ro_out[r * heads + h].astype(F32)
        merged_out[:, h * DH : (h + 1) * DH] = merged
        mixed_out[:, h * DH : (h + 1) * DH] = merged.astype(BF16)
    wts_out[...] = weights

    for chunk in range(chunks):
        line_drain(me, m, zbuf, zs, zr, chunk)
    for block in range(heads * chunks):
        share_drain(g, n, table, block, xs, xr)
    for k in range(cot_out.shape[0]):

        @pl.loop(1, m)
        def _(i):
            src = lax.rem(me + i, m)
            remote(cot_out.at[k, src], cot_out.at[k, src], cs.at[k, i], cr.at[k, src], "mp", src).wait()

    @pl.loop(0, count)
    def _(item):
        all_of(returning.at[item], peers_rows, bks.at[item], bkr.at[item], g).wait_send()
        remote(ext.at[item, pl.ds(tokens, SPAN)], ext.at[item, pl.ds(0, SPAN)], prs.at[item], prr.at[item], "seq", after).wait_send()

    for h in range(heads):
        all_of(lse_send.at[h], n - 1, lss.at[h], lsr.at[h], g).wait_send()


def front(n, m, heads, second, second_cot, order, gain, shift, wq, wv):
    tokens, part_width = second.shape
    width = wq.shape[0]
    rounds = order.shape[0]
    count = rounds * heads
    piece = tokens // n
    blocks = tokens // SPAN
    chunks = 4
    dma = pltpu.SemaphoreType.DMA
    sds = jax.ShapeDtypeStruct
    outs = (
        sds((tokens, width), BF16),
        sds((1, m, tokens, part_width), BF16),
        sds((count, SPAN + tokens, 2 * DH), BF16),
        sds((count, tokens, DH), BF16),
        sds((tokens, 128), F32),
        sds((tokens, heads * DH), BF16),
        sds((tokens, heads * DH), F32),
        sds((count, tokens), F32),
        sds((count, tokens), F32),
        sds((count, tokens), F32),
        sds((blocks, count, 2 * SPAN), F32),
        sds((count, tokens), F32),
        sds((count, tokens), F32),
        sds((m, chunks, tokens // chunks, part_width), BF16),
    )
    scratch = [
        pltpu.VMEM((n, heads * chunks, tokens // chunks, 2 * DH), BF16),
        pltpu.VMEM((count, tokens, 2 * DH), BF16),
        pltpu.VMEM((count, tokens, DH), BF16),
        pltpu.VMEM((count, tokens, DH), BF16),
        pltpu.VMEM((SPAN + tokens, DH), BF16),
        pltpu.VMEM((count, tokens + 128), F32),
        pltpu.VMEM((count, tokens, 1), F32),
        pltpu.VMEM((count, tokens, 1), F32),
        pltpu.VMEM((count, tokens, 1), F32),
        pltpu.VMEM((count, tokens, 1), F32),
        pltpu.VMEM((count, tokens, 1), F32),
        pltpu.VMEM((heads, n, 8, max(128, piece)), F32),
        pltpu.VMEM((heads, n, 8, max(128, piece)), F32),
        pltpu.VMEM((heads, 8, tokens), F32),
        pltpu.VMEM((tokens, part_width), F32),
        pltpu.VMEM((tokens, part_width), F32),
        pltpu.VMEM((count, order.shape[2]), jnp.int32),
        pltpu.VMEM(order.shape, jnp.int32),
        pltpu.VMEM((1, width), F32),
        pltpu.VMEM((1, width), F32),
        pltpu.VMEM(wq.shape, BF16),
        pltpu.VMEM(wv.shape, BF16),
        dma((2, m, chunks)),
        dma((2, m, chunks)),
        dma((2, m)),
        dma((2, m)),
        dma((n, heads * chunks)),
        dma((n, heads * chunks)),
        dma((count,)),
        dma((count,)),
        dma((count,)),
        dma((count,)),
        dma((heads,)),
        dma((heads,)),
        dma((7,)),
    ]
    return pl.pallas_call(
        functools.partial(front_kernel, n, m, heads, piece),
        out_shape=outs,
        in_specs=[HBM] * 7,
        out_specs=[VMEM] * len(outs),
        scratch_shapes=scratch,
        compiler_params=pltpu.CompilerParams(
            collective_id=0, has_side_effects=True, vmem_limit_bytes=38 << 20
        ),
        name="front",
    )(*(pltpu.with_memory_space_constraint(x, pltpu.HBM) for x in (second, second_cot, order, gain, shift, wq, wv)))


def reduce_start(me, m, own, got, send, recv, chunk):
    @pl.when(me == 0)
    def _():
        for s in range(m - 1, 0, -1):
            remote(own.at[s, chunk], got.at[0, s, chunk], send.at[0, s, chunk], recv.at[0, s, chunk], "mp", me + 1).start()

    @pl.when(me == m - 1)
    def _():
        for s in range(m - 1):
            remote(own.at[s, chunk], got.at[1, s, chunk], send.at[1, s, chunk], recv.at[1, s, chunk], "mp", me - 1).start()


def reduce_forward(me, m, own, got, passing, send, recv, tick, chunks):
    for direction, chunk, peer in ((0, tick - me, me + 1), (1, tick - (m - 1 - me), me - 1)):

        @pl.when((me > 0) & (me < m - 1) & (chunk >= 0) & (chunk < chunks))
        def _():
            for i in range(m - 1):
                s = m - 1 - i if direction == 0 else i

                @pl.when(s > me if direction == 0 else s < me)
                def _():
                    place = (direction, s, chunk)
                    hop = remote(passing.at[place], got.at[place], send.at[place], recv.at[place], "mp", peer)
                    hop.wait_recv()
                    passing[place] = (own[s, chunk].astype(F32) + got[place].astype(F32)).astype(BF16)
                    hop.start()


def reduce_final(me, m, own, got, total, send, recv, chunk):
    total[...] = own[me, chunk].astype(F32)
    for direction, expected in ((0, me > 0), (1, me < m - 1)):

        @pl.when(expected)
        def _():
            place = (direction, me, chunk)
            remote(own.at[me, chunk], got.at[place], send.at[place], recv.at[place], "mp", me).wait_recv()
            total[...] += got[place].astype(F32)


def reduce_drain(me, m, own, got, send, recv, chunk):
    for s in range(m):
        for direction, sent in ((0, me < s), (1, me > s)):
            place = (direction, s, chunk)

            @pl.when(sent)
            def _():
                remote(own.at[s, chunk], got.at[place], send.at[place], recv.at[place], "mp", me).wait_send()


def pack_stats(a, b):
    lane = iota((a.shape[0], 128), 1)
    return jnp.transpose(jnp.where(lane == 0, a, jnp.where(lane == 1, b, 0.0)))[0:8]


def stats_start(me, m, stats, send, recv, chunk):
    @pl.loop(1, m)
    def _(i):
        remote(stats.at[me, chunk], stats.at[me, chunk], send.at[i, chunk], recv.at[me, chunk], "mp", lax.rem(me + i, m)).start()


def stats_wait(me, m, stats, send, recv, chunk):
    @pl.loop(1, m)
    def _(i):
        src = lax.rem(me + i, m)
        remote(stats.at[src, chunk], stats.at[src, chunk], send.at[i, chunk], recv.at[src, chunk], "mp", src).wait()

    return jnp.transpose(sum(stats[s, chunk] for s in range(m)))


def pair_send(g, q, own, got, send, recv):
    odd = lax.rem(g, 2)
    return remote(own.at[2 * q + 1 - odd], got.at[q], send.at[q], recv.at[q], "seq", g + 1 - 2 * odd)


def pair_pass(g, q, own, got, passing, part, fin, send1, recv1, send2, recv2):
    odd = lax.rem(g, 2)
    home = g // 2
    pair_send(g, q, own, got, send1, recv1).wait_recv()
    passing[q] = (own[2 * q + odd].astype(F32) + got[q].astype(F32)).astype(BF16)

    @pl.when(q != home)
    def _():
        remote(passing.at[(q,) + part], fin.at[home], send2.at[q], recv2.at[home], "seq", 2 * q + odd).start()


def pair_total(g, pairs, passing, part, fin, send2, recv2):
    home = g // 2

    @pl.loop(1, pairs)
    def _(i):
        q = lax.rem(home + i, pairs)
        remote(fin.at[q], fin.at[q], send2.at[q], recv2.at[q], "seq", g).wait_recv()

    fin[home] = passing[(home,) + part]


def pair_drain(g, pairs, own, got, passing, part, fin, send1, recv1, send2, recv2):
    home = g // 2

    @pl.loop(0, pairs)
    def _(q):
        pair_send(g, q, own, got, send1, recv1).wait_send()

        @pl.when(q != home)
        def _():
            remote(passing.at[(q,) + part], fin.at[home], send2.at[q], recv2.at[home], "seq", g).wait_send()


def middle_kernel(
    n, m, heads, chunks,
    mixed, mixing_in, first_in, first_cot_in, cot_full, gain, shift, expand_in, expand_bias, contract_in,
    out_first, grad_first, gm_out, fo_out, pe_out, pc_out, pm_out, vec_out,
    part_a, got_a, pass_a, full_a, part_b, got_b, pass_b, full_b, total, stats,
    gact, feed, active, gpre, grad_feed, grad_att, mean_scr, rstd_scr, w_own, w_got, w_pass, w_fin, mixing, first, first_cot, expand, contract,
    ras, rar, gas, gar, rbs, rbr, gbs, gbr, sts, str_, w1s, w1r, w2s, w2r, fs,
):
    g = lax.axis_index("seq")
    me = lax.axis_index("mp")
    tokens, part_width = first.shape
    width = mixing.shape[1]
    hidden = expand.shape[1]
    rows = tokens // chunks
    loads = fetch(
        (
            (mixing_in, mixing), (contract_in, contract), (first_in, first),
            (expand_in, expand), (first_cot_in, first_cot),
        ),
        fs,
    )
    hops = m - 1
    pairs = n // 2
    slice_rows = width // n
    tile = max(256, 2 * slice_rows)
    tiles = width // tile
    tile_pairs = tile // slice_rows // 2
    greet(n, m, g, me)
    loads[0].wait()

    def scatter(part, value, chunk):
        for s in range(m):
            part[s, chunk] = value[:, s * part_width : (s + 1) * part_width].astype(BF16)

    def gather(full, chunk):
        return jnp.concatenate([full[s, chunk] for s in range(m)], axis=1)

    def rows_of(chunk):
        return pl.ds(pl.multiple_of(chunk * rows, rows), rows)

    def during(tick, delay, body, length=chunks):
        @pl.when((tick >= delay) & (tick < delay + length))
        def _():
            body(tick - delay)

    for chunk in range(chunks):
        scatter(part_a, dot(mixed[chunk * rows : (chunk + 1) * rows, :], mixing[...]), chunk)
        reduce_start(me, m, part_a, got_a, ras, rar, chunk)
    for load in loads[1:]:
        load.wait()
    own_cols = pl.multiple_of(me * part_width, part_width)
    gain_own = gain[:, pl.ds(own_cols, part_width)]
    vec_out[...] = jnp.zeros_like(vec_out)

    def finish_first(chunk):
        part = rows_of(chunk)
        reduce_final(me, m, part_a, got_a, total, ras, rar, chunk)
        stream = first[part, :] + total[...]
        out_first[part, :] = stream
        full_a[me, chunk] = stream.astype(BF16)
        line_start(me, m, full_a, gas, gar, chunk)

    def back_of_feed(chunk):
        part = rows_of(chunk)
        cot = jnp.concatenate([cot_full[0, s, part, :] for s in range(m)], axis=1)
        grad_feed[part, :] = cot
        gact[part, :] = dot_nt(cot, contract[...])

    def feed_forward(chunk):
        part = rows_of(chunk)
        x = gather(full_a, chunk).astype(F32)
        mean = jnp.mean(x, axis=1, keepdims=True)
        center = x - mean
        rstd = lax.rsqrt(jnp.mean(center * center, axis=1, keepdims=True) + EPSILON)
        mean_scr[part, :] = mean
        rstd_scr[part, :] = rstd
        xhat = center * rstd
        normed = (xhat * gain[...] + shift[...]).astype(BF16)
        feed[part, :] = normed
        pre = dot(normed, expand[...]) + expand_bias[...]
        gate = 0.5 * (1.0 + lax.erf(pre * (1.0 / math.sqrt(2.0))))
        active[part, :] = (pre * gate).astype(BF16)
        slope = gate + pre * jnp.exp(-0.5 * pre * pre) * (1.0 / math.sqrt(2.0 * math.pi))
        back = (gact[part, :] * slope).astype(BF16)
        gpre[part, :] = back
        term = dot_nt(back, expand[...])
        scatter(part_b, term, chunk)
        reduce_start(me, m, part_b, got_b, rbs, rbr, chunk)
        e = term * gain[...]
        stats[me, chunk] = pack_stats(
            jnp.sum(e, axis=1, keepdims=True), jnp.sum(e * xhat, axis=1, keepdims=True)
        )
        stats_start(me, m, stats, sts, str_, chunk)
        vec_out[0:1, :] += jnp.sum(term * xhat, axis=0, keepdims=True)
        vec_out[1:2, :] += jnp.sum(term, axis=0, keepdims=True)
        vec_out[2:3, :] += jnp.sum(grad_feed[part, :].astype(F32), axis=0, keepdims=True)
        vec_out[3:4, :] += jnp.sum(back.astype(F32), axis=0, keepdims=True)

    def finish_grad(chunk):
        part = rows_of(chunk)
        reduce_final(me, m, part_b, got_b, total, rbs, rbr, chunk)
        sums = stats_wait(me, m, stats, sts, str_, chunk) * (1.0 / width)
        rstd = rstd_scr[part, :]
        xhat = (full_a[me, chunk].astype(F32) - mean_scr[part, :]) * rstd
        stream = first_cot[part, :] + rstd * (
            total[...] * gain_own - sums[:, 0:1] - xhat * sums[:, 1:2]
        )
        grad_first[part, :] = stream
        full_b[me, chunk] = stream.astype(BF16)
        line_start(me, m, full_b, gbs, gbr, chunk)

    def merged_grad(chunk):
        part = rows_of(chunk)
        att = gather(full_b, chunk)
        grad_att[part, :] = att
        gm_out[part, :] = dot_nt(att, mixing[...])

    def weight_tile(k):
        cols = pl.ds(pl.multiple_of(k * tile, tile), tile)
        for lanes, left, right in (
            (slice(0, hidden), feed, gpre),
            (slice(hidden, 2 * hidden), grad_feed, active),
        ):
            product = dot_tn(left[:, cols], right[...]).astype(BF16)
            for i in range(2 * tile_pairs):
                w_own[k * 2 * tile_pairs + i, :, lanes] = product[i * slice_rows : (i + 1) * slice_rows]
        for i in range(tile_pairs):
            pair_send(g, k * tile_pairs + i, w_own, w_got, w1s, w1r).start()

    second_part = (slice(None), pl.ds(hidden, hidden))

    def weight_pass(k):
        for i in range(tile_pairs):
            pair_pass(g, k * tile_pairs + i, w_own, w_got, w_pass, second_part, w_fin, w1s, w1r, w2s, w2r)

    def feed_out(k):
        s = k
        fo_out[s] = dot(active[...], contract[:, pl.ds(pl.multiple_of(s * part_width, part_width), part_width)]).astype(BF16)

    @pl.loop(0, chunks + 4 * hops)
    def _(tick):
        reduce_forward(me, m, part_a, got_a, pass_a, ras, rar, tick, chunks)
        reduce_forward(me, m, part_b, got_b, pass_b, rbs, rbr, tick - 2 * hops, chunks)
        for hop in range(hops, 0, -1):
            during(tick, hops + hop, lambda chunk: line_step(me, m, full_a, gas, gar, chunk, hop))
            during(tick, 3 * hops + hop, lambda chunk: line_step(me, m, full_b, gbs, gbr, chunk, hop))
        during(tick, hops, finish_first)
        during(tick, 3 * hops, finish_grad)
        during(tick, 4 * hops, merged_grad)
        during(tick, 0, back_of_feed)
        during(tick, 2 * hops, feed_forward)
        for j in range(2):
            during(tick, chunks + 2 * hops, lambda k: weight_pass(2 * k + j), tiles // 2)
            during(tick, chunks + 2 * hops - 1, lambda k: weight_tile(2 * k + j), tiles // 2)

    @pl.loop(0, m)
    def _(s):
        feed_out(s)

    @pl.loop(0, width // 256)
    def _(k):
        cols = pl.ds(pl.multiple_of(k * 256, 256), 256)
        pm_out[cols, :] = dot_tn(grad_att[:, cols], mixed[...]).astype(BF16)

    pe_out[...] = w_pass[:, :, 0:hidden]
    pair_total(g, pairs, w_pass, second_part, w_fin, w2s, w2r)
    pc_out[...] = jnp.transpose(sum(w_fin[q].astype(F32) for q in range(pairs)))

    for chunk in range(chunks):
        reduce_drain(me, m, part_a, got_a, ras, rar, chunk)
        reduce_drain(me, m, part_b, got_b, rbs, rbr, chunk)
        line_drain(me, m, full_a, gas, gar, chunk)
        line_drain(me, m, full_b, gbs, gbr, chunk)
    pair_drain(g, pairs, w_own, w_got, w_pass, second_part, w_fin, w1s, w1r, w2s, w2r)


def middle(n, m, heads, mixed, mixing, first, first_cot, cot_full, gain, shift, expand, expand_bias, contract):
    tokens, part_width = first.shape
    width = mixing.shape[1]
    hidden = expand.shape[1]
    chunks = 4
    rows = tokens // chunks
    slice_rows = width // n
    dma = pltpu.SemaphoreType.DMA
    sds = jax.ShapeDtypeStruct
    outs = (
        sds((tokens, part_width), F32),
        sds((tokens, part_width), F32),
        sds((tokens, heads * DH), F32),
        sds((m, tokens, part_width), BF16),
        sds((n // 2, slice_rows, hidden), BF16),
        sds((hidden, slice_rows), F32),
        sds((width, heads * DH), BF16),
        sds((8, width), F32),
    )
    shards = pltpu.VMEM((m, chunks, rows, part_width), BF16)
    both = pltpu.VMEM((2, m, chunks, rows, part_width), BF16)
    pieces = pltpu.VMEM((n // 2, slice_rows, 2 * hidden), BF16)
    scratch = [
        shards, both, both, shards, shards, both, both, shards,
        pltpu.VMEM((rows, part_width), F32),
        pltpu.VMEM((m, chunks, 8, rows), F32),
        pltpu.VMEM((tokens, hidden), F32),
        pltpu.VMEM((tokens, width), BF16),
        pltpu.VMEM((tokens, hidden), BF16),
        pltpu.VMEM((tokens, hidden), BF16),
        pltpu.VMEM((tokens, width), BF16),
        pltpu.VMEM((tokens, width), BF16),
        pltpu.VMEM((tokens, 1), F32),
        pltpu.VMEM((tokens, 1), F32),
        pltpu.VMEM((n, slice_rows, 2 * hidden), BF16),
        pieces, pieces,
        pltpu.VMEM((n // 2, slice_rows, hidden), BF16),
        pltpu.VMEM(mixing.shape, BF16),
        pltpu.VMEM(first.shape, F32),
        pltpu.VMEM(first.shape, F32),
        pltpu.VMEM(expand.shape, BF16),
        pltpu.VMEM(contract.shape, BF16),
    ] + [dma((2, m, chunks))] * 8 + [dma((m, chunks))] * 2 + [dma((n // 2,))] * 4 + [dma((5,))]
    return pl.pallas_call(
        functools.partial(middle_kernel, n, m, heads, chunks),
        out_shape=outs,
        in_specs=[VMEM, HBM, HBM, HBM, VMEM, VMEM, VMEM, HBM, VMEM, HBM],
        out_specs=[VMEM] * len(outs),
        scratch_shapes=scratch,
        compiler_params=pltpu.CompilerParams(
            collective_id=1, has_side_effects=True, vmem_limit_bytes=46 << 20
        ),
        name="middle",
    )(mixed, mixing, first, first_cot, cot_full, gain, shift, expand, expand_bias, contract)


def back_kernel(
    n, m, heads, piece, chunks,
    gm, merged, wts, ro, ext, rank, sendp, pos, kpos, slots, pe, normed, gathered, wq, wv, second, second_cot, fo, pm, vec_feed, gain, bias,
    out_second, grad_second, pe_out, pq_out, pv_out, pm_out, vec_out,
    outgoing, arrived, returning, back, unit, poscol, rankcol, sendcol, lsecol, gl_send, gl_recv, gl_rows, gradk, gradq, grads, wsel,
    prior, incoming, gpair, fo_recv, part_c, got_c, pass_c, total, stats, mean_scr, rstd_scr, w_own, w_got, w_pass, w_fin, e_fin, vec, vec_send, vec_recv, vec_all,
    ins, inr, prs, prr, bks, bkr, gls, glr, es, er, fos, fore, rcs, rcr, sts, str_, w1s, w1r, w2s, w2r, vs, vr, vzs, vzr,
):
    g = lax.axis_index("seq")
    me = lax.axis_index("mp")
    tokens, width = normed.shape
    part_width = second.shape[1]
    count = ro.shape[0]
    rounds = count // heads
    blocks = tokens // SPAN
    rows = tokens // chunks
    scaling = 1.0 / math.sqrt(DH)
    greet(n, m, g, me)

    @pl.loop(1, m)
    def _(i):
        peer = lax.rem(me + i, m)
        remote(fo.at[peer], fo_recv.at[me], fos.at[i], fore.at[me], "mp", peer).start()

    pos_col = jnp.transpose(pos[...])
    send_col = jnp.transpose(sendp[...])
    rank_col = jnp.transpose(rank[...])
    lse_col = jnp.transpose(slots[...])
    for item in range(count):
        poscol[item] = pos_col[:, item : item + 1]
        lsecol[item] = lse_col[:, item : item + 1]
        sendcol[item] = send_col[:, item : item + 1]
        rankcol[item] = rank_col[:, item : item + 1]

    lane = iota((tokens, 128), 1)

    def weight_of(item):
        return jnp.sum(jnp.where(lane == item, wts[...], 0.0), axis=1, keepdims=True)

    def send_item(item):
        h = item % heads
        select = onehot_rows(sendp[item : item + 1, :], tokens)
        outgoing[item] = dot(select, (weight_of(item) * gm[:, h * DH : (h + 1) * DH]).astype(BF16)).astype(BF16)
        spread(n, g, outgoing.at[item], arrived.at[item], piece, ins.at[item], inr.at[item])

    for item in range(2):
        send_item(item)

    for h in range(heads):
        cols = slice(h * DH, (h + 1) * DH)
        gmh = gm[:, cols]
        inner = jnp.sum(gmh * merged[:, cols], axis=1, keepdims=True)
        for r in range(rounds):
            item = r * heads + h
            gs = weight_of(item) * (jnp.sum(gmh * ro[item].astype(F32), axis=1, keepdims=True) - inner)
            row = column_to_row(gs, onehot_rows(sendp[item : item + 1, :], tokens))
            for d in range(n):
                gl_send[d, item : item + 1, 0:piece] = row[:, d * piece : (d + 1) * piece]

    gl_recv[g] = gl_send[g]

    @pl.loop(1, n)
    def _(i):
        d = lax.rem(g + i, n)
        remote(gl_send.at[d], gl_recv.at[g], gls, glr, "seq", d).start()

    for item in range(2, count):
        send_item(item)

    all_of(gl_recv, n - 1, gls, glr, g).wait_recv()
    gl_rows[...] = jnp.concatenate([gl_recv[d][:, 0:piece] for d in range(n)], axis=1)
    peers_rows = (n - 1) * piece
    before = lax.rem(g + n - 1, n)

    @pl.loop(0, count + 2)
    def _(step):
        @pl.when(step < count)
        def _():
            item = step
            slot = lax.rem(item, 3)
            all_of(arrived.at[item], peers_rows, ins.at[item], inr.at[item], g).wait_recv()
            select = onehot_columns(rankcol[item], tokens)
            grads[...] = dot(select, arrived[item]).astype(BF16)
            wsel[...] = row_to_column(gl_rows[pl.ds(item, 1), :], select)
            w = ext[item, :, 0:DH].astype(F32)
            unit[...] = (w * lax.rsqrt(jnp.sum(w * w, axis=1, keepdims=True) + EPSILON)).astype(BF16)
            spans = [slice(block * SPAN, (block + 2) * SPAN) for block in range(blocks)]
            queries = [ext[item, span.start + SPAN : span.stop, 0:DH] for span in spans]
            raw = jnp.concatenate([dot_nt(q, unit[span]) for q, span in zip(queries, spans)], axis=0) * scaling
            gp = jnp.concatenate(
                [dot_nt(grads[span.start : span.start + SPAN], ext[item, span, DH : 2 * DH]) for span in spans], axis=0
            )
            scores, earlier = masked(raw, kpos, poscol, item, blocks)
            probs = jnp.exp(scores - lsecol[item])
            inner = jnp.sum(probs * gp, axis=1, keepdims=True)
            gs = (jnp.where(earlier, probs * (gp - inner + wsel[...]), 0.0) * scaling).astype(BF16)
            low = probs.astype(BF16)
            gradq[slot] = jnp.concatenate(
                [dot(gs[span.start : span.start + SPAN], unit[span]) for span in spans], axis=0
            )
            gk = [dot_tn(gs[span.start : span.start + SPAN], q) for q, span in zip(queries, spans)]
            gv = [
                dot_tn(low[span.start : span.start + SPAN], grads[span.start : span.start + SPAN])
                for span in spans
            ]
            for lanes, slots in ((slice(0, DH), gk), (slice(DH, 2 * DH), gv)):
                prior[item, :, lanes] = slots[0][0:SPAN].astype(BF16)
                for block in range(blocks):
                    lo = block * SPAN
                    own = slots[block][SPAN : 2 * SPAN]
                    if block + 1 < blocks:
                        own = own + slots[block + 1][0:SPAN]
                    gradk[slot, lo : lo + SPAN, lanes] = own
            remote(prior.at[item], incoming.at[item], prs.at[item], prr.at[item], "seq", before).start()

        @pl.when(step > 1)
        def _():
            item = step - 2
            slot = lax.rem(item, 3)
            remote(prior.at[item], incoming.at[item], prs.at[item], prr.at[item], "seq", before).wait_recv()
            gradk[slot, tokens - SPAN :, :] += incoming[item].astype(F32)
            w = ext[item, SPAN:, 0:DH].astype(F32)
            inv = lax.rsqrt(jnp.sum(w * w, axis=1, keepdims=True) + EPSILON)
            gk = gradk[slot, :, 0:DH]
            along = jnp.sum(w * gk, axis=1, keepdims=True)
            gq = gradq[slot] + inv * gk - (inv * inv * inv * along) * w
            done = jnp.concatenate([gq.astype(BF16), gradk[slot, :, DH : 2 * DH].astype(BF16)], axis=1)
            select = onehot_rows(rank[pl.ds(item, 1), :], tokens)
            returning[item] = dot(select, done).astype(BF16)
            spread(n, g, returning.at[item], back.at[item], piece, bks.at[item], bkr.at[item])

    home = g // 2
    pairs = n // 2

    @pl.loop(1, pairs)
    def _(i):
        q = lax.rem(home + i, pairs)
        remote(pe.at[q], e_fin.at[home], es.at[q], er.at[home], "seq", 2 * q + lax.rem(g, 2)).start()

    for chunk in range(gathered.shape[1]):
        high = gathered.shape[2]
        x = jnp.concatenate([gathered[s, chunk].astype(F32) for s in range(m)], axis=1)
        mean = jnp.mean(x, axis=1, keepdims=True)
        center = x - mean
        mean_scr[chunk * high : (chunk + 1) * high] = mean
        rstd_scr[chunk * high : (chunk + 1) * high] = lax.rsqrt(
            jnp.mean(center * center, axis=1, keepdims=True) + EPSILON
        )

    gpair[...] = jnp.zeros_like(gpair)

    @pl.loop(0, count)
    def _(item):
        all_of(back.at[item], peers_rows, bks.at[item], bkr.at[item], g).wait_recv()
        select = onehot_columns(sendcol[item], tokens)
        gpair[lax.rem(item, heads)] += dot(select, back[item])

    gq = jnp.concatenate([gpair[h][:, 0:DH] for h in range(heads)], axis=1).astype(BF16)
    gv = jnp.concatenate([gpair[h][:, DH : 2 * DH] for h in range(heads)], axis=1).astype(BF16)
    vec[0:2, :] = jnp.zeros((2, width), F32)
    vec[2:6, :] = vec_feed[0:4, :]
    vec[6:8, :] = jnp.zeros((2, width), F32)
    sub = gathered.shape[2] // rows
    for chunk in range(chunks):
        part = slice(chunk * rows, (chunk + 1) * rows)
        inside = slice((chunk % sub) * rows, (chunk % sub + 1) * rows)
        term = dot_nt(gq[part], wq[...]) + dot_nt(gv[part], wv[...])
        for s in range(m):
            part_c[s, chunk] = term[:, s * part_width : (s + 1) * part_width].astype(BF16)
        reduce_start(me, m, part_c, got_c, rcs, rcr, chunk)
        x = jnp.concatenate([gathered[s, chunk // sub, inside, :].astype(F32) for s in range(m)], axis=1)
        xhat = (x - mean_scr[part]) * rstd_scr[part]
        e = term * gain[...]
        stats[me, chunk] = pack_stats(
            jnp.sum(e, axis=1, keepdims=True), jnp.sum(e * xhat, axis=1, keepdims=True)
        )
        stats_start(me, m, stats, sts, str_, chunk)
        vec[0:1, :] += jnp.sum(term * xhat, axis=0, keepdims=True)
        vec[1:2, :] += jnp.sum(term, axis=0, keepdims=True)

    slice_rows = width // n
    for d in range(n):
        vec_send[d, :, 0:slice_rows] = vec[:, d * slice_rows : (d + 1) * slice_rows]
    vec_recv[g] = vec_send[g]

    @pl.loop(1, n)
    def _(i):
        d = lax.rem(g + i, n)
        remote(vec_send.at[d], vec_recv.at[g], vs, vr, "seq", d).start()

    tile = max(256, 2 * slice_rows)
    tile_pairs = tile // slice_rows // 2
    own_heads = heads * DH

    def weight_tile(k):
        cols = pl.ds(pl.multiple_of(k * tile, tile), tile)
        products = (
            dot_tn(normed[:, cols], gq).astype(BF16),
            dot_tn(normed[:, cols], gv).astype(BF16),
            pm[cols, :],
        )
        for j, product in enumerate(products):
            for i in range(2 * tile_pairs):
                w_own[k * 2 * tile_pairs + i, :, j * own_heads : (j + 1) * own_heads] = product[
                    i * slice_rows : (i + 1) * slice_rows
                ]
        for i in range(tile_pairs):
            pair_send(g, k * tile_pairs + i, w_own, w_got, w1s, w1r).start()

    own_cols = pl.multiple_of(me * part_width, part_width)
    gain_own = gain[:, pl.ds(own_cols, part_width)]
    hops = m - 1

    def finish(chunk):
        part = pl.ds(pl.multiple_of(chunk * rows, rows), rows)
        inside = pl.ds(pl.multiple_of(lax.rem(chunk, sub) * rows, rows), rows)
        reduce_final(me, m, part_c, got_c, total, rcs, rcr, chunk)
        sums = stats_wait(me, m, stats, sts, str_, chunk) * (1.0 / width)
        rstd = rstd_scr[part, :]
        xhat = (gathered[me, chunk // sub, inside, :].astype(F32) - mean_scr[part, :]) * rstd
        grad_second[part, :] = second_cot[part, :] + rstd * (
            total[...] * gain_own - sums[:, 0:1] - xhat * sums[:, 1:2]
        )

    def weight_pass(k):
        for i in range(tile_pairs):
            pair_pass(g, k * tile_pairs + i, w_own, w_got, w_pass, (), w_fin, w1s, w1r, w2s, w2r)

    tiles = width // tile

    @pl.loop(0, max(chunks + hops, tiles + 1))
    def _(tick):
        reduce_forward(me, m, part_c, got_c, pass_c, rcs, rcr, tick, chunks)

        @pl.when((tick >= hops) & (tick < chunks + hops))
        def _():
            finish(tick - hops)

        @pl.when((tick >= 1) & (tick < tiles + 1))
        def _():
            weight_pass(tick - 1)

        @pl.when(tick < tiles)
        def _():
            weight_tile(tick)

        @pl.when(tick == 2)
        def _():
            all_of(vec_recv, n - 1, vs, vr, g).wait_recv()
            vec_all[me] = sum(vec_recv[d] for d in range(n))

            @pl.loop(1, m)
            def _(i):
                peer = lax.rem(me + i, m)
                remote(vec_all.at[me], vec_all.at[me], vzs.at[i], vzr.at[me], "mp", peer).start()

    fo_recv[me] = fo[me]

    @pl.loop(1, m)
    def _(i):
        src = lax.rem(me + i, m)
        remote(fo.at[src], fo_recv.at[src], fos.at[i], fore.at[src], "mp", src).wait()

    out_second[...] = (
        second[...]
        + sum(fo_recv[s].astype(F32) for s in range(m))
        + bias[:, pl.ds(own_cols, part_width)]
    )
    @pl.loop(1, m)
    def _(i):
        src = lax.rem(me + i, m)
        remote(vec_all.at[src], vec_all.at[src], vzs.at[i], vzr.at[src], "mp", src).wait()

    row = iota((8, vec_all.shape[2]), 0)
    vec_out[...] = jnp.where(row < 4, sum(vec_all[s] for s in range(m)), vec_all[me])
    pair_total(g, pairs, pe, (), e_fin, es, er)
    pe_out[...] = sum(e_fin[q].astype(F32) for q in range(pairs))
    pair_total(g, pairs, w_pass, (), w_fin, w2s, w2r)
    for j, out in enumerate((pq_out, pv_out)):
        out[...] = sum(w_fin[q, :, j * own_heads : (j + 1) * own_heads].astype(F32) for q in range(pairs))
    pm_out[...] = jnp.transpose(
        sum(w_fin[q, :, 2 * own_heads : 3 * own_heads].astype(F32) for q in range(pairs))
    )
    for chunk in range(chunks):
        reduce_drain(me, m, part_c, got_c, rcs, rcr, chunk)
    pair_drain(g, pairs, w_own, w_got, w_pass, (), w_fin, w1s, w1r, w2s, w2r)
    all_of(vec_send, n - 1, vs, vr, g).wait_send()

    @pl.loop(0, count)
    def _(item):
        all_of(outgoing.at[item], peers_rows, ins.at[item], inr.at[item], g).wait_send()
        all_of(returning.at[item], peers_rows, bks.at[item], bkr.at[item], g).wait_send()
        remote(prior.at[item], incoming.at[item], prs.at[item], prr.at[item], "seq", before).wait_send()

    all_of(gl_send, n - 1, gls, glr, g).wait_send()

    @pl.loop(1, pairs)
    def _(i):
        q = lax.rem(home + i, pairs)
        remote(pe.at[q], e_fin.at[home], es.at[q], er.at[home], "seq", g).wait_send()


def behind(n, m, heads, gm, merged, wts, ro, ext, rank, sendp, pos, kpos, slots, pe, normed, gathered, wq, wv, second, second_cot, fo, pm, vec_feed, gain, bias):
    tokens, part_width = second.shape
    width = normed.shape[1]
    count = ro.shape[0]
    piece = tokens // n
    chunks = 4
    rows = tokens // chunks
    slice_rows = width // n
    dma = pltpu.SemaphoreType.DMA
    sds = jax.ShapeDtypeStruct
    outs = (
        sds((tokens, part_width), F32),
        sds((tokens, part_width), F32),
        sds((slice_rows, pe.shape[2]), F32),
        sds((slice_rows, heads * DH), F32),
        sds((slice_rows, heads * DH), F32),
        sds((heads * DH, slice_rows), F32),
        sds((8, max(128, slice_rows)), F32),
    )
    both = pltpu.VMEM((2, m, chunks, rows, part_width), BF16)
    column = pltpu.VMEM((count, tokens, 1), F32)
    pieces = pltpu.VMEM((n // 2, slice_rows, 3 * heads * DH), BF16)
    scratch = [
        pltpu.VMEM((count, tokens, DH), BF16),
        pltpu.VMEM((count, tokens, DH), BF16),
        pltpu.VMEM((count, tokens, 2 * DH), BF16),
        pltpu.VMEM((count, tokens, 2 * DH), BF16),
        pltpu.VMEM((SPAN + tokens, DH), BF16),
        column, column, column, column,
        pltpu.VMEM((n, count, max(128, piece)), F32),
        pltpu.VMEM((n, count, max(128, piece)), F32),
        pltpu.VMEM((count, tokens), F32),
        pltpu.VMEM((3, tokens, 2 * DH), F32),
        pltpu.VMEM((3, tokens, DH), F32),
        pltpu.VMEM((tokens, DH), BF16),
        pltpu.VMEM((tokens, 1), F32),
        pltpu.VMEM((count, SPAN, 2 * DH), BF16),
        pltpu.VMEM((count, SPAN, 2 * DH), BF16),
        pltpu.VMEM((heads, tokens, 2 * DH), F32),
        pltpu.VMEM((m, tokens, part_width), BF16),
        pltpu.VMEM((m, chunks, rows, part_width), BF16),
        both, both,
        pltpu.VMEM((rows, part_width), F32),
        pltpu.VMEM((m, chunks, 8, rows), F32),
        pltpu.VMEM((tokens, 1), F32),
        pltpu.VMEM((tokens, 1), F32),
        pltpu.VMEM((n, slice_rows, 3 * heads * DH), BF16),
        pieces, pieces, pieces,
        pltpu.VMEM(pe.shape, BF16),
        pltpu.VMEM((8, width), F32),
        pltpu.VMEM((n, 8, max(128, slice_rows)), F32),
        pltpu.VMEM((n, 8, max(128, slice_rows)), F32),
        pltpu.VMEM((m, 8, max(128, slice_rows)), F32),
    ] + [dma((count,))] * 6 + [dma, dma, dma((n // 2,)), dma((n // 2,)), dma((m,)), dma((m,))] + [dma((2, m, chunks))] * 2 + [dma((m, chunks))] * 2 + [dma((n // 2,))] * 4 + [dma, dma, dma((m,)), dma((m,))]
    return pl.pallas_call(
        functools.partial(back_kernel, n, m, heads, piece, chunks),
        out_shape=outs,
        in_specs=[VMEM] * 22,
        out_specs=[VMEM] * len(outs),
        scratch_shapes=scratch,
        compiler_params=pltpu.CompilerParams(
            collective_id=2, has_side_effects=True, vmem_limit_bytes=40 << 20
        ),
        name="back",
    )(gm, merged, wts, ro, ext, rank, sendp, pos, kpos, slots, pe, normed, gathered, wq, wv, second, second_cot, fo, pm, vec_feed, gain, bias)


def local(
    first_half,
    second_half,
    bucket_order,
    attend_gain,
    attend_shift,
    queries,
    values,
    mixing,
    feed_gain,
    feed_shift,
    expand,
    expand_bias,
    contract,
    contract_bias,
    cot_first,
    cot_second,
):
    n = lax.axis_size("seq")
    m = lax.axis_size("mp")
    heads = bucket_order.shape[1]
    normed, cot_full, ext, ro, wts, mixed, merged, rank, sendp, pos, kpos, slots, _, gathered = front(
        n, m, heads, second_half, cot_second, bucket_order,
        attend_gain[None], attend_shift[None], queries, values,
    )
    out_first, grad_first, gm, fo, pe, pc, pm, vec_feed = middle(
        n, m, heads, mixed, mixing, first_half, cot_first, cot_full,
        feed_gain[None], feed_shift[None], expand, expand_bias[None], contract,
    )
    out_second, grad_second, pe, pq, pv, pm, vectors = behind(
        n, m, heads, gm, merged, wts, ro, ext, rank, sendp, pos, kpos, slots, pe, normed, gathered,
        queries, values, second_half, cot_second, fo, pm, vec_feed, attend_gain[None], contract_bias[None],
    )
    vectors = vectors[:, 0 : pq.shape[0]]
    return (
        out_first,
        out_second,
        grad_first,
        grad_second,
        vectors[0],
        vectors[1],
        pq,
        pv,
        pm,
        vectors[2],
        vectors[3],
        pe,
        vectors[5],
        pc,
        vectors[4],
    )


def solution(mesh):
    in_specs = (
        P("seq", "mp"),
        P("seq", "mp"),
        P(None, "mp", None),
        P(),
        P(),
        P(None, "mp"),
        P(None, "mp"),
        P("mp", None),
        P(),
        P(),
        P(None, "mp"),
        P("mp"),
        P("mp", None),
        P(),
        P("seq", "mp"),
        P("seq", "mp"),
    )
    out_specs = (
        P("seq", "mp"),
        P("seq", "mp"),
        P("seq", "mp"),
        P("seq", "mp"),
        P("seq"),
        P("seq"),
        P("seq", "mp"),
        P("seq", "mp"),
        P("mp", "seq"),
        P("seq"),
        P("seq"),
        P("seq", "mp"),
        P(("mp", "seq")),
        P("mp", "seq"),
        P("seq"),
    )
    return jax.shard_map(local, mesh=mesh, in_specs=in_specs, out_specs=out_specs, check_vma=False)
```

```python
import functools
import math

import jax
import jax.numpy as jnp
from jax import lax
from jax.experimental import pallas as pl
from jax.experimental.pallas import tpu as pltpu
from jax.sharding import PartitionSpec as P

DH = 128
SPAN = 64
EPSILON = 1e-06
SELF_SCORE = -100000.0
MASKED = -1000000000.0
F32 = jnp.float32
BF16 = jnp.bfloat16
MESH = pl.DeviceIdType.MESH
VMEM = pl.BlockSpec(memory_space=pltpu.VMEM)
HBM = pl.BlockSpec(memory_space=pltpu.HBM)
ROW = (((1,), (1,)), ((), ()))
COL = (((0,), (0,)), ((), ()))


def dot(a, b):
    return jnp.dot(a, b, preferred_element_type=F32)


def dot_nt(a, b):
    return lax.dot_general(a, b, ROW, preferred_element_type=F32)


def dot_tn(a, b):
    return lax.dot_general(a, b, COL, preferred_element_type=F32)


def remote(src, dst, send_sem, recv_sem, axis, index):
    return pltpu.make_async_remote_copy(
        src_ref=src,
        dst_ref=dst,
        send_sem=send_sem,
        recv_sem=recv_sem,
        device_id={axis: index},
        device_id_type=MESH,
    )


def greet(n, m, g, me):
    barrier = pltpu.get_barrier_semaphore()

    @pl.loop(1, n)
    def _(i):
        pl.semaphore_signal(
            barrier, inc=1, device_id={"seq": lax.rem(g + i, n)}, device_id_type=MESH
        )

    @pl.loop(1, m)
    def _(i):
        pl.semaphore_signal(
            barrier, inc=1, device_id={"mp": lax.rem(me + i, m)}, device_id_type=MESH
        )

    pl.semaphore_wait(barrier, n + m - 2)


def iota(shape, dim):
    return lax.broadcasted_iota(jnp.int32, shape, dim)


def fiota(shape, dim):
    return iota(shape, dim).astype(F32)


def split3(x):
    hi = x.astype(BF16).astype(F32)
    rest = x - hi
    mid = rest.astype(BF16).astype(F32)
    return hi, mid, rest - mid


def columns3(x):
    hi, mid, low = split3(x)
    lane = iota((x.shape[0], 128), 1)
    return jnp.where(lane == 0, hi, jnp.where(lane == 1, mid, jnp.where(lane == 2, low, 0.0)))


def rows3(x):
    hi, mid, low = split3(x)
    part = iota((16, x.shape[1]), 0)
    return jnp.where(part == 0, hi, jnp.where(part == 1, mid, jnp.where(part == 2, low, 0.0)))


def column_to_row(x, onehot):
    packed = jnp.transpose(columns3(x))[0:16].astype(BF16)
    return jnp.sum(dot_nt(packed, onehot), axis=0, keepdims=True)


def row_to_column(x, onehot):
    return jnp.sum(dot_nt(onehot, rows3(x).astype(BF16)), axis=1, keepdims=True)


def onehot_rows(row, count):
    return jnp.where(fiota((count, row.shape[1]), 0) == row, 1.0, 0.0).astype(BF16)


def onehot_columns(column, count):
    return jnp.where(fiota((column.shape[0], count), 1) == column, 1.0, 0.0).astype(BF16)


def line_start(me, m, buf, send, recv, chunk):
    @pl.when(me < m - 1)
    def _():
        remote(buf.at[me, chunk], buf.at[me, chunk], send.at[0, me, chunk], recv.at[0, me, chunk], "mp", me + 1).start()

    @pl.when(me > 0)
    def _():
        remote(buf.at[me, chunk], buf.at[me, chunk], send.at[1, me, chunk], recv.at[1, me, chunk], "mp", me - 1).start()


def line_step(me, m, buf, send, recv, chunk, hop):
    @pl.when(me - hop >= 0)
    def _():
        src = me - hop
        part = buf.at[src, chunk]
        remote(part, part, send.at[0, src, chunk], recv.at[0, src, chunk], "mp", me - 1).wait_recv()

        @pl.when(me < m - 1)
        def _():
            remote(part, part, send.at[0, src, chunk], recv.at[0, src, chunk], "mp", me + 1).start()

    @pl.when(me + hop < m)
    def _():
        src = me + hop
        part = buf.at[src, chunk]
        remote(part, part, send.at[1, src, chunk], recv.at[1, src, chunk], "mp", me + 1).wait_recv()

        @pl.when(me > 0)
        def _():
            remote(part, part, send.at[1, src, chunk], recv.at[1, src, chunk], "mp", me - 1).start()


def line_drain(me, m, buf, send, recv, chunk):
    for hop in range(m):

        @pl.when((me - hop >= 0) & (me < m - 1))
        def _():
            part = buf.at[me - hop, chunk]
            remote(part, part, send.at[0, me - hop, chunk], recv.at[0, me - hop, chunk], "mp", me + 1).wait_send()

        @pl.when((me + hop < m) & (me > 0))
        def _():
            part = buf.at[me + hop, chunk]
            remote(part, part, send.at[1, me + hop, chunk], recv.at[1, me + hop, chunk], "mp", me - 1).wait_send()


def spread(n, g, src, dst, piece, send_sem, recv_sem):
    own = pl.multiple_of(g * piece, piece)
    dst[pl.ds(own, piece)] = src[pl.ds(own, piece)]

    @pl.loop(1, n)
    def _(i):
        d = lax.rem(g + i, n)
        there = pl.multiple_of(d * piece, piece)
        remote(src.at[pl.ds(there, piece)], dst.at[pl.ds(own, piece)], send_sem, recv_sem, "seq", d).start()


def all_of(buf, rows, send_sem, recv_sem, g):
    part = buf.at[pl.ds(0, rows)]
    return remote(part, part, send_sem, recv_sem, "seq", g)


def rank_rows(keys_row, keys_col):
    return jnp.sum(jnp.where(keys_col < keys_row, 1.0, 0.0), axis=0, keepdims=True)


def masked(raw, kpos, poscol, item, blocks):
    keys = jnp.concatenate(
        [jnp.broadcast_to(kpos[b, pl.ds(item, 1), :], (SPAN, 2 * SPAN)) for b in range(blocks)], axis=0
    )
    query = poscol[item]
    earlier = keys < query
    return jnp.where(earlier, raw, jnp.where(keys == query, SELF_SCORE, MASKED)), earlier


def share_start(g, n, buf, chunk, send, recv):
    odd = lax.rem(g, 2)
    block = buf.at[g, chunk]
    remote(block, block, send.at[0, chunk], recv.at[g, chunk], "seq", g + 1 - 2 * odd).start()

    @pl.loop(1, n // 2)
    def _(i):
        remote(block, block, send.at[i, chunk], recv.at[g, chunk], "seq", lax.rem(g + 2 * i, n)).start()


def share_forward(g, n, buf, chunk, send, recv):
    odd = lax.rem(g, 2)

    @pl.loop(1, n // 2)
    def _(i):
        src = lax.rem(g + 2 * i, n)
        block = buf.at[src, chunk]
        hop = remote(block, block, send.at[n // 2 + i, chunk], recv.at[src, chunk], "seq", g + 1 - 2 * odd)
        hop.wait_recv()
        hop.start()


def share_wait(g, n, buf, chunk, send, recv):
    sibling = g + 1 - 2 * lax.rem(g, 2)

    @pl.loop(0, n // 2)
    def _(i):
        src = lax.rem(sibling + 2 * i, n)
        block = buf.at[src, chunk]
        remote(block, block, send.at[0, chunk], recv.at[src, chunk], "seq", g).wait_recv()


def share_drain(g, n, buf, chunk, send, recv):
    block = buf.at[g, chunk]

    @pl.loop(0, n // 2)
    def _(i):
        remote(block, block, send.at[i, chunk], recv.at[g, chunk], "seq", g).wait_send()

    @pl.loop(1, n // 2)
    def _(i):
        remote(block, block, send.at[n // 2 + i, chunk], recv.at[g, chunk], "seq", g).wait_send()


def pick(n, piece, tokens, rounds, heads, h, tokcol, table, arrived):
    @pl.loop(0, n)
    def _(s):
        place = pl.ds(pl.multiple_of(s * piece, piece), piece)
        wanted = jnp.concatenate([tokcol[r * heads + h, place, :] for r in range(rounds)], axis=0)
        select = onehot_columns(wanted - (s * tokens).astype(F32), tokens)
        rows = dot(select, table(s)).astype(BF16)
        for r in range(rounds):
            arrived[r * heads + h, place, :] = rows[r * piece : (r + 1) * piece]


def fetch(pairs, sems):
    copies = [pltpu.make_async_copy(src, dst, sems.at[k]) for k, (src, dst) in enumerate(pairs)]
    for copy in copies:
        copy.start()
    return copies


def front_kernel(
    n, m, heads, piece,
    second_in, second_cot_in, order_in, gain_in, shift_in, wq_in, wv_in,
    rows_out, cot_out, ext, ro_out, wts_out, mixed_out, merged_out, rank_out, send_out, pos_out, kpos_out, slots_out, tok_out, zbuf,
    table, arrived, returning, back, unit, pos_ext, poscol, rankcol, sendcol, tokcol, lsecol, lse_send, lse_recv, lse_rows, second, second_cot, order, order_parts, gain, shift, wq, wv,
    zs, zr, cs, cr, xs, xr, prs, prr, bks, bkr, lss, lsr, fs,
):
    g = lax.axis_index("seq")
    me = lax.axis_index("mp")
    tokens, width = rows_out.shape
    part_width = second.shape[1]
    count = order.shape[0]
    rounds = count // heads
    blocks = tokens // SPAN
    chunks = zbuf.shape[1]
    chunk_rows = tokens // chunks
    loads = fetch(
        (
            (second_in, second), (order_in, order_parts), (gain_in, gain), (shift_in, shift),
            (wq_in, wq), (wv_in, wv), (second_cot_in, second_cot),
        ),
        fs,
    )
    greet(n, m, g, me)
    loads[0].wait()

    for chunk in range(chunks):
        zbuf[me, chunk] = second[chunk * chunk_rows : (chunk + 1) * chunk_rows].astype(BF16)
        line_start(me, m, zbuf, zs, zr, chunk)

    for load in loads[1:]:
        load.wait()
    for r in range(rounds):
        order[r * heads : (r + 1) * heads, :] = order_parts[r]
    start = pl.multiple_of(g * tokens, tokens)
    before = pl.multiple_of(lax.rem(g + n - 1, n) * tokens + tokens - 128, 128)
    own_pos = order[:, pl.ds(start, tokens)].astype(F32)
    pos_ext[:, 0:SPAN] = order[:, pl.ds(before, 128)][:, 128 - SPAN :].astype(F32)
    pos_ext[:, SPAN : SPAN + tokens] = own_pos
    for block in range(blocks):
        kpos_out[block] = pos_ext[:, block * SPAN : (block + 2) * SPAN]
    pos_out[...] = own_pos
    total = order.shape[1]
    place = jnp.right_shift(iota((1, total), 1), tokens.bit_length() - 1).astype(F32)
    high = jnp.right_shift(iota((32, tokens), 1), 4) == iota((32, tokens), 0)
    low = jnp.where(jnp.bitwise_and(iota((16, tokens), 1), 15) == iota((16, tokens), 0), 1.0, 0.0).astype(BF16)
    token = fiota((1, tokens), 1)
    for item in range(count):
        local = order[item : item + 1, :] - g * tokens
        a = jnp.where(jnp.right_shift(local, 4) == iota((32, total), 0), place, 0.0).astype(BF16)
        b = jnp.where(jnp.bitwise_and(local, 15) == iota((16, total), 0), 1.0, 0.0).astype(BF16)
        spot = dot_nt(a, b).astype(BF16)
        target = jnp.sum(jnp.where(high, dot(spot, low), 0.0), axis=0, keepdims=True)
        send_out[item : item + 1, :] = target * tokens + token
    keys_row = send_out[...]
    keys_col = jnp.transpose(keys_row)
    pos_col = jnp.transpose(own_pos)
    lane = iota((tokens, 128), 1)

    def tables(item):
        poscol[item] = pos_col[:, item : item + 1]
        send_out[item : item + 1, :] = rank_rows(keys_row[item : item + 1], keys_col[:, item : item + 1])
        rank = rank_rows(own_pos[item : item + 1], pos_col[:, item : item + 1])
        rank_out[item : item + 1, :] = rank
        tokcol[item] = row_to_column(own_pos[item : item + 1], onehot_rows(rank, tokens))

    def project(chunk):
        part = slice(chunk * chunk_rows, (chunk + 1) * chunk_rows)
        rows = jnp.concatenate([zbuf[s, chunk].astype(F32) for s in range(m)], axis=1)
        center = rows - jnp.mean(rows, axis=1, keepdims=True)
        var = jnp.mean(center * center, axis=1, keepdims=True)
        normed = (center * lax.rsqrt(var + EPSILON) * gain[...] + shift[...]).astype(BF16)
        rows_out[part, :] = normed
        q = dot(normed, wq[...]).astype(BF16)
        v = dot(normed, wv[...]).astype(BF16)
        for h in range(heads):
            table[g, h * chunks + chunk, :, 0:DH] = q[:, h * DH : (h + 1) * DH]
            table[g, h * chunks + chunk, :, DH : 2 * DH] = v[:, h * DH : (h + 1) * DH]
        share_start(g, n, table, chunk, xs, xr)

    for wave in range(1, chunks + m - 1):
        for hop in range(m - 1, 0, -1):
            chunk = wave - hop
            if 0 <= chunk < chunks:
                line_step(me, m, zbuf, zs, zr, chunk, hop)
                if hop == m - 1:
                    project(chunk)
                    if chunk > 0:
                        share_forward(g, n, table, chunk - 1, xs, xr)
    for block in range(chunks, heads * chunks):
        share_start(g, n, table, block, xs, xr)
    for item in range(count):
        tables(item)
        if item == count // 2 - 1:
            share_forward(g, n, table, chunks - 1, xs, xr)
    send_col = jnp.transpose(send_out[...])
    rank_col = jnp.transpose(rank_out[...])
    sorted_pos = jnp.zeros((tokens, 128), F32)
    for item in range(count):
        sendcol[item] = send_col[:, item : item + 1]
        rankcol[item] = rank_col[:, item : item + 1]
        sorted_pos = jnp.where(lane == item, tokcol[item], sorted_pos)
    tok_out[...] = jnp.transpose(sorted_pos)[0:count]

    for k, cot in enumerate((second_cot,)):
        cot_out[k, me] = cot[...].astype(BF16)

        @pl.loop(1, m)
        def _(i):
            peer = lax.rem(me + i, m)
            remote(cot_out.at[k, me], cot_out.at[k, me], cs.at[k, i], cr.at[k, me], "mp", peer).start()

    peers_rows = (n - 1) * piece
    after = lax.rem(g + 1, n)
    for h in range(heads):
        blocks_of = range(h * chunks, (h + 1) * chunks)
        for block in blocks_of:
            share_wait(g, n, table, block, xs, xr)
        pick(
            n, piece, tokens, rounds, heads, h, tokcol,
            lambda s: jnp.concatenate([table[s, block] for block in blocks_of], axis=0), arrived,
        )

        @pl.loop(0, rounds)
        def _(r):
            item = r * heads + h
            select = onehot_columns(rankcol[item], tokens)
            ext[item, SPAN:, :] = dot(select, arrived[item]).astype(BF16)
            remote(ext.at[item, pl.ds(tokens, SPAN)], ext.at[item, pl.ds(0, SPAN)], prs.at[item], prr.at[item], "seq", after).start()

        if h + 1 < heads:
            for block in range((h + 1) * chunks, (h + 2) * chunks):
                share_forward(g, n, table, block, xs, xr)

        @pl.loop(0, rounds)
        def _(r):
            item = r * heads + h
            remote(ext.at[item, pl.ds(tokens, SPAN)], ext.at[item, pl.ds(0, SPAN)], prs.at[item], prr.at[item], "seq", after).wait_recv()
            w = ext[item, :, 0:DH].astype(F32)
            unit[...] = (w * lax.rsqrt(jnp.sum(w * w, axis=1, keepdims=True) + EPSILON)).astype(BF16)
            spans = [slice(block * SPAN, (block + 2) * SPAN) for block in range(blocks)]
            raw = jnp.concatenate(
                [dot_nt(ext[item, span.start + SPAN : span.stop, 0:DH], unit[span]) for span in spans], axis=0
            ) * (1.0 / math.sqrt(DH))
            scores = masked(raw, kpos_out, poscol, item, blocks)[0]
            peak = jnp.max(scores, axis=1, keepdims=True)
            lse = peak + jnp.log(jnp.sum(jnp.exp(scores - peak), axis=1, keepdims=True))
            probs = jnp.exp(scores - lse).astype(BF16)
            outs = jnp.concatenate(
                [dot(probs[span.start : span.start + SPAN], ext[item, span, DH : 2 * DH]) for span in spans], axis=0
            ).astype(BF16)
            select = onehot_rows(rank_out[pl.ds(item, 1), :], tokens)
            returning[item] = dot(select, outs).astype(BF16)
            spread(n, g, returning.at[item], back.at[item], piece, bks.at[item], bkr.at[item])
            packed = jnp.transpose(columns3(lse))[0:16]
            slots_out[pl.ds(item, 1), :] = jnp.sum(packed, axis=0, keepdims=True)
            lse_row = jnp.sum(dot_nt(packed.astype(BF16), select), axis=0, keepdims=True)
            for d in range(n):
                lse_send[h, d, pl.ds(r, 1), 0:piece] = lse_row[:, d * piece : (d + 1) * piece]

        lse_recv[h, g] = lse_send[h, g]

        @pl.loop(1, n)
        def _(i):
            d = lax.rem(g + i, n)
            remote(lse_send.at[h, d], lse_recv.at[h, g], lss.at[h], lsr.at[h], "seq", d).start()

    for h in range(heads):

        @pl.loop(0, rounds)
        def _(r):
            item = r * heads + h
            all_of(back.at[item], peers_rows, bks.at[item], bkr.at[item], g).wait_recv()
            ro_out[item] = dot(onehot_columns(sendcol[item], tokens), back[item]).astype(BF16)

    for h in range(heads):
        all_of(lse_recv.at[h], n - 1, lss.at[h], lsr.at[h], g).wait_recv()
        lse_rows[h] = jnp.concatenate([lse_recv[h, d][:, 0:piece] for d in range(n)], axis=1)
        for r in range(rounds):
            item = r * heads + h
            lsecol[item] = row_to_column(lse_rows[h, r : r + 1, :], onehot_columns(sendcol[item], tokens))

    weights = jnp.zeros((tokens, 128), F32)
    for h in range(heads):
        logs = [lsecol[r * heads + h] for r in range(rounds)]
        peak = functools.reduce(jnp.maximum, logs)
        full = peak + jnp.log(sum(jnp.exp(x - peak) for x in logs))
        merged = jnp.zeros((tokens, DH), F32)
        for r in range(rounds):
            w = jnp.exp(logs[r] - full)
            weights = jnp.where(lane == r * heads + h, w, weights)
            merged = merged + w * ro_out[r * heads + h].astype(F32)
        merged_out[:, h * DH : (h + 1) * DH] = merged
        mixed_out[:, h * DH : (h + 1) * DH] = merged.astype(BF16)
    wts_out[...] = weights

    for chunk in range(chunks):
        line_drain(me, m, zbuf, zs, zr, chunk)
    for block in range(heads * chunks):
        share_drain(g, n, table, block, xs, xr)
    for k in range(cot_out.shape[0]):

        @pl.loop(1, m)
        def _(i):
            src = lax.rem(me + i, m)
            remote(cot_out.at[k, src], cot_out.at[k, src], cs.at[k, i], cr.at[k, src], "mp", src).wait()

    @pl.loop(0, count)
    def _(item):
        all_of(returning.at[item], peers_rows, bks.at[item], bkr.at[item], g).wait_send()
        remote(ext.at[item, pl.ds(tokens, SPAN)], ext.at[item, pl.ds(0, SPAN)], prs.at[item], prr.at[item], "seq", after).wait_send()

    for h in range(heads):
        all_of(lse_send.at[h], n - 1, lss.at[h], lsr.at[h], g).wait_send()


def front(n, m, heads, second, second_cot, order, gain, shift, wq, wv):
    tokens, part_width = second.shape
    width = wq.shape[0]
    rounds = order.shape[0]
    count = rounds * heads
    piece = tokens // n
    blocks = tokens // SPAN
    chunks = 4
    dma = pltpu.SemaphoreType.DMA
    sds = jax.ShapeDtypeStruct
    outs = (
        sds((tokens, width), BF16),
        sds((1, m, tokens, part_width), BF16),
        sds((count, SPAN + tokens, 2 * DH), BF16),
        sds((count, tokens, DH), BF16),
        sds((tokens, 128), F32),
        sds((tokens, heads * DH), BF16),
        sds((tokens, heads * DH), F32),
        sds((count, tokens), F32),
        sds((count, tokens), F32),
        sds((count, tokens), F32),
        sds((blocks, count, 2 * SPAN), F32),
        sds((count, tokens), F32),
        sds((count, tokens), F32),
        sds((m, chunks, tokens // chunks, part_width), BF16),
    )
    scratch = [
        pltpu.VMEM((n, heads * chunks, tokens // chunks, 2 * DH), BF16),
        pltpu.VMEM((count, tokens, 2 * DH), BF16),
        pltpu.VMEM((count, tokens, DH), BF16),
        pltpu.VMEM((count, tokens, DH), BF16),
        pltpu.VMEM((SPAN + tokens, DH), BF16),
        pltpu.VMEM((count, tokens + 128), F32),
        pltpu.VMEM((count, tokens, 1), F32),
        pltpu.VMEM((count, tokens, 1), F32),
        pltpu.VMEM((count, tokens, 1), F32),
        pltpu.VMEM((count, tokens, 1), F32),
        pltpu.VMEM((count, tokens, 1), F32),
        pltpu.VMEM((heads, n, 8, max(128, piece)), F32),
        pltpu.VMEM((heads, n, 8, max(128, piece)), F32),
        pltpu.VMEM((heads, 8, tokens), F32),
        pltpu.VMEM((tokens, part_width), F32),
        pltpu.VMEM((tokens, part_width), F32),
        pltpu.VMEM((count, order.shape[2]), jnp.int32),
        pltpu.VMEM(order.shape, jnp.int32),
        pltpu.VMEM((1, width), F32),
        pltpu.VMEM((1, width), F32),
        pltpu.VMEM(wq.shape, BF16),
        pltpu.VMEM(wv.shape, BF16),
        dma((2, m, chunks)),
        dma((2, m, chunks)),
        dma((2, m)),
        dma((2, m)),
        dma((n, heads * chunks)),
        dma((n, heads * chunks)),
        dma((count,)),
        dma((count,)),
        dma((count,)),
        dma((count,)),
        dma((heads,)),
        dma((heads,)),
        dma((7,)),
    ]
    return pl.pallas_call(
        functools.partial(front_kernel, n, m, heads, piece),
        out_shape=outs,
        in_specs=[HBM] * 7,
        out_specs=[VMEM] * len(outs),
        scratch_shapes=scratch,
        compiler_params=pltpu.CompilerParams(
            collective_id=0, has_side_effects=True, vmem_limit_bytes=38 << 20
        ),
        name="front",
    )(*(pltpu.with_memory_space_constraint(x, pltpu.HBM) for x in (second, second_cot, order, gain, shift, wq, wv)))


def reduce_start(me, m, own, got, send, recv, chunk):
    @pl.when(me == 0)
    def _():
        for s in range(m - 1, 0, -1):
            remote(own.at[s, chunk], got.at[0, s, chunk], send.at[0, s, chunk], recv.at[0, s, chunk], "mp", me + 1).start()

    @pl.when(me == m - 1)
    def _():
        for s in range(m - 1):
            remote(own.at[s, chunk], got.at[1, s, chunk], send.at[1, s, chunk], recv.at[1, s, chunk], "mp", me - 1).start()


def reduce_forward(me, m, own, got, passing, send, recv, tick, chunks):
    for direction, chunk, peer in ((0, tick - me, me + 1), (1, tick - (m - 1 - me), me - 1)):

        @pl.when((me > 0) & (me < m - 1) & (chunk >= 0) & (chunk < chunks))
        def _():
            for i in range(m - 1):
                s = m - 1 - i if direction == 0 else i

                @pl.when(s > me if direction == 0 else s < me)
                def _():
                    place = (direction, s, chunk)
                    hop = remote(passing.at[place], got.at[place], send.at[place], recv.at[place], "mp", peer)
                    hop.wait_recv()
                    passing[place] = (own[s, chunk].astype(F32) + got[place].astype(F32)).astype(BF16)
                    hop.start()


def reduce_final(me, m, own, got, total, send, recv, chunk):
    total[...] = own[me, chunk].astype(F32)
    for direction, expected in ((0, me > 0), (1, me < m - 1)):

        @pl.when(expected)
        def _():
            place = (direction, me, chunk)
            remote(own.at[me, chunk], got.at[place], send.at[place], recv.at[place], "mp", me).wait_recv()
            total[...] += got[place].astype(F32)


def reduce_drain(me, m, own, got, send, recv, chunk):
    for s in range(m):
        for direction, sent in ((0, me < s), (1, me > s)):
            place = (direction, s, chunk)

            @pl.when(sent)
            def _():
                remote(own.at[s, chunk], got.at[place], send.at[place], recv.at[place], "mp", me).wait_send()


def pack_stats(a, b):
    lane = iota((a.shape[0], 128), 1)
    return jnp.transpose(jnp.where(lane == 0, a, jnp.where(lane == 1, b, 0.0)))[0:8]


def stats_start(me, m, stats, send, recv, chunk):
    @pl.loop(1, m)
    def _(i):
        remote(stats.at[me, chunk], stats.at[me, chunk], send.at[i, chunk], recv.at[me, chunk], "mp", lax.rem(me + i, m)).start()


def stats_wait(me, m, stats, send, recv, chunk):
    @pl.loop(1, m)
    def _(i):
        src = lax.rem(me + i, m)
        remote(stats.at[src, chunk], stats.at[src, chunk], send.at[i, chunk], recv.at[src, chunk], "mp", src).wait()

    return jnp.transpose(sum(stats[s, chunk] for s in range(m)))


def pair_send(g, q, own, got, send, recv):
    odd = lax.rem(g, 2)
    return remote(own.at[2 * q + 1 - odd], got.at[q], send.at[q], recv.at[q], "seq", g + 1 - 2 * odd)


def pair_pass(g, q, own, got, passing, part, fin, send1, recv1, send2, recv2):
    odd = lax.rem(g, 2)
    home = g // 2
    pair_send(g, q, own, got, send1, recv1).wait_recv()
    passing[q] = (own[2 * q + odd].astype(F32) + got[q].astype(F32)).astype(BF16)

    @pl.when(q != home)
    def _():
        remote(passing.at[(q,) + part], fin.at[home], send2.at[q], recv2.at[home], "seq", 2 * q + odd).start()


def pair_total(g, pairs, passing, part, fin, send2, recv2):
    home = g // 2

    @pl.loop(1, pairs)
    def _(i):
        q = lax.rem(home + i, pairs)
        remote(fin.at[q], fin.at[q], send2.at[q], recv2.at[q], "seq", g).wait_recv()

    fin[home] = passing[(home,) + part]


def pair_drain(g, pairs, own, got, passing, part, fin, send1, recv1, send2, recv2):
    home = g // 2

    @pl.loop(0, pairs)
    def _(q):
        pair_send(g, q, own, got, send1, recv1).wait_send()

        @pl.when(q != home)
        def _():
            remote(passing.at[(q,) + part], fin.at[home], send2.at[q], recv2.at[home], "seq", g).wait_send()


def middle_kernel(
    n, m, heads, chunks,
    mixed, mixing_in, first_in, first_cot_in, cot_full, gain, shift, expand_in, expand_bias, contract_in,
    out_first, grad_first, gm_out, fo_out, pe_out, pc_out, pm_out, vec_out,
    part_a, got_a, pass_a, full_a, part_b, got_b, pass_b, full_b, total, stats,
    gact, feed, active, gpre, grad_feed, grad_att, mean_scr, rstd_scr, w_own, w_got, w_pass, w_fin, mixing, first, first_cot, expand, contract,
    ras, rar, gas, gar, rbs, rbr, gbs, gbr, sts, str_, w1s, w1r, w2s, w2r, fs,
):
    g = lax.axis_index("seq")
    me = lax.axis_index("mp")
    tokens, part_width = first.shape
    width = mixing.shape[1]
    hidden = expand.shape[1]
    rows = tokens // chunks
    loads = fetch(
        (
            (mixing_in, mixing), (contract_in, contract), (first_in, first),
            (expand_in, expand), (first_cot_in, first_cot),
        ),
        fs,
    )
    hops = m - 1
    pairs = n // 2
    slice_rows = width // n
    tile = max(256, 2 * slice_rows)
    tiles = width // tile
    tile_pairs = tile // slice_rows // 2
    greet(n, m, g, me)
    loads[0].wait()

    def scatter(part, value, chunk):
        for s in range(m):
            part[s, chunk] = value[:, s * part_width : (s + 1) * part_width].astype(BF16)

    def gather(full, chunk):
        return jnp.concatenate([full[s, chunk] for s in range(m)], axis=1)

    def rows_of(chunk):
        return pl.ds(pl.multiple_of(chunk * rows, rows), rows)

    def during(tick, delay, body, length=chunks):
        @pl.when((tick >= delay) & (tick < delay + length))
        def _():
            body(tick - delay)

    for chunk in range(chunks):
        scatter(part_a, dot(mixed[chunk * rows : (chunk + 1) * rows, :], mixing[...]), chunk)
        reduce_start(me, m, part_a, got_a, ras, rar, chunk)
    for load in loads[1:]:
        load.wait()
    own_cols = pl.multiple_of(me * part_width, part_width)
    gain_own = gain[:, pl.ds(own_cols, part_width)]
    vec_out[...] = jnp.zeros_like(vec_out)

    def finish_first(chunk):
        part = rows_of(chunk)
        reduce_final(me, m, part_a, got_a, total, ras, rar, chunk)
        stream = first[part, :] + total[...]
        out_first[part, :] = stream
        full_a[me, chunk] = stream.astype(BF16)
        line_start(me, m, full_a, gas, gar, chunk)

    def back_of_feed(chunk):
        part = rows_of(chunk)
        cot = jnp.concatenate([cot_full[0, s, part, :] for s in range(m)], axis=1)
        grad_feed[part, :] = cot
        gact[part, :] = dot_nt(cot, contract[...])

    def feed_forward(chunk):
        part = rows_of(chunk)
        x = gather(full_a, chunk).astype(F32)
        mean = jnp.mean(x, axis=1, keepdims=True)
        center = x - mean
        rstd = lax.rsqrt(jnp.mean(center * center, axis=1, keepdims=True) + EPSILON)
        mean_scr[part, :] = mean
        rstd_scr[part, :] = rstd
        xhat = center * rstd
        normed = (xhat * gain[...] + shift[...]).astype(BF16)
        feed[part, :] = normed
        pre = dot(normed, expand[...]) + expand_bias[...]
        gate = 0.5 * (1.0 + lax.erf(pre * (1.0 / math.sqrt(2.0))))
        active[part, :] = (pre * gate).astype(BF16)
        slope = gate + pre * jnp.exp(-0.5 * pre * pre) * (1.0 / math.sqrt(2.0 * math.pi))
        back = (gact[part, :] * slope).astype(BF16)
        gpre[part, :] = back
        term = dot_nt(back, expand[...])
        scatter(part_b, term, chunk)
        reduce_start(me, m, part_b, got_b, rbs, rbr, chunk)
        e = term * gain[...]
        stats[me, chunk] = pack_stats(
            jnp.sum(e, axis=1, keepdims=True), jnp.sum(e * xhat, axis=1, keepdims=True)
        )
        stats_start(me, m, stats, sts, str_, chunk)
        vec_out[0:1, :] += jnp.sum(term * xhat, axis=0, keepdims=True)
        vec_out[1:2, :] += jnp.sum(term, axis=0, keepdims=True)
        vec_out[2:3, :] += jnp.sum(grad_feed[part, :].astype(F32), axis=0, keepdims=True)
        vec_out[3:4, :] += jnp.sum(back.astype(F32), axis=0, keepdims=True)

    def finish_grad(chunk):
        part = rows_of(chunk)
        reduce_final(me, m, part_b, got_b, total, rbs, rbr, chunk)
        sums = stats_wait(me, m, stats, sts, str_, chunk) * (1.0 / width)
        rstd = rstd_scr[part, :]
        xhat = (full_a[me, chunk].astype(F32) - mean_scr[part, :]) * rstd
        stream = first_cot[part, :] + rstd * (
            total[...] * gain_own - sums[:, 0:1] - xhat * sums[:, 1:2]
        )
        grad_first[part, :] = stream
        full_b[me, chunk] = stream.astype(BF16)
        line_start(me, m, full_b, gbs, gbr, chunk)

    def merged_grad(chunk):
        part = rows_of(chunk)
        att = gather(full_b, chunk)
        grad_att[part, :] = att
        gm_out[part, :] = dot_nt(att, mixing[...])

    def weight_tile(k):
        cols = pl.ds(pl.multiple_of(k * tile, tile), tile)
        for lanes, left, right in (
            (slice(0, hidden), feed, gpre),
            (slice(hidden, 2 * hidden), grad_feed, active),
        ):
            product = dot_tn(left[:, cols], right[...]).astype(BF16)
            for i in range(2 * tile_pairs):
                w_own[k * 2 * tile_pairs + i, :, lanes] = product[i * slice_rows : (i + 1) * slice_rows]
        for i in range(tile_pairs):
            pair_send(g, k * tile_pairs + i, w_own, w_got, w1s, w1r).start()

    second_part = (slice(None), pl.ds(hidden, hidden))

    def weight_pass(k):
        for i in range(tile_pairs):
            pair_pass(g, k * tile_pairs + i, w_own, w_got, w_pass, second_part, w_fin, w1s, w1r, w2s, w2r)

    def feed_out(k):
        s = k
        fo_out[s] = dot(active[...], contract[:, pl.ds(pl.multiple_of(s * part_width, part_width), part_width)]).astype(BF16)

    @pl.loop(0, chunks + 4 * hops)
    def _(tick):
        reduce_forward(me, m, part_a, got_a, pass_a, ras, rar, tick, chunks)
        reduce_forward(me, m, part_b, got_b, pass_b, rbs, rbr, tick - 2 * hops, chunks)
        for hop in range(hops, 0, -1):
            during(tick, hops + hop, lambda chunk: line_step(me, m, full_a, gas, gar, chunk, hop))
            during(tick, 3 * hops + hop, lambda chunk: line_step(me, m, full_b, gbs, gbr, chunk, hop))
        during(tick, hops, finish_first)
        during(tick, 3 * hops, finish_grad)
        during(tick, 4 * hops, merged_grad)
        during(tick, 0, back_of_feed)
        during(tick, 2 * hops, feed_forward)
        for j in range(2):
            during(tick, chunks + 2 * hops, lambda k: weight_pass(2 * k + j), tiles // 2)
            during(tick, chunks + 2 * hops - 1, lambda k: weight_tile(2 * k + j), tiles // 2)

    @pl.loop(0, m)
    def _(s):
        feed_out(s)

    @pl.loop(0, width // 256)
    def _(k):
        cols = pl.ds(pl.multiple_of(k * 256, 256), 256)
        pm_out[cols, :] = dot_tn(grad_att[:, cols], mixed[...]).astype(BF16)

    pe_out[...] = w_pass[:, :, 0:hidden]
    pair_total(g, pairs, w_pass, second_part, w_fin, w2s, w2r)
    pc_out[...] = jnp.transpose(sum(w_fin[q].astype(F32) for q in range(pairs)))

    for chunk in range(chunks):
        reduce_drain(me, m, part_a, got_a, ras, rar, chunk)
        reduce_drain(me, m, part_b, got_b, rbs, rbr, chunk)
        line_drain(me, m, full_a, gas, gar, chunk)
        line_drain(me, m, full_b, gbs, gbr, chunk)
    pair_drain(g, pairs, w_own, w_got, w_pass, second_part, w_fin, w1s, w1r, w2s, w2r)


def middle(n, m, heads, mixed, mixing, first, first_cot, cot_full, gain, shift, expand, expand_bias, contract):
    tokens, part_width = first.shape
    width = mixing.shape[1]
    hidden = expand.shape[1]
    chunks = 4
    rows = tokens // chunks
    slice_rows = width // n
    dma = pltpu.SemaphoreType.DMA
    sds = jax.ShapeDtypeStruct
    outs = (
        sds((tokens, part_width), F32),
        sds((tokens, part_width), F32),
        sds((tokens, heads * DH), F32),
        sds((m, tokens, part_width), BF16),
        sds((n // 2, slice_rows, hidden), BF16),
        sds((hidden, slice_rows), F32),
        sds((width, heads * DH), BF16),
        sds((8, width), F32),
    )
    shards = pltpu.VMEM((m, chunks, rows, part_width), BF16)
    both = pltpu.VMEM((2, m, chunks, rows, part_width), BF16)
    pieces = pltpu.VMEM((n // 2, slice_rows, 2 * hidden), BF16)
    scratch = [
        shards, both, both, shards, shards, both, both, shards,
        pltpu.VMEM((rows, part_width), F32),
        pltpu.VMEM((m, chunks, 8, rows), F32),
        pltpu.VMEM((tokens, hidden), F32),
        pltpu.VMEM((tokens, width), BF16),
        pltpu.VMEM((tokens, hidden), BF16),
        pltpu.VMEM((tokens, hidden), BF16),
        pltpu.VMEM((tokens, width), BF16),
        pltpu.VMEM((tokens, width), BF16),
        pltpu.VMEM((tokens, 1), F32),
        pltpu.VMEM((tokens, 1), F32),
        pltpu.VMEM((n, slice_rows, 2 * hidden), BF16),
        pieces, pieces,
        pltpu.VMEM((n // 2, slice_rows, hidden), BF16),
        pltpu.VMEM(mixing.shape, BF16),
        pltpu.VMEM(first.shape, F32),
        pltpu.VMEM(first.shape, F32),
        pltpu.VMEM(expand.shape, BF16),
        pltpu.VMEM(contract.shape, BF16),
    ] + [dma((2, m, chunks))] * 8 + [dma((m, chunks))] * 2 + [dma((n // 2,))] * 4 + [dma((5,))]
    return pl.pallas_call(
        functools.partial(middle_kernel, n, m, heads, chunks),
        out_shape=outs,
        in_specs=[VMEM, HBM, HBM, HBM, VMEM, VMEM, VMEM, HBM, VMEM, HBM],
        out_specs=[VMEM] * len(outs),
        scratch_shapes=scratch,
        compiler_params=pltpu.CompilerParams(
            collective_id=1, has_side_effects=True, vmem_limit_bytes=46 << 20
        ),
        name="middle",
    )(mixed, mixing, first, first_cot, cot_full, gain, shift, expand, expand_bias, contract)


def back_kernel(
    n, m, heads, piece, chunks,
    gm, merged, wts, ro, ext, rank, sendp, pos, kpos, slots, pe, normed, gathered, wq, wv, second, second_cot, fo, pm, vec_feed, gain, bias,
    out_second, grad_second, pe_out, pq_out, pv_out, pm_out, vec_out,
    outgoing, arrived, returning, back, unit, poscol, rankcol, sendcol, lsecol, gl_send, gl_recv, gl_rows, gradk, gradq, grads, wsel,
    prior, incoming, gpair, fo_recv, part_c, got_c, pass_c, total, stats, mean_scr, rstd_scr, w_own, w_got, w_pass, w_fin, e_fin, vec, vec_send, vec_recv, vec_all,
    ins, inr, prs, prr, bks, bkr, gls, glr, es, er, fos, fore, rcs, rcr, sts, str_, w1s, w1r, w2s, w2r, vs, vr, vzs, vzr,
):
    g = lax.axis_index("seq")
    me = lax.axis_index("mp")
    tokens, width = normed.shape
    part_width = second.shape[1]
    count = ro.shape[0]
    rounds = count // heads
    blocks = tokens // SPAN
    rows = tokens // chunks
    scaling = 1.0 / math.sqrt(DH)
    greet(n, m, g, me)

    @pl.loop(1, m)
    def _(i):
        peer = lax.rem(me + i, m)
        remote(fo.at[peer], fo_recv.at[me], fos.at[i], fore.at[me], "mp", peer).start()

    pos_col = jnp.transpose(pos[...])
    send_col = jnp.transpose(sendp[...])
    rank_col = jnp.transpose(rank[...])
    lse_col = jnp.transpose(slots[...])
    for item in range(count):
        poscol[item] = pos_col[:, item : item + 1]
        lsecol[item] = lse_col[:, item : item + 1]
        sendcol[item] = send_col[:, item : item + 1]
        rankcol[item] = rank_col[:, item : item + 1]

    lane = iota((tokens, 128), 1)

    def weight_of(item):
        return jnp.sum(jnp.where(lane == item, wts[...], 0.0), axis=1, keepdims=True)

    def send_item(item):
        h = item % heads
        select = onehot_rows(sendp[item : item + 1, :], tokens)
        outgoing[item] = dot(select, (weight_of(item) * gm[:, h * DH : (h + 1) * DH]).astype(BF16)).astype(BF16)
        spread(n, g, outgoing.at[item], arrived.at[item], piece, ins.at[item], inr.at[item])

    for item in range(2):
        send_item(item)

    for h in range(heads):
        cols = slice(h * DH, (h + 1) * DH)
        gmh = gm[:, cols]
        inner = jnp.sum(gmh * merged[:, cols], axis=1, keepdims=True)
        for r in range(rounds):
            item = r * heads + h
            gs = weight_of(item) * (jnp.sum(gmh * ro[item].astype(F32), axis=1, keepdims=True) - inner)
            row = column_to_row(gs, onehot_rows(sendp[item : item + 1, :], tokens))
            for d in range(n):
                gl_send[d, item : item + 1, 0:piece] = row[:, d * piece : (d + 1) * piece]

    gl_recv[g] = gl_send[g]

    @pl.loop(1, n)
    def _(i):
        d = lax.rem(g + i, n)
        remote(gl_send.at[d], gl_recv.at[g], gls, glr, "seq", d).start()

    for item in range(2, count):
        send_item(item)

    all_of(gl_recv, n - 1, gls, glr, g).wait_recv()
    gl_rows[...] = jnp.concatenate([gl_recv[d][:, 0:piece] for d in range(n)], axis=1)
    peers_rows = (n - 1) * piece
    before = lax.rem(g + n - 1, n)

    @pl.loop(0, count + 2)
    def _(step):
        @pl.when(step < count)
        def _():
            item = step
            slot = lax.rem(item, 3)
            all_of(arrived.at[item], peers_rows, ins.at[item], inr.at[item], g).wait_recv()
            select = onehot_columns(rankcol[item], tokens)
            grads[...] = dot(select, arrived[item]).astype(BF16)
            wsel[...] = row_to_column(gl_rows[pl.ds(item, 1), :], select)
            w = ext[item, :, 0:DH].astype(F32)
            unit[...] = (w * lax.rsqrt(jnp.sum(w * w, axis=1, keepdims=True) + EPSILON)).astype(BF16)
            spans = [slice(block * SPAN, (block + 2) * SPAN) for block in range(blocks)]
            queries = [ext[item, span.start + SPAN : span.stop, 0:DH] for span in spans]
            raw = jnp.concatenate([dot_nt(q, unit[span]) for q, span in zip(queries, spans)], axis=0) * scaling
            gp = jnp.concatenate(
                [dot_nt(grads[span.start : span.start + SPAN], ext[item, span, DH : 2 * DH]) for span in spans], axis=0
            )
            scores, earlier = masked(raw, kpos, poscol, item, blocks)
            probs = jnp.exp(scores - lsecol[item])
            inner = jnp.sum(probs * gp, axis=1, keepdims=True)
            gs = (jnp.where(earlier, probs * (gp - inner + wsel[...]), 0.0) * scaling).astype(BF16)
            low = probs.astype(BF16)
            gradq[slot] = jnp.concatenate(
                [dot(gs[span.start : span.start + SPAN], unit[span]) for span in spans], axis=0
            )
            gk = [dot_tn(gs[span.start : span.start + SPAN], q) for q, span in zip(queries, spans)]
            gv = [
                dot_tn(low[span.start : span.start + SPAN], grads[span.start : span.start + SPAN])
                for span in spans
            ]
            for lanes, slots in ((slice(0, DH), gk), (slice(DH, 2 * DH), gv)):
                prior[item, :, lanes] = slots[0][0:SPAN].astype(BF16)
                for block in range(blocks):
                    lo = block * SPAN
                    own = slots[block][SPAN : 2 * SPAN]
                    if block + 1 < blocks:
                        own = own + slots[block + 1][0:SPAN]
                    gradk[slot, lo : lo + SPAN, lanes] = own
            remote(prior.at[item], incoming.at[item], prs.at[item], prr.at[item], "seq", before).start()

        @pl.when(step > 1)
        def _():
            item = step - 2
            slot = lax.rem(item, 3)
            remote(prior.at[item], incoming.at[item], prs.at[item], prr.at[item], "seq", before).wait_recv()
            gradk[slot, tokens - SPAN :, :] += incoming[item].astype(F32)
            w = ext[item, SPAN:, 0:DH].astype(F32)
            inv = lax.rsqrt(jnp.sum(w * w, axis=1, keepdims=True) + EPSILON)
            gk = gradk[slot, :, 0:DH]
            along = jnp.sum(w * gk, axis=1, keepdims=True)
            gq = gradq[slot] + inv * gk - (inv * inv * inv * along) * w
            done = jnp.concatenate([gq.astype(BF16), gradk[slot, :, DH : 2 * DH].astype(BF16)], axis=1)
            select = onehot_rows(rank[pl.ds(item, 1), :], tokens)
            returning[item] = dot(select, done).astype(BF16)
            spread(n, g, returning.at[item], back.at[item], piece, bks.at[item], bkr.at[item])

    home = g // 2
    pairs = n // 2

    @pl.loop(1, pairs)
    def _(i):
        q = lax.rem(home + i, pairs)
        remote(pe.at[q], e_fin.at[home], es.at[q], er.at[home], "seq", 2 * q + lax.rem(g, 2)).start()

    for chunk in range(gathered.shape[1]):
        high = gathered.shape[2]
        x = jnp.concatenate([gathered[s, chunk].astype(F32) for s in range(m)], axis=1)
        mean = jnp.mean(x, axis=1, keepdims=True)
        center = x - mean
        mean_scr[chunk * high : (chunk + 1) * high] = mean
        rstd_scr[chunk * high : (chunk + 1) * high] = lax.rsqrt(
            jnp.mean(center * center, axis=1, keepdims=True) + EPSILON
        )

    gpair[...] = jnp.zeros_like(gpair)

    @pl.loop(0, count)
    def _(item):
        all_of(back.at[item], peers_rows, bks.at[item], bkr.at[item], g).wait_recv()
        select = onehot_columns(sendcol[item], tokens)
        gpair[lax.rem(item, heads)] += dot(select, back[item])

    gq = jnp.concatenate([gpair[h][:, 0:DH] for h in range(heads)], axis=1).astype(BF16)
    gv = jnp.concatenate([gpair[h][:, DH : 2 * DH] for h in range(heads)], axis=1).astype(BF16)
    vec[0:2, :] = jnp.zeros((2, width), F32)
    vec[2:6, :] = vec_feed[0:4, :]
    vec[6:8, :] = jnp.zeros((2, width), F32)
    sub = gathered.shape[2] // rows
    for chunk in range(chunks):
        part = slice(chunk * rows, (chunk + 1) * rows)
        inside = slice((chunk % sub) * rows, (chunk % sub + 1) * rows)
        term = dot_nt(gq[part], wq[...]) + dot_nt(gv[part], wv[...])
        for s in range(m):
            part_c[s, chunk] = term[:, s * part_width : (s + 1) * part_width].astype(BF16)
        reduce_start(me, m, part_c, got_c, rcs, rcr, chunk)
        x = jnp.concatenate([gathered[s, chunk // sub, inside, :].astype(F32) for s in range(m)], axis=1)
        xhat = (x - mean_scr[part]) * rstd_scr[part]
        e = term * gain[...]
        stats[me, chunk] = pack_stats(
            jnp.sum(e, axis=1, keepdims=True), jnp.sum(e * xhat, axis=1, keepdims=True)
        )
        stats_start(me, m, stats, sts, str_, chunk)
        vec[0:1, :] += jnp.sum(term * xhat, axis=0, keepdims=True)
        vec[1:2, :] += jnp.sum(term, axis=0, keepdims=True)

    slice_rows = width // n
    for d in range(n):
        vec_send[d, :, 0:slice_rows] = vec[:, d * slice_rows : (d + 1) * slice_rows]
    vec_recv[g] = vec_send[g]

    @pl.loop(1, n)
    def _(i):
        d = lax.rem(g + i, n)
        remote(vec_send.at[d], vec_recv.at[g], vs, vr, "seq", d).start()

    tile = max(256, 2 * slice_rows)
    tile_pairs = tile // slice_rows // 2
    own_heads = heads * DH

    def weight_tile(k):
        cols = pl.ds(pl.multiple_of(k * tile, tile), tile)
        products = (
            dot_tn(normed[:, cols], gq).astype(BF16),
            dot_tn(normed[:, cols], gv).astype(BF16),
            pm[cols, :],
        )
        for j, product in enumerate(products):
            for i in range(2 * tile_pairs):
                w_own[k * 2 * tile_pairs + i, :, j * own_heads : (j + 1) * own_heads] = product[
                    i * slice_rows : (i + 1) * slice_rows
                ]
        for i in range(tile_pairs):
            pair_send(g, k * tile_pairs + i, w_own, w_got, w1s, w1r).start()

    own_cols = pl.multiple_of(me * part_width, part_width)
    gain_own = gain[:, pl.ds(own_cols, part_width)]
    hops = m - 1

    def finish(chunk):
        part = pl.ds(pl.multiple_of(chunk * rows, rows), rows)
        inside = pl.ds(pl.multiple_of(lax.rem(chunk, sub) * rows, rows), rows)
        reduce_final(me, m, part_c, got_c, total, rcs, rcr, chunk)
        sums = stats_wait(me, m, stats, sts, str_, chunk) * (1.0 / width)
        rstd = rstd_scr[part, :]
        xhat = (gathered[me, chunk // sub, inside, :].astype(F32) - mean_scr[part, :]) * rstd
        grad_second[part, :] = second_cot[part, :] + rstd * (
            total[...] * gain_own - sums[:, 0:1] - xhat * sums[:, 1:2]
        )

    def weight_pass(k):
        for i in range(tile_pairs):
            pair_pass(g, k * tile_pairs + i, w_own, w_got, w_pass, (), w_fin, w1s, w1r, w2s, w2r)

    tiles = width // tile

    @pl.loop(0, max(chunks + hops, tiles + 1))
    def _(tick):
        reduce_forward(me, m, part_c, got_c, pass_c, rcs, rcr, tick, chunks)

        @pl.when((tick >= hops) & (tick < chunks + hops))
        def _():
            finish(tick - hops)

        @pl.when((tick >= 1) & (tick < tiles + 1))
        def _():
            weight_pass(tick - 1)

        @pl.when(tick < tiles)
        def _():
            weight_tile(tick)

        @pl.when(tick == 2)
        def _():
            all_of(vec_recv, n - 1, vs, vr, g).wait_recv()
            vec_all[me] = sum(vec_recv[d] for d in range(n))

            @pl.loop(1, m)
            def _(i):
                peer = lax.rem(me + i, m)
                remote(vec_all.at[me], vec_all.at[me], vzs.at[i], vzr.at[me], "mp", peer).start()

    fo_recv[me] = fo[me]

    @pl.loop(1, m)
    def _(i):
        src = lax.rem(me + i, m)
        remote(fo.at[src], fo_recv.at[src], fos.at[i], fore.at[src], "mp", src).wait()

    out_second[...] = (
        second[...]
        + sum(fo_recv[s].astype(F32) for s in range(m))
        + bias[:, pl.ds(own_cols, part_width)]
    )
    @pl.loop(1, m)
    def _(i):
        src = lax.rem(me + i, m)
        remote(vec_all.at[src], vec_all.at[src], vzs.at[i], vzr.at[src], "mp", src).wait()

    row = iota((8, vec_all.shape[2]), 0)
    vec_out[...] = jnp.where(row < 4, sum(vec_all[s] for s in range(m)), vec_all[me])
    pair_total(g, pairs, pe, (), e_fin, es, er)
    pe_out[...] = sum(e_fin[q].astype(F32) for q in range(pairs))
    pair_total(g, pairs, w_pass, (), w_fin, w2s, w2r)
    for j, out in enumerate((pq_out, pv_out)):
        out[...] = sum(w_fin[q, :, j * own_heads : (j + 1) * own_heads].astype(F32) for q in range(pairs))
    pm_out[...] = jnp.transpose(
        sum(w_fin[q, :, 2 * own_heads : 3 * own_heads].astype(F32) for q in range(pairs))
    )
    for chunk in range(chunks):
        reduce_drain(me, m, part_c, got_c, rcs, rcr, chunk)
    pair_drain(g, pairs, w_own, w_got, w_pass, (), w_fin, w1s, w1r, w2s, w2r)
    all_of(vec_send, n - 1, vs, vr, g).wait_send()

    @pl.loop(0, count)
    def _(item):
        all_of(outgoing.at[item], peers_rows, ins.at[item], inr.at[item], g).wait_send()
        all_of(returning.at[item], peers_rows, bks.at[item], bkr.at[item], g).wait_send()
        remote(prior.at[item], incoming.at[item], prs.at[item], prr.at[item], "seq", before).wait_send()

    all_of(gl_send, n - 1, gls, glr, g).wait_send()

    @pl.loop(1, pairs)
    def _(i):
        q = lax.rem(home + i, pairs)
        remote(pe.at[q], e_fin.at[home], es.at[q], er.at[home], "seq", g).wait_send()


def behind(n, m, heads, gm, merged, wts, ro, ext, rank, sendp, pos, kpos, slots, pe, normed, gathered, wq, wv, second, second_cot, fo, pm, vec_feed, gain, bias):
    tokens, part_width = second.shape
    width = normed.shape[1]
    count = ro.shape[0]
    piece = tokens // n
    chunks = 4
    rows = tokens // chunks
    slice_rows = width // n
    dma = pltpu.SemaphoreType.DMA
    sds = jax.ShapeDtypeStruct
    outs = (
        sds((tokens, part_width), F32),
        sds((tokens, part_width), F32),
        sds((slice_rows, pe.shape[2]), F32),
        sds((slice_rows, heads * DH), F32),
        sds((slice_rows, heads * DH), F32),
        sds((heads * DH, slice_rows), F32),
        sds((8, max(128, slice_rows)), F32),
    )
    both = pltpu.VMEM((2, m, chunks, rows, part_width), BF16)
    column = pltpu.VMEM((count, tokens, 1), F32)
    pieces = pltpu.VMEM((n // 2, slice_rows, 3 * heads * DH), BF16)
    scratch = [
        pltpu.VMEM((count, tokens, DH), BF16),
        pltpu.VMEM((count, tokens, DH), BF16),
        pltpu.VMEM((count, tokens, 2 * DH), BF16),
        pltpu.VMEM((count, tokens, 2 * DH), BF16),
        pltpu.VMEM((SPAN + tokens, DH), BF16),
        column, column, column, column,
        pltpu.VMEM((n, count, max(128, piece)), F32),
        pltpu.VMEM((n, count, max(128, piece)), F32),
        pltpu.VMEM((count, tokens), F32),
        pltpu.VMEM((3, tokens, 2 * DH), F32),
        pltpu.VMEM((3, tokens, DH), F32),
        pltpu.VMEM((tokens, DH), BF16),
        pltpu.VMEM((tokens, 1), F32),
        pltpu.VMEM((count, SPAN, 2 * DH), BF16),
        pltpu.VMEM((count, SPAN, 2 * DH), BF16),
        pltpu.VMEM((heads, tokens, 2 * DH), F32),
        pltpu.VMEM((m, tokens, part_width), BF16),
        pltpu.VMEM((m, chunks, rows, part_width), BF16),
        both, both,
        pltpu.VMEM((rows, part_width), F32),
        pltpu.VMEM((m, chunks, 8, rows), F32),
        pltpu.VMEM((tokens, 1), F32),
        pltpu.VMEM((tokens, 1), F32),
        pltpu.VMEM((n, slice_rows, 3 * heads * DH), BF16),
        pieces, pieces, pieces,
        pltpu.VMEM(pe.shape, BF16),
        pltpu.VMEM((8, width), F32),
        pltpu.VMEM((n, 8, max(128, slice_rows)), F32),
        pltpu.VMEM((n, 8, max(128, slice_rows)), F32),
        pltpu.VMEM((m, 8, max(128, slice_rows)), F32),
    ] + [dma((count,))] * 6 + [dma, dma, dma((n // 2,)), dma((n // 2,)), dma((m,)), dma((m,))] + [dma((2, m, chunks))] * 2 + [dma((m, chunks))] * 2 + [dma((n // 2,))] * 4 + [dma, dma, dma((m,)), dma((m,))]
    return pl.pallas_call(
        functools.partial(back_kernel, n, m, heads, piece, chunks),
        out_shape=outs,
        in_specs=[VMEM] * 22,
        out_specs=[VMEM] * len(outs),
        scratch_shapes=scratch,
        compiler_params=pltpu.CompilerParams(
            collective_id=2, has_side_effects=True, vmem_limit_bytes=40 << 20
        ),
        name="back",
    )(gm, merged, wts, ro, ext, rank, sendp, pos, kpos, slots, pe, normed, gathered, wq, wv, second, second_cot, fo, pm, vec_feed, gain, bias)


def local(
    first_half,
    second_half,
    bucket_order,
    attend_gain,
    attend_shift,
    queries,
    values,
    mixing,
    feed_gain,
    feed_shift,
    expand,
    expand_bias,
    contract,
    contract_bias,
    cot_first,
    cot_second,
):
    n = lax.axis_size("seq")
    m = lax.axis_size("mp")
    heads = bucket_order.shape[1]
    normed, cot_full, ext, ro, wts, mixed, merged, rank, sendp, pos, kpos, slots, _, gathered = front(
        n, m, heads, second_half, cot_second, bucket_order,
        attend_gain[None], attend_shift[None], queries, values,
    )
    out_first, grad_first, gm, fo, pe, pc, pm, vec_feed = middle(
        n, m, heads, mixed, mixing, first_half, cot_first, cot_full,
        feed_gain[None], feed_shift[None], expand, expand_bias[None], contract,
    )
    out_second, grad_second, pe, pq, pv, pm, vectors = behind(
        n, m, heads, gm, merged, wts, ro, ext, rank, sendp, pos, kpos, slots, pe, normed, gathered,
        queries, values, second_half, cot_second, fo, pm, vec_feed, attend_gain[None], contract_bias[None],
    )
    vectors = vectors[:, 0 : pq.shape[0]]
    return (
        out_first,
        out_second,
        grad_first,
        grad_second,
        vectors[0],
        vectors[1],
        pq,
        pv,
        pm,
        vectors[2],
        vectors[3],
        pe,
        vectors[5],
        pc,
        vectors[4],
    )


def solution(mesh):
    in_specs = (
        P("seq", "mp"),
        P("seq", "mp"),
        P(None, "mp", None),
        P(),
        P(),
        P(None, "mp"),
        P(None, "mp"),
        P("mp", None),
        P(),
        P(),
        P(None, "mp"),
        P("mp"),
        P("mp", None),
        P(),
        P("seq", "mp"),
        P("seq", "mp"),
    )
    out_specs = (
        P("seq", "mp"),
        P("seq", "mp"),
        P("seq", "mp"),
        P("seq", "mp"),
        P("seq"),
        P("seq"),
        P("seq", "mp"),
        P("seq", "mp"),
        P("mp", "seq"),
        P("seq"),
        P("seq"),
        P("seq", "mp"),
        P(("mp", "seq")),
        P("mp", "seq"),
        P("seq"),
    )
    return jax.shard_map(local, mesh=mesh, in_specs=in_specs, out_specs=out_specs, check_vma=False)
```
